32 devices in a mesh: groups: 2 (over x), seq: 8 (over z, y), dp: 2 (over core).
Axes of the slice: x: 2, y: 2, z: 4, core: 2. Of those that a mesh axis runs over, the one named last changes fastest.
Arguments:
- tokens: bfloat16 [4, 4096, 1024], P(('groups', 'dp'), 'seq'), parts along dimension 0, may hold values from -12 to 12
- qk_weight: bfloat16 [1024, 1024], replicated, may hold values from -0.1875 to 0.1875
- value_weight: bfloat16 [1024, 1024], replicated, may hold values from -0.1875 to 0.1875
- out_weight: bfloat16 [1024, 1024], replicated, may hold values from -0.1875 to 0.1875
- neighbour_list: int32 [4, 32, 4], P(('groups', 'dp'), 'seq'), parts along dimension 0, may hold values from 0 to 31, as said below
- neighbour_count: int32 [4, 32], P(('groups', 'dp'), 'seq'), parts along dimension 0, may hold values from 1 to 4, as said below
Outputs:
- update: bfloat16 [4, 4096, 1024], P(('groups', 'dp'), 'seq'), parts along dimension 0
The draws below stay inside these ranges and needn't reach their ends.
There are 2 independent parts, one for each index of `groups`. The reference program is written for one: setup_inputs(seed, part) draws one part's arguments, and reference() takes and returns one part's arrays. A program takes and returns all parts, laid end to end along the dimension named above; an argument that names none is the same for every part. Nothing has to cross between parts.
Inputs may be any that keep to these rules, and one draw needn't show every extreme that they name: `neighbour_list`: slot 0 of block b's list is b itself; the other slots name distinct blocks within 4 blocks of b on either side; slots at or beyond the count also name such blocks but are not attended. `neighbour_count`: every query block whose index is a multiple of 7 has count 4.
All inputs are finite; a program needn't handle non-finite values.
Results may differ from the reference program's by a relative error of at most 0.0066.
Values may be sent and summed in bfloat16 or wider, within the bound.
No kernel may reach another device: no remote copies, remote signals or barrier semaphores. Data moves between devices by JAX's collectives and lax.ppermute only.
A program may use at most 192 MiB of HBM per device.

```python
import jax
import jax.numpy as jnp
from jax import lax

D = 1024
H = 16
DH = 64
HL = 8
DL = 128
BLOCK = 128
MAXK = 4
BPD = 4
SEQS = 2
LENGTH = 4096
NBLK = 32


def draw_tokens(key, part):
    array_shape = (SEQS, LENGTH, D)
    return jnp.clip(jax.random.normal(key, array_shape, jnp.float32), -6.0, 6.0).astype(jnp.bfloat16)


def neighbour_tables(key):
    folded = jax.random.fold_in(key, 11)
    key_density, key_pick, key_order = jax.random.split(folded, 3)
    blocks = jnp.arange(NBLK, dtype=jnp.int32)
    density = jax.random.randint(key_density, (SEQS, NBLK // BPD), 1, MAXK + 1)
    density_rows = jnp.repeat(density, BPD, axis=1)
    pick_bits = jax.random.randint(key_pick, (SEQS, NBLK), 0, 1 << 20)
    counts = 1 + pick_bits % density_rows
    counts = jnp.where((blocks % 7 == 0)[None, :], MAXK, counts)
    offsets = jnp.arange(-BPD, BPD + 1, dtype=jnp.int32)
    window = 2 * BPD + 1
    ranks = jax.random.randint(key_order, (SEQS, NBLK, window), 0, 1 << 20) * window + jnp.arange(window, dtype=jnp.int32)
    target = blocks[:, None] + offsets[None, :]
    usable = (target >= 0) & (target < NBLK) & (offsets[None, :] != 0)
    ranks = jnp.where(usable[None], ranks, -1)
    ranked = jnp.argsort(-ranks, axis=-1, stable=True)[..., :MAXK - 1]
    chosen = blocks[None, :, None] + offsets[ranked]
    own_block = jnp.broadcast_to(blocks[None, :, None], (SEQS, NBLK, 1))
    tables = jnp.concatenate([own_block, chosen], axis=-1)
    return (tables.astype(jnp.int32), counts.astype(jnp.int32))


def draw_neighbour_list(key, part):
    return neighbour_tables(key)[0]


def draw_neighbour_count(key, part):
    return neighbour_tables(key)[1]


def scatter_about(key, shape, scale, bound, held_as=jnp.bfloat16):
    array = scale * jax.random.normal(key, shape, jnp.float32)
    return jnp.clip(array, min=-bound, max=bound).astype(held_as)


def setup_inputs(seed: int = 0, part: int = 0) -> dict:
    streams_of = jax.random.split(jax.random.key(seed), 7)
    own_keys = jax.random.split(jax.random.fold_in(streams_of[6], part), 7)
    tokens = draw_tokens(jax.random.fold_in(jax.random.fold_in(streams_of[6], part), 71), part)
    qk_weight = scatter_about(streams_of[1], (D, D), D ** -0.5, 0.1875)
    value_weight = scatter_about(streams_of[2], (D, D), D ** -0.5, 0.1875)
    out_weight = scatter_about(streams_of[3], (D, D), D ** -0.5, 0.1875)
    neighbour_list = draw_neighbour_list(jax.random.fold_in(jax.random.fold_in(streams_of[6], part), 71), part)
    neighbour_count = draw_neighbour_count(jax.random.fold_in(jax.random.fold_in(streams_of[6], part), 71), part)
    return {"tokens": tokens, "qk_weight": qk_weight, "value_weight": value_weight, "out_weight": out_weight, "neighbour_list": neighbour_list, "neighbour_count": neighbour_count}


def one_sequence(sequence_in, qk_weight, value_weight, out_weight, tables, live_counts):
    keyed = jnp.dot(sequence_in, qk_weight, preferred_element_type=jnp.float32).astype(jnp.bfloat16)
    values = jnp.dot(sequence_in, value_weight, preferred_element_type=jnp.float32).astype(jnp.bfloat16)
    block_total = tables.shape[0]
    keyed_blocks = keyed.reshape(block_total, BLOCK, H, DH)
    value_blocks = values.reshape(block_total, BLOCK, H, DH)
    score_scale = DH ** (-0.5)

    def attend(packed):
        query_block, key_ids, live_count = packed
        key_rows = keyed_blocks[key_ids].reshape(MAXK * BLOCK, H, DH).astype(jnp.float32)
        value_rows = value_blocks[key_ids].reshape(MAXK * BLOCK, H, DH).astype(jnp.float32)
        queries = keyed_blocks[query_block].astype(jnp.float32)
        scores = jnp.einsum('qhd,khd->hqk', queries, key_rows) * score_scale
        key_pos = (key_ids[:, None] * BLOCK + jnp.arange(BLOCK, dtype=jnp.int32)[None, :]).reshape(-1)
        query_pos = query_block * BLOCK + jnp.arange(BLOCK, dtype=jnp.int32)
        live_slots = jnp.repeat(jnp.arange(MAXK, dtype=jnp.int32) < live_count, BLOCK)
        allowed = live_slots[None, :] & (key_pos[None, :] != query_pos[:, None])
        scores = jnp.where(allowed[None], scores, -1e+30)
        row_max = lax.optimization_barrier(jnp.max(scores, axis=-1, keepdims=True))
        raised = jnp.exp(scores - row_max)
        weights = (raised / lax.optimization_barrier(jnp.sum(raised, axis=-1, keepdims=True))).astype(jnp.bfloat16)
        mixed_heads = jnp.einsum('hqk,khd->qhd', weights.astype(jnp.float32), value_rows)
        return mixed_heads.reshape(BLOCK, D)
    softmax_out = lax.map(attend, (jnp.arange(block_total, dtype=jnp.int32), tables, live_counts)).reshape(-1, D)
    features = jax.nn.silu(keyed.astype(jnp.float32)).astype(jnp.bfloat16)
    feature_blocks = features.reshape(block_total, BLOCK, HL, DL)
    linear_values = values.reshape(block_total, BLOCK, HL, DL)
    causal = jnp.arange(BLOCK)[:, None] >= jnp.arange(BLOCK)[None, :]
    highest = lax.Precision.HIGHEST

    def advance(running_state, segment):
        feature_rows = segment[0].astype(jnp.float32)
        segment_values = segment[1].astype(jnp.float32)
        carried = jnp.einsum('bhi,hij->bhj', feature_rows, running_state, precision=highest)
        affinity = jnp.einsum('bhi,shi->hbs', feature_rows, feature_rows, precision=highest)
        affinity = jnp.where(causal[None], affinity, 0.0)
        within = jnp.einsum('hbs,shj->bhj', affinity, segment_values, precision=highest)
        running_state = running_state + jnp.einsum('bhi,bhj->hij', feature_rows, segment_values, precision=highest)
        return (running_state, carried + within)
    start_state = jnp.zeros((HL, DL, DL), jnp.float32)
    _, numerator = lax.scan(advance, start_state, (feature_blocks, linear_values))
    numerator = numerator.reshape(-1, HL, DL)
    linear_out = numerator * lax.rsqrt(lax.optimization_barrier(jnp.mean(numerator * numerator, axis=-1, keepdims=True)) + 1e-06)
    combined = (softmax_out + linear_out.reshape(-1, D)).astype(jnp.bfloat16)
    return jnp.dot(combined, out_weight, preferred_element_type=jnp.float32).astype(jnp.bfloat16)

def reference(tokens, qk_weight, value_weight, out_weight, neighbour_list, neighbour_count):
    results = []
    for seq_index in range(SEQS):
        results.append(one_sequence(tokens[seq_index], qk_weight, value_weight, out_weight, neighbour_list[seq_index], neighbour_count[seq_index]))
    return jnp.stack(results)
```

```python
import functools

import jax
import jax.numpy as jnp
from jax import lax
from jax.experimental import pallas as pl
from jax.experimental.pallas import tpu as pltpu
from jax.sharding import PartitionSpec as P

H = 16
DH = 64
HL = 8
DL = 128
F32 = jnp.float32
BF16 = jnp.bfloat16
NT = (((1,), (1,)), ((), ()))
VMEM = pl.BlockSpec(memory_space=pltpu.VMEM)
SMEM = pl.BlockSpec(memory_space=pltpu.SMEM)
MIB = 1 << 20


def dot_nt(a, b):
    return lax.dot_general(a, b, NT, preferred_element_type=F32)


def dot_nn(a, b):
    return jnp.dot(a, b, preferred_element_type=F32)


def tile(i, size):
    return pl.ds(pl.multiple_of(i * size, size), size)


def project(x, wk_ref, wvt_ref, k_ref, vt_ref, f_ref=None):
    width = wk_ref.shape[1]

    def keyed_tile(n, carry):
        cols = tile(n, 256)
        k = dot_nn(x, wk_ref[:, cols]).astype(BF16)
        k_ref[:, cols] = k
        if f_ref is not None:
            kf = k.astype(F32)
            f_ref[:, cols] = (kf / (1.0 + jnp.exp(-kf))).astype(BF16)
        return carry

    def value_tile(n, carry):
        rows = tile(n, 256)
        vt_ref[rows, :] = dot_nt(wvt_ref[rows, :], x).astype(BF16)
        return carry

    lax.fori_loop(0, width // 256, keyed_tile, 0)
    lax.fori_loop(0, width // 256, value_tile, 0)


def own_kernel(x_ref, wk_ref, wvt_ref, k_ref, f_ref, vt_ref, s_ref):
    project(x_ref[...], wk_ref, wvt_ref, k_ref, vt_ref, f_ref)
    for h in range(HL):
        part = slice(h * DL, (h + 1) * DL)
        s_ref[part, :] = dot_nn(vt_ref[part, :], f_ref[:, part]).astype(BF16)


def before_kernel(count, t_ref, o_ref):
    rows = t_ref.shape[0] // count
    total = jnp.zeros((rows, t_ref.shape[1]), F32)
    for i in range(count):
        part = slice(i * rows, (i + 1) * rows)
        o_ref[part, :] = total.astype(BF16)
        total = total + t_ref[part, :].astype(F32)


def within_kernel(f_ref, vt_ref, n_ref):
    rows = f_ref.shape[0]
    half = rows // 2
    upper = lax.broadcasted_iota(jnp.int32, (half, half), 0) <= lax.broadcasted_iota(
        jnp.int32, (half, half), 1
    )

    def head(h, carry):
        cols = tile(h, DL)
        f0 = f_ref[:half, cols]
        f1 = f_ref[half:, cols]
        v0 = vt_ref[cols, :half]
        v1 = vt_ref[cols, half:]
        a00 = jnp.where(upper, dot_nt(f0, f0), 0.0).astype(BF16)
        a01 = dot_nt(f0, f1).astype(BF16)
        a11 = jnp.where(upper, dot_nt(f1, f1), 0.0).astype(BF16)
        n_ref[cols, :half] = dot_nn(v0, a00)
        n_ref[cols, half:] = dot_nn(v0, a01) + dot_nn(v1, a11)
        return carry

    lax.fori_loop(0, HL, head, 0, unroll=2)


def linear_kernel(f_ref, n_ref, s_ref, o_ref):
    def head(h, carry):
        cols = tile(h, DL)
        n = n_ref[cols, :] + dot_nt(s_ref[cols, :], f_ref[:, cols])
        mean = jnp.sum(n * n, axis=0, keepdims=True) * (1.0 / DL)
        o_ref[cols, :] = n * lax.rsqrt(mean + 1e-06)
        return carry

    lax.fori_loop(0, HL, head, 0, unroll=2)


def listed(list_ref, count_ref, qb, block):
    found = False
    for j in range(list_ref.shape[1]):
        found = jnp.logical_or(
            found, jnp.logical_and(j < count_ref[qb], list_ref[qb, j] == block)
        )
    return found


def attend(first, qb, kb, size, q_ref, k_ref, vt_ref, m_ref, l_ref, acc_ref):
    qrows = tile(qb, size)
    krows = tile(kb, size)
    lane = lax.broadcasted_iota(jnp.int32, (size, 2 * DH), 1)
    if first:
        shape = (size, 2 * size)
        key = lax.broadcasted_iota(jnp.int32, shape, 0)
        query = lax.broadcasted_iota(jnp.int32, shape, 1) % size
        other = key != query
    for p in range(H // 2):
        cols = slice(p * 2 * DH, (p + 1) * 2 * DH)
        q = q_ref[qrows, cols] * jnp.asarray(DH ** (-0.5), BF16)
        zero = jnp.zeros_like(q)
        pair = jnp.concatenate([jnp.where(lane < DH, q, zero), jnp.where(lane < DH, zero, q)], axis=0)
        s = dot_nt(k_ref[krows, cols], pair)
        if first:
            s = jnp.where(other, s, -1e30)
        top = jnp.max(s, axis=0, keepdims=True)
        if not first:
            old = m_ref[qb, p : p + 1, :]
            top = jnp.maximum(top, old)
        e = jnp.exp(s - top)
        total = jnp.sum(e, axis=0, keepdims=True)
        o = dot_nn(vt_ref[cols, krows], e.astype(BF16))
        o = jnp.concatenate([o[:DH, :size], o[DH:, size:]], axis=0)
        if not first:
            fade = jnp.exp(old - top)
            total = total + l_ref[qb, p : p + 1, :] * fade
            faded = jnp.concatenate(
                [
                    jnp.broadcast_to(fade[:, :size], (DH, size)),
                    jnp.broadcast_to(fade[:, size:], (DH, size)),
                ],
                axis=0,
            )
            o = o + acc_ref[qb, cols, :] * faded
        m_ref[qb, p : p + 1, :] = top
        l_ref[qb, p : p + 1, :] = total
        acc_ref[qb, cols, :] = o


def attend_listed(size, base, blocks, list_ref, count_ref, *rest, skip_own=False):
    queries = list_ref.shape[0]

    def pair(i, carry):
        qb, kb = i // blocks, i % blocks
        wanted = listed(list_ref, count_ref, qb, base + kb)
        if skip_own:
            wanted = jnp.logical_and(wanted, qb != kb)

        @pl.when(wanted)
        def _():
            attend(False, qb, kb, size, *rest)

        return carry

    lax.fori_loop(0, queries * blocks, pair, 0)


def own_attention_kernel(size, list_ref, count_ref, pos_ref, k_ref, vt_ref, m_ref, l_ref, acc_ref):
    queries = list_ref.shape[0]
    rest = (k_ref, k_ref, vt_ref, m_ref, l_ref, acc_ref)

    def first(qb, carry):
        attend(True, qb, qb, size, *rest)
        return carry

    lax.fori_loop(0, queries, first, 0)
    attend_listed(
        size, pos_ref[0] * queries, queries, list_ref, count_ref, *rest, skip_own=True
    )


def halo_run(pos, kind):
    even = pos % 2 == 0
    if kind == "partner":
        return jnp.where(even, pos + 1, pos - 1)
    return jnp.where(even, pos - 1, pos + 1)


def halo_pieces(size, pieces, list_ref, count_ref, pos_ref, piece_refs, wk_ref, wvt_ref, q_ref, rest, scratch):
    x_ref, k_ref, vt_ref = scratch
    queries = list_ref.shape[0]
    row = 0
    for ref in piece_refs:
        x_ref[row : row + ref.shape[0], :] = ref[...]
        row += ref.shape[0]
    project(x_ref[...], wk_ref, wvt_ref, k_ref, vt_ref)
    row = 0
    for (kind, chunk), ref in zip(pieces, piece_refs):
        base = halo_run(pos_ref[0], kind) * queries + chunk
        rows = ref.shape[0]
        attend_listed(
            size,
            base,
            rows // size,
            list_ref,
            count_ref,
            q_ref,
            k_ref.at[row : row + rows, :],
            vt_ref.at[:, row : row + rows],
            *rest,
        )
        row += rows


def halo_kernel(size, pieces, list_ref, count_ref, pos_ref, *refs):
    n = len(pieces)
    piece_refs = refs[:n]
    wk_ref, wvt_ref, q_ref = refs[n : n + 3]
    m_ref, l_ref, acc_ref = refs[n + 6 : n + 9]
    scratch = refs[n + 9 :]
    for src, dst in zip(refs[n + 3 : n + 6], refs[n + 6 : n + 9]):
        del src, dst
    halo_pieces(
        size, pieces, list_ref, count_ref, pos_ref, piece_refs, wk_ref, wvt_ref, q_ref, (m_ref, l_ref, acc_ref), scratch
    )


def final_kernel(size, pieces, list_ref, count_ref, pos_ref, *refs):
    n = len(pieces)
    piece_refs = refs[:n]
    wk_ref, wvt_ref, q_ref, lin_ref, wo_ref = refs[n : n + 5]
    out_ref, m_ref, l_ref, acc_ref = refs[n + 8 : n + 12]
    comb_ref = refs[n + 12]
    scratch = refs[n + 13 :]
    halo_pieces(
        size, pieces, list_ref, count_ref, pos_ref, piece_refs, wk_ref, wvt_ref, q_ref, (m_ref, l_ref, acc_ref), scratch
    )
    queries = list_ref.shape[0]

    def finish(qb, carry):
        rows = tile(qb, size)
        for p in range(H // 2):
            cols = slice(p * 2 * DH, (p + 1) * 2 * DH)
            share = 1.0 / l_ref[qb, p : p + 1, :]
            shares = jnp.concatenate(
                [
                    jnp.broadcast_to(share[:, :size], (DH, size)),
                    jnp.broadcast_to(share[:, size:], (DH, size)),
                ],
                axis=0,
            )
            both = acc_ref[qb, cols, :] * shares + lin_ref[cols, rows]
            comb_ref[rows, cols] = both.T.astype(BF16)
        return carry

    lax.fori_loop(0, queries, finish, 0)

    def update_tile(j, carry):
        cols = tile(j, 256)
        out_ref[:, cols] = dot_nn(comb_ref[...], wo_ref[:, cols]).astype(BF16)
        return carry

    lax.fori_loop(0, wo_ref.shape[1] // 256, update_tile, 0)


def call(kernel, name, ins, outs, flops, smem=0, scratch=(), aliases=None, limit=40 * MIB):
    size = sum(a.size * a.dtype.itemsize for a in ins)
    return pl.pallas_call(
        kernel,
        name=name,
        in_specs=[SMEM] * smem + [VMEM] * (len(ins) - smem),
        out_specs=[VMEM] * len(outs),
        out_shape=[jax.ShapeDtypeStruct(s, d) for s, d in outs],
        scratch_shapes=list(scratch),
        input_output_aliases=aliases or {},
        cost_estimate=pl.CostEstimate(flops=flops, bytes_accessed=size, transcendentals=0),
        compiler_params=pltpu.CompilerParams(vmem_limit_bytes=limit),
    )(*ins)


def on_device(tokens, qk_weight, value_weight, out_weight, neighbour_list, neighbour_count):
    rows = tokens.shape[1]
    width = tokens.shape[2]
    blocks = neighbour_list.shape[1]
    size = rows // blocks
    count = lax.axis_size("seq")
    position = lax.axis_index("seq").astype(jnp.int32).reshape(1)
    own = tokens[0]
    lists = neighbour_list[0]
    counts = neighbour_count[0]
    tables = (lists, counts, position)

    partner = [(i, i ^ 1) for i in range(count)]
    onward = [(i, i + 2) for i in range(0, count - 2, 2)] + [(i, i - 2) for i in range(3, count, 2)]
    near = [
        lax.ppermute(own[c * size : (c + 1) * size], "seq", partner) for c in range(blocks)
    ]
    far = [lax.ppermute(piece, "seq", onward) for piece in near]

    value_t = value_weight.T
    keyed, features, values_t, state = call(
        own_kernel,
        "own",
        (own, qk_weight, value_t),
        [((rows, width), BF16), ((rows, width), BF16), ((width, rows), BF16), ((width, DL), BF16)],
        4 * rows * width * width,
    )
    sent = lax.all_to_all(state, "seq", 0, 0, tiled=True)
    (before,) = call(
        functools.partial(before_kernel, count), "before", (sent,), [((width, DL), BF16)], width * DL
    )
    earlier = lax.all_to_all(before, "seq", 0, 0, tiled=True)
    (within,) = call(
        within_kernel, "within", (features, values_t), [((width, rows), F32)], 3 * rows * rows * width
    )
    softmax = call(
        functools.partial(own_attention_kernel, size),
        "own_attention",
        tables + (keyed, values_t),
        [
            ((blocks, H // 2, 2 * size), F32),
            ((blocks, H // 2, 2 * size), F32),
            ((blocks, width, size), F32),
        ],
        8 * rows * rows * width,
        smem=3,
    )
    (linear,) = call(
        linear_kernel, "linear", (features, within, earlier), [((width, rows), F32)], 2 * rows * DL * width
    )

    def scratch_for(total):
        return (
            pltpu.VMEM((total, width), BF16),
            pltpu.VMEM((total, width), BF16),
            pltpu.VMEM((width, total), BF16),
        )

    stages = [[("partner", 0)]]
    for c in range(1, blocks):
        stages.append([("partner", c), ("onward", c - 1)])
    shapes = [(a.shape, a.dtype) for a in softmax]
    for pieces in stages:
        arrays = tuple(near[c] if kind == "partner" else far[c] for kind, c in pieces)
        ins = tables + arrays + (qk_weight, value_t, keyed) + tuple(softmax)
        first = len(ins) - 3
        softmax = call(
            functools.partial(halo_kernel, size, pieces),
            "halo",
            ins,
            shapes,
            4 * len(pieces) * size * width * width,
            smem=3,
            scratch=scratch_for(size * len(pieces)),
            aliases={first + i: i for i in range(3)},
        )
    pieces = [("onward", blocks - 1)]
    ins = tables + (far[-1], qk_weight, value_t, keyed, linear, out_weight) + tuple(softmax)
    first = len(ins) - 3
    update, *_ = call(
        functools.partial(final_kernel, size, pieces),
        "final",
        ins,
        [((rows, width), BF16)] + shapes,
        4 * size * width * width + 2 * rows * width * width,
        smem=3,
        scratch=(pltpu.VMEM((rows, width), BF16),) + scratch_for(size),
        aliases={first + i: i + 1 for i in range(3)},
    )
    return update[None]


def solution(mesh):
    placed = (
        P(("groups", "dp"), "seq", None),
        P(),
        P(),
        P(),
        P(("groups", "dp"), "seq", None),
        P(("groups", "dp"), "seq"),
    )
    return jax.shard_map(
        on_device,
        mesh=mesh,
        in_specs=placed,
        out_specs=P(("groups", "dp"), "seq", None),
        check_vma=False,
    )
```

```python
import functools

import jax
import jax.numpy as jnp
from jax import lax
from jax.experimental import pallas as pl
from jax.experimental.pallas import tpu as pltpu
from jax.sharding import PartitionSpec as P

H = 16
DH = 64
HL = 8
DL = 128
F32 = jnp.float32
BF16 = jnp.bfloat16
NT = (((1,), (1,)), ((), ()))
VMEM = pl.BlockSpec(memory_space=pltpu.VMEM)
SMEM = pl.BlockSpec(memory_space=pltpu.SMEM)
MIB = 1 << 20


def dot_nt(a, b):
    return lax.dot_general(a, b, NT, preferred_element_type=F32)


def dot_nn(a, b):
    return jnp.dot(a, b, preferred_element_type=F32)


def tile(i, size):
    return pl.ds(pl.multiple_of(i * size, size), size)


def project(x, wk_ref, wvt_ref, k_ref, vt_ref):
    k_ref[...] = dot_nn(x, wk_ref[...]).astype(BF16)
    vt_ref[...] = dot_nt(wvt_ref[...], x).astype(BF16)


def own_kernel(x_ref, wk_ref, wvt_ref, k_ref, f_ref, vt_ref, s_ref):
    project(x_ref[...], wk_ref, wvt_ref, k_ref, vt_ref)
    for h in range(HL):
        part = slice(h * DL, (h + 1) * DL)
        k = k_ref[:, part].astype(F32)
        f = (k / (1.0 + jnp.exp(-k))).astype(BF16)
        f_ref[:, part] = f
        s_ref[part, :] = dot_nn(vt_ref[part, :], f).astype(BF16)


def within_kernel(f_ref, vt_ref, n_ref):
    rows = f_ref.shape[0]
    half = rows // 2
    upper = lax.broadcasted_iota(jnp.int32, (half, half), 0) <= lax.broadcasted_iota(
        jnp.int32, (half, half), 1
    )

    def head(h, carry):
        cols = tile(h, DL)
        f0 = f_ref[:half, cols]
        f1 = f_ref[half:, cols]
        v0 = vt_ref[cols, :half]
        v1 = vt_ref[cols, half:]
        a00 = jnp.where(upper, dot_nt(f0, f0), 0.0).astype(BF16)
        a01 = dot_nt(f0, f1).astype(BF16)
        a11 = jnp.where(upper, dot_nt(f1, f1), 0.0).astype(BF16)
        n_ref[cols, :half] = dot_nn(v0, a00)
        n_ref[cols, half:] = dot_nn(v0, a01) + dot_nn(v1, a11)
        return carry

    lax.fori_loop(0, HL, head, 0, unroll=2)


def linear_kernel(stages, pos_ref, f_ref, n_ref, *refs):
    heard = refs[:stages]
    o_ref = refs[stages]
    bits = [((pos_ref[0] >> k) & 1).astype(F32) for k in range(stages)]

    def head(h, carry):
        cols = tile(h, DL)
        before = sum(ref[cols, :].astype(F32) * bit for ref, bit in zip(heard, bits)).astype(BF16)
        n = n_ref[cols, :] + dot_nt(before, f_ref[:, cols])
        mean = jnp.sum(n * n, axis=0, keepdims=True) * (1.0 / DL)
        o_ref[cols, :] = n * lax.rsqrt(mean + 1e-06)
        return carry

    lax.fori_loop(0, HL, head, 0, unroll=2)


def listed(list_ref, count_ref, qb, block):
    found = False
    for j in range(list_ref.shape[1]):
        found = jnp.logical_or(
            found, jnp.logical_and(j < count_ref[qb], list_ref[qb, j] == block)
        )
    return found


def attend(first, size, qb, kbs, q_ref, k_ref, vt_ref, m_ref, l_ref, acc_ref):
    qrows = tile(qb, size)
    krows = [tile(kb, size) for kb in kbs]
    lane = lax.broadcasted_iota(jnp.int32, (size, 2 * DH), 1)
    pairs = H // 2
    cols = [slice(p * 2 * DH, (p + 1) * 2 * DH) for p in range(pairs)]
    if first:
        shape = (size * len(kbs), 2 * size)
        key = lax.broadcasted_iota(jnp.int32, shape, 0)
        query = lax.broadcasted_iota(jnp.int32, shape, 1) % size
        other = key != query
    else:
        tops = m_ref[qb]
        totals = l_ref[qb]
    scores = []
    for p in range(pairs):
        q = q_ref[qrows, cols[p]] * jnp.asarray(DH ** (-0.5), BF16)
        zero = jnp.zeros_like(q)
        pair = jnp.concatenate([jnp.where(lane < DH, q, zero), jnp.where(lane < DH, zero, q)], axis=0)
        k = jnp.concatenate([k_ref[r, cols[p]] for r in krows], axis=0)
        s = dot_nt(k, pair)
        scores.append(jnp.where(other, s, -1e30) if first else s)
    raised = []
    new_tops = []
    new_totals = []
    for p in range(pairs):
        top = jnp.max(scores[p], axis=0, keepdims=True)
        if not first:
            top = jnp.maximum(top, tops[p : p + 1])
        e = jnp.exp(scores[p] - top)
        new_tops.append(top)
        new_totals.append(jnp.sum(e, axis=0, keepdims=True))
        raised.append(e.astype(BF16))
    for p in range(pairs):
        v = jnp.concatenate([vt_ref[cols[p], r] for r in krows], axis=1)
        o = dot_nn(v, raised[p])
        o = jnp.concatenate([o[:DH, :size], o[DH:, size:]], axis=0)
        if not first:
            fade = jnp.exp(tops[p : p + 1] - new_tops[p])
            new_totals[p] = new_totals[p] + totals[p : p + 1] * fade
            o = o + acc_ref[qb, cols[p], :] * by_head(fade, size)
        acc_ref[qb, cols[p], :] = o
    m_ref[qb] = jnp.concatenate(new_tops, axis=0)
    l_ref[qb] = jnp.concatenate(new_totals, axis=0)


def by_head(row, size):
    return jnp.concatenate(
        [jnp.broadcast_to(row[:, :size], (DH, size)), jnp.broadcast_to(row[:, size:], (DH, size))], axis=0
    )


def attend_listed(own, size, blocks, list_ref, count_ref, found_ref, *rest):
    def query(qb, carry):
        found_ref[0] = qb
        n = jnp.int32(1 if own else 0)
        for kb, block in enumerate(blocks):
            wanted = listed(list_ref, count_ref, qb, block)
            if own:
                wanted = jnp.logical_and(wanted, qb != kb)

            @pl.when(wanted)
            def _(n=n, kb=kb):
                found_ref[n] = kb

            n = n + wanted.astype(jnp.int32)
        start = 0
        if own:

            @pl.when(n == 1)
            def _():
                attend(True, size, qb, [qb], *rest)

            @pl.when(n > 1)
            def _():
                attend(True, size, qb, [qb, found_ref[1]], *rest)

            start = 2
        if len(blocks) - start > 1:

            def two(i, carry):
                attend(False, size, qb, [found_ref[start + 2 * i], found_ref[start + 2 * i + 1]], *rest)
                return carry

            lax.fori_loop(0, jnp.maximum(n - start, 0) // 2, two, 0)

        @pl.when(jnp.logical_and(n > start, n % 2 == 1))
        def _():
            attend(False, size, qb, [found_ref[n - 1]], *rest)

        return carry

    lax.fori_loop(0, list_ref.shape[0], query, 0)


def own_attention_kernel(size, list_ref, count_ref, pos_ref, k_ref, vt_ref, m_ref, l_ref, acc_ref, found_ref):
    queries = list_ref.shape[0]
    blocks = [pos_ref[0] * queries + kb for kb in range(queries)]
    attend_listed(
        True, size, blocks, list_ref, count_ref, found_ref, k_ref, k_ref, vt_ref, m_ref, l_ref, acc_ref
    )


def attend_halo(size, pieces, list_ref, count_ref, pos_ref, piece_refs, wk_ref, wvt_ref, q_ref, state, scratch):
    found_ref, x_ref, k_ref, vt_ref = scratch
    queries = list_ref.shape[0]
    pos = pos_ref[0]
    step = 1 - 2 * (pos % 2)
    row = 0
    blocks = []
    for (near, first), ref in zip(pieces, piece_refs):
        rows = ref.shape[0]
        x_ref[row : row + rows, :] = ref[...]
        row += rows
        run = pos + step if near else pos - step
        blocks += [run * queries + first + i for i in range(rows // size)]
    project(x_ref[...], wk_ref, wvt_ref, k_ref, vt_ref)
    attend_listed(
        False, size, blocks, list_ref, count_ref, found_ref, q_ref, k_ref, vt_ref, *state
    )


def halo_kernel(size, pieces, list_ref, count_ref, pos_ref, *refs):
    n = len(pieces)
    wk_ref, wvt_ref, q_ref = refs[n : n + 3]
    attend_halo(
        size, pieces, list_ref, count_ref, pos_ref, refs[:n], wk_ref, wvt_ref, q_ref, refs[n + 6 : n + 9], refs[n + 9 :]
    )


def final_kernel(size, pieces, list_ref, count_ref, pos_ref, *refs):
    n = len(pieces)
    wk_ref, wvt_ref, q_ref, lin_ref, wo_ref = refs[n : n + 5]
    out_ref, m_ref, l_ref, acc_ref, comb_ref = refs[n + 8 : n + 13]
    attend_halo(
        size,
        pieces,
        list_ref,
        count_ref,
        pos_ref,
        refs[:n],
        wk_ref,
        wvt_ref,
        q_ref,
        (m_ref, l_ref, acc_ref),
        refs[n + 13 :],
    )

    def finish(qb, carry):
        rows = tile(qb, size)
        share = 1.0 / l_ref[qb]
        for p in range(H // 2):
            cols = slice(p * 2 * DH, (p + 1) * 2 * DH)
            both = acc_ref[qb, cols, :] * by_head(share[p : p + 1], size) + lin_ref[cols, rows]
            comb_ref[rows, cols] = both.T.astype(BF16)
        return carry

    lax.fori_loop(0, list_ref.shape[0], finish, 0)
    out_ref[...] = dot_nn(comb_ref[...], wo_ref[...]).astype(BF16)


def call(kernel, name, ins, outs, smem=0, scratch=(), aliases=None, limit=20 * MIB):
    return pl.pallas_call(
        kernel,
        name=name,
        in_specs=[SMEM] * smem + [VMEM] * (len(ins) - smem),
        out_specs=[VMEM] * len(outs),
        out_shape=[jax.ShapeDtypeStruct(s, d) for s, d in outs],
        scratch_shapes=list(scratch),
        input_output_aliases=aliases or {},
        cost_estimate=pl.CostEstimate(flops=1000, bytes_accessed=1000, transcendentals=0),
        compiler_params=pltpu.CompilerParams(vmem_limit_bytes=limit),
    )(*ins)


def after(value, *done):
    return lax.optimization_barrier((value,) + done)[0]


def on_device(tokens, qk_weight, value_weight, out_weight, neighbour_list, neighbour_count):
    rows = tokens.shape[1]
    width = tokens.shape[2]
    blocks = neighbour_list.shape[1]
    size = rows // blocks
    half = blocks // 2
    count = lax.axis_size("seq")
    position = lax.axis_index("seq").astype(jnp.int32).reshape(1)
    own = tokens[0]
    tables = (neighbour_list[0], neighbour_count[0], position)

    def swap(value, bit):
        return lax.ppermute(value, "seq", [(i, i ^ bit) for i in range(count)])

    def onward(value):
        pairs = [(i, i + 2) for i in range(0, count - 2, 2)] + [(i, i - 2) for i in range(3, count, 2)]
        return lax.ppermute(value, "seq", pairs)

    def across(value):
        odd = range(1, count - 1, 2)
        return lax.ppermute(value, "seq", [(i, i + 1) for i in odd] + [(i + 1, i) for i in odd])

    def flat(total):
        return (
            pltpu.SMEM((total // size + 2,), jnp.int32),
            pltpu.VMEM((total, width), BF16),
            pltpu.VMEM((total, width), BF16),
            pltpu.VMEM((width, total), BF16),
        )

    def join_halo(softmax, pieces, arrays):
        ins = tables + tuple(arrays) + (qk_weight, value_t, keyed) + tuple(softmax)
        first = len(ins) - 3
        return call(
            functools.partial(halo_kernel, size, pieces),
            "halo",
            ins,
            shapes,
            smem=3,
            scratch=flat(sum(a.shape[0] for a in arrays)),
            aliases={first + i: i for i in range(3)},
        )

    cuts = [0, half * size, (half + 1) * size, rows]
    near_a = swap(own[: cuts[1]], 1)
    value_t = value_weight.T
    keyed, features, values_t, state = call(
        own_kernel,
        "own",
        (own, qk_weight, value_t),
        [((rows, width), BF16), ((rows, width), BF16), ((width, rows), BF16), ((width, DL), BF16)],
    )
    heard = [swap(state, 1)]
    rest = after(own, state)
    near_b = swap(rest[cuts[1] : cuts[2]], 1)
    near_c = swap(rest[cuts[2] :], 1)
    far_c = across(rest[cuts[2] :])
    shapes = [((blocks, H // 2, 2 * size), F32)] * 2 + [((blocks, width, size), F32)]
    softmax = call(
        functools.partial(own_attention_kernel, size),
        "own_attention",
        tables + (keyed, values_t),
        shapes,
        smem=3,
        scratch=(pltpu.SMEM((blocks + 1,), jnp.int32),),
    )
    far_a = onward(after(near_a, softmax[0]))
    total = state + after(heard[0], softmax[0])
    heard.append(swap(total, 2))
    (within,) = call(
        within_kernel,
        "within",
        (after(features, near_a, total), values_t),
        [((width, rows), F32)],
    )
    softmax = join_halo(softmax, [(True, 0)], [after(near_a, within)])
    far_b = onward(after(near_b, softmax[0]))
    stride = 4
    while stride < count:
        total = total + after(heard[-1], softmax[0])
        heard.append(swap(total, stride))
        stride *= 2
    softmax = join_halo(
        softmax, [(True, half), (False, 0)], [after(near_b, total), far_a]
    )
    (linear,) = call(
        functools.partial(linear_kernel, len(heard)),
        "linear",
        (position, after(features, softmax[0]), within) + tuple(heard),
        [((width, rows), F32)],
        smem=1,
    )
    softmax = join_halo(softmax, [(False, half)], [after(far_b, linear)])
    pieces = [(True, half + 1), (False, half + 1)]
    arrays = (near_c, far_c)
    ins = tables + arrays + (qk_weight, value_t, keyed, linear, out_weight) + tuple(softmax)
    first = len(ins) - 3
    update, *_ = call(
        functools.partial(final_kernel, size, pieces),
        "final",
        ins,
        [((rows, width), BF16)] + shapes,
        smem=3,
        scratch=(pltpu.VMEM((rows, width), BF16),) + flat(sum(a.shape[0] for a in arrays)),
        aliases={first + i: i + 1 for i in range(3)},
    )
    return update[None]


def solution(mesh):
    placed = (
        P(("groups", "dp"), "seq", None),
        P(),
        P(),
        P(),
        P(("groups", "dp"), "seq", None),
        P(("groups", "dp"), "seq"),
    )
    return jax.shard_map(
        on_device,
        mesh=mesh,
        in_specs=placed,
        out_specs=P(("groups", "dp"), "seq", None),
        check_vma=False,
    )
```

```python
import functools

import jax
import jax.numpy as jnp
from jax import lax
from jax.experimental import pallas as pl
from jax.experimental.pallas import tpu as pltpu
from jax.sharding import PartitionSpec as P

H = 16
DH = 64
HL = 8
DL = 128
F32 = jnp.float32
BF16 = jnp.bfloat16
NT = (((1,), (1,)), ((), ()))
SMEM = pl.BlockSpec(memory_space=pltpu.SMEM)
MIB = 1 << 20


def dot_nt(a, b):
    return lax.dot_general(a, b, NT, preferred_element_type=F32)


def dot_nn(a, b):
    return jnp.dot(a, b, preferred_element_type=F32)


def tile(i, size):
    return pl.ds(pl.multiple_of(i * size, size), size)


def project(x, wk_ref, wvt_ref, k_ref, vt_ref):
    k_ref[...] = dot_nn(x, wk_ref[...]).astype(BF16)
    vt_ref[...] = dot_nt(wvt_ref[...], x).astype(BF16)


def cut_kernel(x_ref, a_ref, sem):
    copy = pltpu.make_async_copy(x_ref.at[: a_ref.shape[0]], a_ref, sem)
    copy.start()
    copy.wait()


def own_kernel(x_hbm, wk_hbm, wv_hbm, k_ref, f_ref, vt_ref, s_ref, wvt_ref, x_ref, wk_ref, wv_ref, sems):
    width = x_ref.shape[1]
    step = 256
    tiles = [slice(i, i + step) for i in range(0, width, step)]
    n = len(tiles)
    copies = [pltpu.make_async_copy(x_hbm, x_ref, sems.at[0])]
    for i, (src, dst) in enumerate(((wk_hbm, wk_ref), (wv_hbm, wv_ref))):
        for j, part in enumerate(tiles):
            copies.append(pltpu.make_async_copy(src.at[:, part], dst.at[:, part], sems.at[1 + i * n + j]))
    for copy in copies:
        copy.start()
    copies[0].wait()
    for j, part in enumerate(tiles):
        copies[1 + j].wait()
        k = dot_nn(x_ref[...], wk_ref[:, part]).astype(BF16)
        k_ref[:, part] = k
        k = k.astype(F32)
        f_ref[:, part] = (k / (1.0 + jnp.exp(-k))).astype(BF16)
    for j, part in enumerate(tiles):
        copies[1 + n + j].wait()
        turned = wv_ref[:, part].T
        wvt_ref[part, :] = turned
        vt_ref[part, :] = dot_nt(turned, x_ref[...]).astype(BF16)
        for h in range(part.start, part.stop, DL):
            head = slice(h, h + DL)
            s_ref[head, :] = dot_nn(vt_ref[head, :], f_ref[:, head]).astype(BF16)


def within_kernel(f_ref, vt_ref, n_ref):
    rows = f_ref.shape[0]
    half = rows // 2
    upper = lax.broadcasted_iota(jnp.int32, (half, half), 0) <= lax.broadcasted_iota(
        jnp.int32, (half, half), 1
    )

    def head(h, carry):
        cols = tile(h, DL)
        f0 = f_ref[:half, cols]
        f1 = f_ref[half:, cols]
        v0 = vt_ref[cols, :half]
        v1 = vt_ref[cols, half:]
        a00 = jnp.where(upper, dot_nt(f0, f0), 0.0).astype(BF16)
        a01 = dot_nt(f0, f1).astype(BF16)
        a11 = jnp.where(upper, dot_nt(f1, f1), 0.0).astype(BF16)
        n_ref[cols, :half] = dot_nn(v0, a00)
        n_ref[cols, half:] = dot_nn(v0, a01) + dot_nn(v1, a11)
        return carry

    lax.fori_loop(0, HL, head, 0, unroll=2)


def linear_kernel(stages, pos_ref, f_ref, n_ref, *refs):
    heard = refs[:stages]
    o_ref = refs[stages]
    bits = [((pos_ref[0] >> k) & 1).astype(F32) for k in range(stages)]

    def head(h, carry):
        cols = tile(h, DL)
        before = sum(ref[cols, :].astype(F32) * bit for ref, bit in zip(heard, bits)).astype(BF16)
        n = n_ref[cols, :] + dot_nt(before, f_ref[:, cols])
        mean = jnp.sum(n * n, axis=0, keepdims=True) * (1.0 / DL)
        o_ref[cols, :] = n * lax.rsqrt(mean + 1e-06)
        return carry

    lax.fori_loop(0, HL, head, 0, unroll=2)


def listed(list_ref, count_ref, qb, block):
    found = False
    for j in range(list_ref.shape[1]):
        found = jnp.logical_or(
            found, jnp.logical_and(j < count_ref[qb], list_ref[qb, j] == block)
        )
    return found


def attend(first, size, qb, kbs, q_ref, k_ref, vt_ref, m_ref, l_ref, acc_ref):
    qrows = tile(qb, size)
    krows = [tile(kb, size) for kb in kbs]
    lane = lax.broadcasted_iota(jnp.int32, (size, 2 * DH), 1)
    pairs = H // 2
    cols = [slice(p * 2 * DH, (p + 1) * 2 * DH) for p in range(pairs)]
    if first:
        shape = (size * len(kbs), 2 * size)
        key = lax.broadcasted_iota(jnp.int32, shape, 0)
        query = lax.broadcasted_iota(jnp.int32, shape, 1) % size
        other = key != query
    else:
        tops = m_ref[qb]
        totals = l_ref[qb]
    scores = []
    for p in range(pairs):
        q = q_ref[qrows, cols[p]] * jnp.asarray(DH ** (-0.5), BF16)
        zero = jnp.zeros_like(q)
        pair = jnp.concatenate([jnp.where(lane < DH, q, zero), jnp.where(lane < DH, zero, q)], axis=0)
        k = jnp.concatenate([k_ref[r, cols[p]] for r in krows], axis=0)
        s = dot_nt(k, pair)
        scores.append(jnp.where(other, s, -1e30) if first else s)
    raised = []
    new_tops = []
    new_totals = []
    for p in range(pairs):
        top = jnp.max(scores[p], axis=0, keepdims=True)
        if not first:
            top = jnp.maximum(top, tops[p : p + 1])
        e = jnp.exp(scores[p] - top)
        new_tops.append(top)
        new_totals.append(jnp.sum(e, axis=0, keepdims=True))
        raised.append(e.astype(BF16))
    for p in range(pairs):
        v = jnp.concatenate([vt_ref[cols[p], r] for r in krows], axis=1)
        o = dot_nn(v, raised[p])
        o = jnp.concatenate([o[:DH, :size], o[DH:, size:]], axis=0)
        if not first:
            fade = jnp.exp(tops[p : p + 1] - new_tops[p])
            new_totals[p] = new_totals[p] + totals[p : p + 1] * fade
            o = o + acc_ref[qb, cols[p], :] * by_head(fade, size)
        acc_ref[qb, cols[p], :] = o
    m_ref[qb] = jnp.concatenate(new_tops, axis=0)
    l_ref[qb] = jnp.concatenate(new_totals, axis=0)


def by_head(row, size):
    return jnp.concatenate(
        [jnp.broadcast_to(row[:, :size], (DH, size)), jnp.broadcast_to(row[:, size:], (DH, size))], axis=0
    )


def attend_listed(own, size, blocks, list_ref, count_ref, found_ref, *rest):
    def query(qb, carry):
        found_ref[0] = qb
        n = jnp.int32(1 if own else 0)
        for kb, block in enumerate(blocks):
            wanted = listed(list_ref, count_ref, qb, block)
            if own:
                wanted = jnp.logical_and(wanted, qb != kb)

            @pl.when(wanted)
            def _(n=n, kb=kb):
                found_ref[n] = kb

            n = n + wanted.astype(jnp.int32)
        start = 0
        if own:

            @pl.when(n == 1)
            def _():
                attend(True, size, qb, [qb], *rest)

            @pl.when(n > 1)
            def _():
                attend(True, size, qb, [qb, found_ref[1]], *rest)

            start = 2
        if len(blocks) - start > 1:

            def two(i, carry):
                attend(False, size, qb, [found_ref[start + 2 * i], found_ref[start + 2 * i + 1]], *rest)
                return carry

            lax.fori_loop(0, jnp.maximum(n - start, 0) // 2, two, 0)

        @pl.when(jnp.logical_and(n > start, n % 2 == 1))
        def _():
            attend(False, size, qb, [found_ref[n - 1]], *rest)

        return carry

    lax.fori_loop(0, list_ref.shape[0], query, 0)


def own_attention_kernel(size, list_ref, count_ref, pos_ref, k_ref, vt_ref, m_ref, l_ref, acc_ref, found_ref):
    queries = list_ref.shape[0]
    blocks = [pos_ref[0] * queries + kb for kb in range(queries)]
    attend_listed(
        True, size, blocks, list_ref, count_ref, found_ref, k_ref, k_ref, vt_ref, m_ref, l_ref, acc_ref
    )


def attend_halo(size, pieces, list_ref, count_ref, pos_ref, piece_refs, wk_ref, wvt_ref, q_ref, state, scratch):
    found_ref, x_ref, k_ref, vt_ref = scratch
    queries = list_ref.shape[0]
    pos = pos_ref[0]
    step = 1 - 2 * (pos % 2)
    row = 0
    blocks = []
    for (near, first), ref in zip(pieces, piece_refs):
        rows = ref.shape[0]
        x_ref[row : row + rows, :] = ref[...]
        row += rows
        run = pos + step if near else pos - step
        blocks += [run * queries + first + i for i in range(rows // size)]
    project(x_ref[...], wk_ref, wvt_ref, k_ref, vt_ref)
    attend_listed(
        False, size, blocks, list_ref, count_ref, found_ref, q_ref, k_ref, vt_ref, *state
    )


def halo_kernel(size, pieces, list_ref, count_ref, pos_ref, *refs):
    n = len(pieces)
    wk_ref, wvt_ref, q_ref = refs[n : n + 3]
    attend_halo(
        size, pieces, list_ref, count_ref, pos_ref, refs[:n], wk_ref, wvt_ref, q_ref, refs[n + 6 : n + 9], refs[n + 9 :]
    )


def final_kernel(size, pieces, list_ref, count_ref, pos_ref, *refs):
    n = len(pieces)
    wk_ref, wvt_ref, q_ref, lin_ref, wo_ref = refs[n : n + 5]
    out_ref, m_ref, l_ref, acc_ref, comb_ref = refs[n + 8 : n + 13]
    attend_halo(
        size,
        pieces,
        list_ref,
        count_ref,
        pos_ref,
        refs[:n],
        wk_ref,
        wvt_ref,
        q_ref,
        (m_ref, l_ref, acc_ref),
        refs[n + 13 :],
    )

    def finish(qb, carry):
        rows = tile(qb, size)
        share = 1.0 / l_ref[qb]
        for p in range(H // 2):
            cols = slice(p * 2 * DH, (p + 1) * 2 * DH)
            both = acc_ref[qb, cols, :] * by_head(share[p : p + 1], size) + lin_ref[cols, rows]
            comb_ref[rows, cols] = both.T.astype(BF16)
        return carry

    lax.fori_loop(0, list_ref.shape[0], finish, 0)
    out_ref[...] = dot_nn(comb_ref[...], wo_ref[...]).astype(BF16)


COSTLY = ("halo_b",)


def call(
    kernel,
    name,
    ins,
    outs,
    smem=0,
    scratch=(),
    aliases=None,
    limit=20 * MIB,
    space=pltpu.VMEM,
    out_space=pltpu.VMEM,
):
    return pl.pallas_call(
        kernel,
        name=name,
        in_specs=[SMEM] * smem + [pl.BlockSpec(memory_space=space)] * (len(ins) - smem),
        out_specs=[pl.BlockSpec(memory_space=out_space)] * len(outs),
        out_shape=[jax.ShapeDtypeStruct(s, d) for s, d in outs],
        scratch_shapes=list(scratch),
        input_output_aliases=aliases or {},
        cost_estimate=pl.CostEstimate(
            flops=10**11 if name in COSTLY else 1, bytes_accessed=1000, transcendentals=0
        ),
        compiler_params=pltpu.CompilerParams(vmem_limit_bytes=limit),
    )(*ins)


def after(value, *done):
    return lax.optimization_barrier((value,) + done)[0]


def on_device(tokens, qk_weight, value_weight, out_weight, neighbour_list, neighbour_count):
    rows = tokens.shape[1]
    width = tokens.shape[2]
    blocks = neighbour_list.shape[1]
    size = rows // blocks
    half = blocks // 2
    count = lax.axis_size("seq")
    position = lax.axis_index("seq").astype(jnp.int32).reshape(1)
    own = tokens[0]
    tables = (neighbour_list[0], neighbour_count[0], position)

    def swap(value, bit):
        return lax.ppermute(value, "seq", [(i, i ^ bit) for i in range(count)])

    def onward(value):
        pairs = [(i, i + 2) for i in range(0, count - 2, 2)] + [(i, i - 2) for i in range(3, count, 2)]
        return lax.ppermute(value, "seq", pairs)

    def across(value):
        odd = range(1, count - 1, 2)
        return lax.ppermute(value, "seq", [(i, i + 1) for i in odd] + [(i + 1, i) for i in odd])

    def flat(total):
        return (
            pltpu.SMEM((total // size + 2,), jnp.int32),
            pltpu.VMEM((total, width), BF16),
            pltpu.VMEM((total, width), BF16),
            pltpu.VMEM((width, total), BF16),
        )

    def join_halo(name, softmax, pieces, arrays):
        ins = tables + tuple(arrays) + (qk_weight, value_t, keyed) + tuple(softmax)
        first = len(ins) - 3
        return call(
            functools.partial(halo_kernel, size, pieces),
            name,
            ins,
            shapes,
            smem=3,
            scratch=flat(sum(a.shape[0] for a in arrays)),
            aliases={first + i: i for i in range(3)},
        )

    cuts = [0, half * size, (half + 1) * size, rows]
    (first_rows,) = call(
        cut_kernel,
        "cut",
        (own,),
        [((cuts[1], width), BF16)],
        scratch=(pltpu.SemaphoreType.DMA(()),),
        limit=60 * MIB,
        space=pltpu.HBM,
        out_space=pltpu.HBM,
    )
    near_a = swap(first_rows, 1)
    keyed, features, values_t, state, value_t = call(
        own_kernel,
        "own",
        (own, qk_weight, value_weight),
        [
            ((rows, width), BF16),
            ((rows, width), BF16),
            ((width, rows), BF16),
            ((width, DL), BF16),
            ((width, width), BF16),
        ],
        scratch=(
            pltpu.VMEM((rows, width), BF16),
            pltpu.VMEM((width, width), BF16),
            pltpu.VMEM((width, width), BF16),
            pltpu.SemaphoreType.DMA((1 + 2 * (width // 256),)),
        ),
        limit=50 * MIB,
        space=pltpu.HBM,
    )
    heard = [swap(state, 1)]
    rest = after(own, state)
    near_b = swap(rest[cuts[1] : cuts[2]], 1)
    near_c = swap(rest[cuts[2] :], 1)
    far_c = across(rest[cuts[2] :])
    shapes = [((blocks, H // 2, 2 * size), F32)] * 2 + [((blocks, width, size), F32)]
    softmax = call(
        functools.partial(own_attention_kernel, size),
        "own_attention",
        tables + (after(keyed, near_a), values_t),
        shapes,
        smem=3,
        scratch=(pltpu.SMEM((blocks + 1,), jnp.int32),),

    )
    far_a = onward(near_a)
    total = state + after(heard[0], softmax[0])
    heard.append(swap(total, 2))
    (within,) = call(
        within_kernel,
        "within",
        (after(features, near_a, total), values_t),
        [((width, rows), F32)],
    )
    softmax = join_halo("halo_a", softmax, [(True, 0)], [after(near_a, within)])
    far_b = onward(after(near_b, softmax[0]))
    stride = 4
    while stride < count:
        total = total + after(heard[-1], softmax[0])
        heard.append(swap(total, stride))
        stride *= 2
    softmax = join_halo(
        "halo_b", softmax, [(True, half), (False, 0)], [after(near_b, total), far_a]
    )
    (linear,) = call(
        functools.partial(linear_kernel, len(heard)),
        "linear",
        (position, after(features, softmax[0]), within) + tuple(heard),
        [((width, rows), F32)],
        smem=1,
    )
    softmax = join_halo("halo_c", softmax, [(False, half)], [after(far_b, linear)])
    pieces = [(True, half + 1), (False, half + 1)]
    arrays = (near_c, far_c)
    ins = tables + arrays + (qk_weight, value_t, keyed, linear, out_weight) + tuple(softmax)
    first = len(ins) - 3
    update, *_ = call(
        functools.partial(final_kernel, size, pieces),
        "final",
        ins,
        [((rows, width), BF16)] + shapes,
        smem=3,
        scratch=(pltpu.VMEM((rows, width), BF16),) + flat(sum(a.shape[0] for a in arrays)),
        aliases={first + i: i + 1 for i in range(3)},
    )
    return update[None]


def solution(mesh):
    placed = (
        P(("groups", "dp"), "seq", None),
        P(),
        P(),
        P(),
        P(("groups", "dp"), "seq", None),
        P(("groups", "dp"), "seq"),
    )
    return jax.shard_map(
        on_device,
        mesh=mesh,
        in_specs=placed,
        out_specs=P(("groups", "dp"), "seq", None),
        check_vma=False,
    )
```

```python
import functools

import jax
import jax.numpy as jnp
from jax import lax
from jax.experimental import pallas as pl
from jax.experimental.pallas import tpu as pltpu
from jax.sharding import PartitionSpec as P

H = 16
DH = 64
HL = 8
DL = 128
F32 = jnp.float32
BF16 = jnp.bfloat16
NT = (((1,), (1,)), ((), ()))
SMEM = pl.BlockSpec(memory_space=pltpu.SMEM)
MIB = 1 << 20


def dot_nt(a, b):
    return lax.dot_general(a, b, NT, preferred_element_type=F32)


def dot_nn(a, b):
    return jnp.dot(a, b, preferred_element_type=F32)


def tile(i, size):
    return pl.ds(pl.multiple_of(i * size, size), size)


def project(x, wk_ref, wvt_ref, k_ref, vt_ref):
    k_ref[...] = dot_nn(x, wk_ref[...]).astype(BF16)
    vt_ref[...] = dot_nt(wvt_ref[...], x).astype(BF16)


def cut_kernel(x_hbm, a_ref, sem):
    copy = pltpu.make_async_copy(x_hbm.at[: a_ref.shape[0]], a_ref, sem)
    copy.start()
    copy.wait()


def own_kernel(
    x_hbm, wk_hbm, wv_hbm, k_hbm, f_hbm, vt_hbm, wvt_hbm, b_hbm, s_ref, x_ref, wk_ref, wv_ref, k_ref, f_ref, vt_ref,
    wvt_ref, in_sems, out_sems
):
    width = x_ref.shape[1]
    step = 256
    tiles = [slice(i, i + step) for i in range(0, width, step)]
    n = len(tiles)
    ins = [pltpu.make_async_copy(x_hbm, x_ref, in_sems.at[0])]
    for i, (src, dst) in enumerate(((wk_hbm, wk_ref), (wv_hbm, wv_ref))):
        for j, part in enumerate(tiles):
            ins.append(pltpu.make_async_copy(src.at[:, part], dst.at[:, part], in_sems.at[1 + i * n + j]))
    for copy in ins:
        copy.start()
    outs = []

    def put(src, dst):
        copy = pltpu.make_async_copy(src, dst, out_sems.at[len(outs)])
        copy.start()
        outs.append(copy)

    ins[0].wait()
    put(x_ref.at[x_ref.shape[0] - b_hbm.shape[0] :], b_hbm)
    for j, part in enumerate(tiles):
        ins[1 + j].wait()
        k = dot_nn(x_ref[...], wk_ref[:, part]).astype(BF16)
        k_ref[:, part] = k
        put(k_ref.at[:, part], k_hbm.at[:, part])
        k = k.astype(F32)
        f_ref[:, part] = (k / (1.0 + jnp.exp(-k))).astype(BF16)
        put(f_ref.at[:, part], f_hbm.at[:, part])
    for j, part in enumerate(tiles):
        ins[1 + n + j].wait()
        turned = wv_ref[:, part].T
        wvt_ref[part, :] = turned
        put(wvt_ref.at[part], wvt_hbm.at[part])
        vt_ref[part, :] = dot_nt(turned, x_ref[...]).astype(BF16)
        put(vt_ref.at[part], vt_hbm.at[part])
        for h in range(part.start, part.stop, DL):
            head = slice(h, h + DL)
            s_ref[head, :] = dot_nn(vt_ref[head, :], f_ref[:, head]).astype(BF16)
    for copy in outs:
        copy.wait()


def add_within(f_ref, vt_ref, n_ref):
    rows = f_ref.shape[0]
    half = rows // 2
    upper = lax.broadcasted_iota(jnp.int32, (half, half), 0) <= lax.broadcasted_iota(
        jnp.int32, (half, half), 1
    )

    def head(h, carry):
        cols = tile(h, DL)
        f0 = f_ref[:half, cols]
        f1 = f_ref[half:, cols]
        v0 = vt_ref[cols, :half]
        v1 = vt_ref[cols, half:]
        a00 = jnp.where(upper, dot_nt(f0, f0), 0.0).astype(BF16)
        a01 = dot_nt(f0, f1).astype(BF16)
        a11 = jnp.where(upper, dot_nt(f1, f1), 0.0).astype(BF16)
        n_ref[cols, :half] = dot_nn(v0, a00)
        n_ref[cols, half:] = dot_nn(v0, a01) + dot_nn(v1, a11)
        return carry

    lax.fori_loop(0, HL, head, 0, unroll=2)


def linear_kernel(stages, pos_ref, f_ref, n_ref, *refs):
    heard = refs[:stages]
    o_ref = refs[stages]
    bits = [((pos_ref[0] >> k) & 1).astype(F32) for k in range(stages)]

    def head(h, carry):
        cols = tile(h, DL)
        before = sum(ref[cols, :].astype(F32) * bit for ref, bit in zip(heard, bits)).astype(BF16)
        n = n_ref[cols, :] + dot_nt(before, f_ref[:, cols])
        mean = jnp.sum(n * n, axis=0, keepdims=True) * (1.0 / DL)
        o_ref[cols, :] = n * lax.rsqrt(mean + 1e-06)
        return carry

    lax.fori_loop(0, HL, head, 0, unroll=2)


def listed(list_ref, count_ref, qb, block):
    found = False
    for j in range(list_ref.shape[1]):
        found = jnp.logical_or(
            found, jnp.logical_and(j < count_ref[qb], list_ref[qb, j] == block)
        )
    return found


def attend(first, size, qb, kbs, q_ref, k_ref, vt_ref, m_ref, l_ref, acc_ref):
    qrows = tile(qb, size)
    krows = [tile(kb, size) for kb in kbs]
    lane = lax.broadcasted_iota(jnp.int32, (size, 2 * DH), 1)
    pairs = H // 2
    cols = [slice(p * 2 * DH, (p + 1) * 2 * DH) for p in range(pairs)]
    if first:
        shape = (size * len(kbs), 2 * size)
        key = lax.broadcasted_iota(jnp.int32, shape, 0)
        query = lax.broadcasted_iota(jnp.int32, shape, 1) % size
        other = key != query
    else:
        tops = m_ref[qb]
        totals = l_ref[qb]
    scores = []
    for p in range(pairs):
        q = q_ref[qrows, cols[p]] * jnp.asarray(DH ** (-0.5), BF16)
        zero = jnp.zeros_like(q)
        pair = jnp.concatenate([jnp.where(lane < DH, q, zero), jnp.where(lane < DH, zero, q)], axis=0)
        k = jnp.concatenate([k_ref[r, cols[p]] for r in krows], axis=0)
        s = dot_nt(k, pair)
        scores.append(jnp.where(other, s, -1e30) if first else s)
    raised = []
    new_tops = []
    new_totals = []
    for p in range(pairs):
        top = jnp.max(scores[p], axis=0, keepdims=True)
        if not first:
            top = jnp.maximum(top, tops[p : p + 1])
        e = jnp.exp(scores[p] - top)
        new_tops.append(top)
        new_totals.append(jnp.sum(e, axis=0, keepdims=True))
        raised.append(e.astype(BF16))
    for p in range(pairs):
        v = jnp.concatenate([vt_ref[cols[p], r] for r in krows], axis=1)
        o = dot_nn(v, raised[p])
        o = jnp.concatenate([o[:DH, :size], o[DH:, size:]], axis=0)
        if not first:
            fade = jnp.exp(tops[p : p + 1] - new_tops[p])
            new_totals[p] = new_totals[p] + totals[p : p + 1] * fade
            o = o + acc_ref[qb, cols[p], :] * by_head(fade, size)
        acc_ref[qb, cols[p], :] = o
    m_ref[qb] = jnp.concatenate(new_tops, axis=0)
    l_ref[qb] = jnp.concatenate(new_totals, axis=0)


def by_head(row, size):
    return jnp.concatenate(
        [jnp.broadcast_to(row[:, :size], (DH, size)), jnp.broadcast_to(row[:, size:], (DH, size))], axis=0
    )


def attend_listed(own, size, blocks, list_ref, count_ref, found_ref, *rest):
    def query(qb, carry):
        found_ref[0] = qb
        n = jnp.int32(1 if own else 0)
        for kb, block in enumerate(blocks):
            wanted = listed(list_ref, count_ref, qb, block)
            if own:
                wanted = jnp.logical_and(wanted, qb != kb)

            @pl.when(wanted)
            def _(n=n, kb=kb):
                found_ref[n] = kb

            n = n + wanted.astype(jnp.int32)
        start = 0
        if own:

            @pl.when(n == 1)
            def _():
                attend(True, size, qb, [qb], *rest)

            @pl.when(n > 1)
            def _():
                attend(True, size, qb, [qb, found_ref[1]], *rest)

            start = 2
        if len(blocks) - start > 1:

            def two(i, carry):
                attend(False, size, qb, [found_ref[start + 2 * i], found_ref[start + 2 * i + 1]], *rest)
                return carry

            lax.fori_loop(0, jnp.maximum(n - start, 0) // 2, two, 0)

        @pl.when(jnp.logical_and(n > start, n % 2 == 1))
        def _():
            attend(False, size, qb, [found_ref[n - 1]], *rest)

        return carry

    lax.fori_loop(0, list_ref.shape[0], query, 0)


def local_kernel(
    size, list_ref, count_ref, pos_ref, k_ref, vt_ref, f_ref, m_ref, l_ref, acc_ref, n_ref, found_ref
):
    queries = list_ref.shape[0]
    blocks = [pos_ref[0] * queries + kb for kb in range(queries)]
    attend_listed(
        True, size, blocks, list_ref, count_ref, found_ref, k_ref, k_ref, vt_ref, m_ref, l_ref, acc_ref
    )
    add_within(f_ref, vt_ref, n_ref)


def attend_halo(size, pieces, list_ref, count_ref, pos_ref, piece_refs, wk_ref, wvt_ref, q_ref, state, scratch):
    found_ref, x_ref, k_ref, vt_ref = scratch
    queries = list_ref.shape[0]
    pos = pos_ref[0]
    step = 1 - 2 * (pos % 2)
    row = 0
    blocks = []
    for (near, first), ref in zip(pieces, piece_refs):
        rows = ref.shape[0]
        x_ref[row : row + rows, :] = ref[...]
        row += rows
        run = pos + step if near else pos - step
        blocks += [run * queries + first + i for i in range(rows // size)]
    project(x_ref[...], wk_ref, wvt_ref, k_ref, vt_ref)
    attend_listed(
        False, size, blocks, list_ref, count_ref, found_ref, q_ref, k_ref, vt_ref, *state
    )


def halo_kernel(size, pieces, list_ref, count_ref, pos_ref, *refs):
    n = len(pieces)
    wk_ref, wvt_ref, q_ref = refs[n : n + 3]
    attend_halo(
        size, pieces, list_ref, count_ref, pos_ref, refs[:n], wk_ref, wvt_ref, q_ref, refs[n + 6 : n + 9], refs[n + 9 :]
    )


def final_kernel(size, pieces, list_ref, count_ref, pos_ref, *refs):
    n = len(pieces)
    wk_ref, wvt_ref, q_ref, lin_ref, wo_ref = refs[n : n + 5]
    out_ref, m_ref, l_ref, acc_ref, comb_ref = refs[n + 8 : n + 13]
    attend_halo(
        size,
        pieces,
        list_ref,
        count_ref,
        pos_ref,
        refs[:n],
        wk_ref,
        wvt_ref,
        q_ref,
        (m_ref, l_ref, acc_ref),
        refs[n + 13 :],
    )

    def finish(qb, carry):
        rows = tile(qb, size)
        share = 1.0 / l_ref[qb]
        for p in range(H // 2):
            cols = slice(p * 2 * DH, (p + 1) * 2 * DH)
            both = acc_ref[qb, cols, :] * by_head(share[p : p + 1], size) + lin_ref[cols, rows]
            comb_ref[rows, cols] = both.T.astype(BF16)
        return carry

    lax.fori_loop(0, list_ref.shape[0], finish, 0)
    out_ref[...] = dot_nn(comb_ref[...], wo_ref[...]).astype(BF16)


COSTLY = ()


def call(
    kernel,
    name,
    ins,
    outs,
    smem=0,
    scratch=(),
    aliases=None,
    limit=20 * MIB,
    space=pltpu.VMEM,
    out_space=pltpu.VMEM,
):
    return pl.pallas_call(
        kernel,
        name=name,
        in_specs=[SMEM] * smem + [pl.BlockSpec(memory_space=space)] * (len(ins) - smem),
        out_specs=[
            pl.BlockSpec(memory_space=m)
            for m in (out_space if isinstance(out_space, list) else [out_space] * len(outs))
        ],
        out_shape=[jax.ShapeDtypeStruct(s, d) for s, d in outs],
        scratch_shapes=list(scratch),
        input_output_aliases=aliases or {},
        cost_estimate=pl.CostEstimate(
            flops=10**11 if name in COSTLY else 1, bytes_accessed=1000, transcendentals=0
        ),
        compiler_params=pltpu.CompilerParams(vmem_limit_bytes=limit),
    )(*ins)


def after(value, *done):
    return lax.optimization_barrier((value,) + done)[0]


def on_device(tokens, qk_weight, value_weight, out_weight, neighbour_list, neighbour_count):
    rows = tokens.shape[1]
    width = tokens.shape[2]
    blocks = neighbour_list.shape[1]
    size = rows // blocks
    half = blocks // 2
    count = lax.axis_size("seq")
    position = lax.axis_index("seq").astype(jnp.int32).reshape(1)
    own = tokens[0]
    tables = (neighbour_list[0], neighbour_count[0], position)

    def swap(value, bit):
        return lax.ppermute(value, "seq", [(i, i ^ bit) for i in range(count)])

    def onward(value):
        pairs = [(i, i + 2) for i in range(0, count - 2, 2)] + [(i, i - 2) for i in range(3, count, 2)]
        return lax.ppermute(value, "seq", pairs)

    def across(value):
        odd = range(1, count - 1, 2)
        return lax.ppermute(value, "seq", [(i, i + 1) for i in odd] + [(i + 1, i) for i in odd])

    def flat(total):
        return (
            pltpu.SMEM((total // size + 2,), jnp.int32),
            pltpu.VMEM((total, width), BF16),
            pltpu.VMEM((total, width), BF16),
            pltpu.VMEM((width, total), BF16),
        )

    def join_halo(name, softmax, pieces, arrays):
        ins = tables + tuple(arrays) + (qk_weight, value_t, keyed) + tuple(softmax)
        first = len(ins) - 3
        return call(
            functools.partial(halo_kernel, size, pieces),
            name,
            ins,
            shapes,
            smem=3,
            scratch=flat(sum(a.shape[0] for a in arrays)),
            aliases={first + i: i for i in range(3)},
        )

    cut = half * size
    own = pltpu.with_memory_space_constraint(own, pltpu.HBM)
    (first_rows,) = call(
        cut_kernel,
        "cut",
        (own,),
        [((cut, width), BF16)],
        scratch=(pltpu.SemaphoreType.DMA(()),),
        space=pltpu.HBM,
    )
    near_a = swap(first_rows, 1)
    steps = width // 256
    keyed, features, values_t, value_t, last_rows, state = call(
        own_kernel,
        "own",
        (own,) + tuple(pltpu.with_memory_space_constraint(w, pltpu.HBM) for w in (qk_weight, value_weight)),
        [
            ((rows, width), BF16),
            ((rows, width), BF16),
            ((width, rows), BF16),
            ((width, width), BF16),
            ((rows - cut, width), BF16),
            ((width, DL), BF16),
        ],
        scratch=(
            pltpu.VMEM((rows, width), BF16),
            pltpu.VMEM((width, width), BF16),
            pltpu.VMEM((width, width), BF16),
            pltpu.VMEM((rows, width), BF16),
            pltpu.VMEM((rows, width), BF16),
            pltpu.VMEM((width, rows), BF16),
            pltpu.VMEM((width, width), BF16),
            pltpu.SemaphoreType.DMA((1 + 2 * steps,)),
            pltpu.SemaphoreType.DMA((1 + 4 * steps,)),
        ),
        limit=56 * MIB,
        space=pltpu.HBM,
        out_space=[pltpu.HBM] * 5 + [pltpu.VMEM],
    )
    heard = [swap(state, 1)]
    near_b = swap(last_rows, 1)
    far_b = across(last_rows)
    shapes = [((blocks, H // 2, 2 * size), F32)] * 2 + [((blocks, width, size), F32)]
    *softmax, within = call(
        functools.partial(local_kernel, size),
        "local",
        tables + tuple(pltpu.with_memory_space_constraint(a, pltpu.HBM) for a in (keyed, values_t, features)),
        shapes + [((width, rows), F32)],
        smem=3,
        scratch=(pltpu.SMEM((blocks + 1,), jnp.int32),),
    )
    far_a = onward(after(near_a, within))
    total = state + after(heard[0], within)
    heard.append(swap(total, 2))
    softmax = join_halo("halo_a", softmax, [(True, 0)], [after(near_a, within, total)])
    stride = 4
    while stride < count:
        total = total + after(heard[-1], softmax[0])
        heard.append(swap(total, stride))
        stride *= 2
    softmax = join_halo(
        "halo_b", softmax, [(False, 0), (True, half)], [after(far_a, total), near_b]
    )
    (linear,) = call(
        functools.partial(linear_kernel, len(heard)),
        "linear",
        (position, after(features, softmax[0]), within) + tuple(heard),
        [((width, rows), F32)],
        smem=1,
    )
    pieces = [(False, half)]
    arrays = (after(far_b, linear),)
    ins = tables + arrays + (qk_weight, value_t, keyed, linear, out_weight) + tuple(softmax)
    first = len(ins) - 3
    update, *_ = call(
        functools.partial(final_kernel, size, pieces),
        "final",
        ins,
        [((rows, width), BF16)] + shapes,
        smem=3,
        scratch=(pltpu.VMEM((rows, width), BF16),) + flat(sum(a.shape[0] for a in arrays)),
        aliases={first + i: i + 1 for i in range(3)},
    )
    return update[None]


def solution(mesh):
    placed = (
        P(("groups", "dp"), "seq", None),
        P(),
        P(),
        P(),
        P(("groups", "dp"), "seq", None),
        P(("groups", "dp"), "seq"),
    )
    return jax.shard_map(
        on_device,
        mesh=mesh,
        in_specs=placed,
        out_specs=P(("groups", "dp"), "seq", None),
        check_vma=False,
    )
```

```python
import functools

import jax
import jax.numpy as jnp
from jax import lax
from jax.experimental import pallas as pl
from jax.experimental.pallas import tpu as pltpu
from jax.sharding import PartitionSpec as P

H = 16
DH = 64
HL = 8
DL = 128
F32 = jnp.float32
BF16 = jnp.bfloat16
NT = (((1,), (1,)), ((), ()))
SMEM = pl.BlockSpec(memory_space=pltpu.SMEM)
MIB = 1 << 20


def dot_nt(a, b):
    return lax.dot_general(a, b, NT, preferred_element_type=F32)


def dot_nn(a, b):
    return jnp.dot(a, b, preferred_element_type=F32)


def tile(i, size):
    return pl.ds(pl.multiple_of(i * size, size), size)


def project(x, wk_ref, wvt_ref, k_ref, vt_ref):
    k_ref[...] = dot_nn(x, wk_ref[...]).astype(BF16)
    vt_ref[...] = dot_nt(wvt_ref[...], x).astype(BF16)


def cut_kernel(x_hbm, a_ref, sem):
    copy = pltpu.make_async_copy(x_hbm.at[: a_ref.shape[0]], a_ref, sem)
    copy.start()
    copy.wait()


def own_kernel(
    x_hbm, wk_hbm, wv_hbm, k_hbm, f_hbm, vt_hbm, wvt_hbm, a_hbm, b_hbm, s_ref, x_ref, wk_ref, wv_ref, k_ref, f_ref, vt_ref,
    wvt_ref, in_sems, out_sems
):
    width = x_ref.shape[1]
    step = 256
    tiles = [slice(i, i + step) for i in range(0, width, step)]
    n = len(tiles)
    ins = [pltpu.make_async_copy(x_hbm, x_ref, in_sems.at[0])]
    for i, (src, dst) in enumerate(((wk_hbm, wk_ref), (wv_hbm, wv_ref))):
        for j, part in enumerate(tiles):
            ins.append(pltpu.make_async_copy(src.at[:, part], dst.at[:, part], in_sems.at[1 + i * n + j]))
    for copy in ins[:2]:
        copy.start()
    outs = []

    def put(src, dst):
        copy = pltpu.make_async_copy(src, dst, out_sems.at[len(outs)])
        copy.start()
        outs.append(copy)

    ins[0].wait()
    last = x_ref.shape[0] - b_hbm.shape[0]
    put(x_ref.at[last - a_hbm.shape[0] : last], a_hbm)
    put(x_ref.at[last:], b_hbm)
    for j, part in enumerate(tiles):
        ins[2 + j].start()
        ins[1 + j].wait()
        k = dot_nn(x_ref[...], wk_ref[:, part]).astype(BF16)
        k_ref[:, part] = k
        put(k_ref.at[:, part], k_hbm.at[:, part])
        k = k.astype(F32)
        f_ref[:, part] = (k / (1.0 + jnp.exp(-k))).astype(BF16)
        put(f_ref.at[:, part], f_hbm.at[:, part])
    for j, part in enumerate(tiles):
        if j + 1 < n:
            ins[2 + n + j].start()
        ins[1 + n + j].wait()
        turned = wv_ref[:, part].T
        wvt_ref[part, :] = turned
        put(wvt_ref.at[part], wvt_hbm.at[part])
        vt_ref[part, :] = dot_nt(turned, x_ref[...]).astype(BF16)
        put(vt_ref.at[part], vt_hbm.at[part])
        for h in range(part.start, part.stop, DL):
            head = slice(h, h + DL)
            s_ref[head, :] = dot_nn(vt_ref[head, :], f_ref[:, head]).astype(BF16)
    for copy in outs:
        copy.wait()


def within_kernel(f_ref, vt_ref, n_ref):
    rows = f_ref.shape[0]
    half = rows // 2
    upper = lax.broadcasted_iota(jnp.int32, (half, half), 0) <= lax.broadcasted_iota(
        jnp.int32, (half, half), 1
    )

    def head(h, carry):
        cols = tile(h, DL)
        f0 = f_ref[:half, cols]
        f1 = f_ref[half:, cols]
        v0 = vt_ref[cols, :half]
        v1 = vt_ref[cols, half:]
        a00 = jnp.where(upper, dot_nt(f0, f0), 0.0).astype(BF16)
        a01 = dot_nt(f0, f1).astype(BF16)
        a11 = jnp.where(upper, dot_nt(f1, f1), 0.0).astype(BF16)
        n_ref[cols, :half] = dot_nn(v0, a00)
        n_ref[cols, half:] = dot_nn(v0, a01) + dot_nn(v1, a11)
        return carry

    lax.fori_loop(0, HL, head, 0, unroll=2)


def linear_kernel(stages, pos_ref, f_ref, n_ref, *refs):
    heard = refs[:stages]
    o_ref = refs[stages]
    bits = [((pos_ref[0] >> k) & 1).astype(F32) for k in range(stages)]

    def head(h, carry):
        cols = tile(h, DL)
        before = sum(ref[cols, :].astype(F32) * bit for ref, bit in zip(heard, bits)).astype(BF16)
        n = n_ref[cols, :] + dot_nt(before, f_ref[:, cols])
        mean = jnp.sum(n * n, axis=0, keepdims=True) * (1.0 / DL)
        o_ref[cols, :] = n * lax.rsqrt(mean + 1e-06)
        return carry

    lax.fori_loop(0, HL, head, 0, unroll=2)


def listed(list_ref, count_ref, qb, block):
    found = False
    for j in range(list_ref.shape[1]):
        found = jnp.logical_or(
            found, jnp.logical_and(j < count_ref[qb], list_ref[qb, j] == block)
        )
    return found


def attend(first, size, qb, kbs, q_ref, k_ref, vt_ref, m_ref, l_ref, acc_ref):
    qrows = tile(qb, size)
    krows = [tile(kb, size) for kb in kbs]
    lane = lax.broadcasted_iota(jnp.int32, (size, 2 * DH), 1)
    pairs = H // 2
    cols = [slice(p * 2 * DH, (p + 1) * 2 * DH) for p in range(pairs)]
    if first:
        shape = (size * len(kbs), 2 * size)
        key = lax.broadcasted_iota(jnp.int32, shape, 0)
        query = lax.broadcasted_iota(jnp.int32, shape, 1) % size
        other = key != query
    else:
        tops = m_ref[qb]
        totals = l_ref[qb]
    scores = []
    for p in range(pairs):
        q = q_ref[qrows, cols[p]] * jnp.asarray(DH ** (-0.5), BF16)
        zero = jnp.zeros_like(q)
        pair = jnp.concatenate([jnp.where(lane < DH, q, zero), jnp.where(lane < DH, zero, q)], axis=0)
        k = jnp.concatenate([k_ref[r, cols[p]] for r in krows], axis=0)
        s = dot_nt(k, pair)
        scores.append(jnp.where(other, s, -1e30) if first else s)
    raised = []
    new_tops = []
    new_totals = []
    for p in range(pairs):
        top = jnp.max(scores[p], axis=0, keepdims=True)
        if not first:
            top = jnp.maximum(top, tops[p : p + 1])
        e = jnp.exp(scores[p] - top)
        new_tops.append(top)
        new_totals.append(jnp.sum(e, axis=0, keepdims=True))
        raised.append(e.astype(BF16))
    for p in range(pairs):
        v = jnp.concatenate([vt_ref[cols[p], r] for r in krows], axis=1)
        o = dot_nn(v, raised[p])
        o = jnp.concatenate([o[:DH, :size], o[DH:, size:]], axis=0)
        if not first:
            fade = jnp.exp(tops[p : p + 1] - new_tops[p])
            new_totals[p] = new_totals[p] + totals[p : p + 1] * fade
            o = o + acc_ref[qb, cols[p], :] * by_head(fade, size)
        acc_ref[qb, cols[p], :] = o
    m_ref[qb] = jnp.concatenate(new_tops, axis=0)
    l_ref[qb] = jnp.concatenate(new_totals, axis=0)


def by_head(row, size):
    return jnp.concatenate(
        [jnp.broadcast_to(row[:, :size], (DH, size)), jnp.broadcast_to(row[:, size:], (DH, size))], axis=0
    )


def attend_listed(own, size, blocks, list_ref, count_ref, found_ref, *rest):
    def query(qb, carry):
        found_ref[0] = qb
        n = jnp.int32(1 if own else 0)
        for kb, block in enumerate(blocks):
            wanted = listed(list_ref, count_ref, qb, block)
            if own:
                wanted = jnp.logical_and(wanted, qb != kb)

            @pl.when(wanted)
            def _(n=n, kb=kb):
                found_ref[n] = kb

            n = n + wanted.astype(jnp.int32)
        start = 0
        if own:

            @pl.when(n == 1)
            def _():
                attend(True, size, qb, [qb], *rest)

            @pl.when(n > 1)
            def _():
                attend(True, size, qb, [qb, found_ref[1]], *rest)

            start = 2
        if len(blocks) - start > 1:

            def two(i, carry):
                attend(False, size, qb, [found_ref[start + 2 * i], found_ref[start + 2 * i + 1]], *rest)
                return carry

            lax.fori_loop(0, jnp.maximum(n - start, 0) // 2, two, 0)

        @pl.when(jnp.logical_and(n > start, n % 2 == 1))
        def _():
            attend(False, size, qb, [found_ref[n - 1]], *rest)

        return carry

    lax.fori_loop(0, list_ref.shape[0], query, 0)


def own_attention_kernel(size, list_ref, count_ref, pos_ref, k_ref, vt_ref, m_ref, l_ref, acc_ref, found_ref):
    queries = list_ref.shape[0]
    blocks = [pos_ref[0] * queries + kb for kb in range(queries)]
    attend_listed(
        True, size, blocks, list_ref, count_ref, found_ref, k_ref, k_ref, vt_ref, m_ref, l_ref, acc_ref
    )


def attend_halo(size, pieces, list_ref, count_ref, pos_ref, piece_refs, wk_ref, wvt_ref, q_ref, state, scratch):
    found_ref, x_ref, k_ref, vt_ref = scratch
    queries = list_ref.shape[0]
    pos = pos_ref[0]
    step = 1 - 2 * (pos % 2)
    row = 0
    blocks = []
    for (near, first), ref in zip(pieces, piece_refs):
        rows = ref.shape[0]
        x_ref[row : row + rows, :] = ref[...]
        row += rows
        run = pos + step if near else pos - step
        blocks += [run * queries + first + i for i in range(rows // size)]
    project(x_ref[...], wk_ref, wvt_ref, k_ref, vt_ref)
    attend_listed(
        False, size, blocks, list_ref, count_ref, found_ref, q_ref, k_ref, vt_ref, *state
    )


def halo_kernel(size, pieces, list_ref, count_ref, pos_ref, *refs):
    n = len(pieces)
    wk_ref, wvt_ref, q_ref = refs[n : n + 3]
    attend_halo(
        size, pieces, list_ref, count_ref, pos_ref, refs[:n], wk_ref, wvt_ref, q_ref, refs[n + 6 : n + 9], refs[n + 9 :]
    )


def final_kernel(size, pieces, list_ref, count_ref, pos_ref, *refs):
    n = len(pieces)
    wk_ref, wvt_ref, q_ref, lin_ref, wo_ref = refs[n : n + 5]
    out_ref, m_ref, l_ref, acc_ref, comb_ref = refs[n + 8 : n + 13]
    attend_halo(
        size,
        pieces,
        list_ref,
        count_ref,
        pos_ref,
        refs[:n],
        wk_ref,
        wvt_ref,
        q_ref,
        (m_ref, l_ref, acc_ref),
        refs[n + 13 :],
    )

    def finish(qb, carry):
        rows = tile(qb, size)
        share = 1.0 / l_ref[qb]
        for p in range(H // 2):
            cols = slice(p * 2 * DH, (p + 1) * 2 * DH)
            both = acc_ref[qb, cols, :] * by_head(share[p : p + 1], size) + lin_ref[cols, rows]
            comb_ref[rows, cols] = both.T.astype(BF16)
        return carry

    lax.fori_loop(0, list_ref.shape[0], finish, 0)
    out_ref[...] = dot_nn(comb_ref[...], wo_ref[...]).astype(BF16)


COSTLY = ("within",)


def call(
    kernel,
    name,
    ins,
    outs,
    smem=0,
    scratch=(),
    aliases=None,
    limit=20 * MIB,
    space=pltpu.VMEM,
    out_space=pltpu.VMEM,
):
    return pl.pallas_call(
        kernel,
        name=name,
        in_specs=[SMEM] * smem + [pl.BlockSpec(memory_space=space)] * (len(ins) - smem),
        out_specs=[
            pl.BlockSpec(memory_space=m)
            for m in (out_space if isinstance(out_space, list) else [out_space] * len(outs))
        ],
        out_shape=[jax.ShapeDtypeStruct(s, d) for s, d in outs],
        scratch_shapes=list(scratch),
        input_output_aliases=aliases or {},
        cost_estimate=pl.CostEstimate(
            flops=10**11 if name in COSTLY else 1, bytes_accessed=1000, transcendentals=0
        ),
        compiler_params=pltpu.CompilerParams(vmem_limit_bytes=limit),
    )(*ins)


def after(value, *done):
    return lax.optimization_barrier((value,) + done)[0]


def on_device(tokens, qk_weight, value_weight, out_weight, neighbour_list, neighbour_count):
    rows = tokens.shape[1]
    width = tokens.shape[2]
    blocks = neighbour_list.shape[1]
    size = rows // blocks
    half = blocks // 2
    count = lax.axis_size("seq")
    position = lax.axis_index("seq").astype(jnp.int32).reshape(1)
    own = tokens[0]
    tables = (neighbour_list[0], neighbour_count[0], position)

    def swap(value, bit):
        return lax.ppermute(value, "seq", [(i, i ^ bit) for i in range(count)])

    def onward(value):
        pairs = [(i, i + 2) for i in range(0, count - 2, 2)] + [(i, i - 2) for i in range(3, count, 2)]
        return lax.ppermute(value, "seq", pairs)

    def across(value):
        odd = range(1, count - 1, 2)
        return lax.ppermute(value, "seq", [(i, i + 1) for i in odd] + [(i + 1, i) for i in odd])

    def flat(total):
        return (
            pltpu.SMEM((total // size + 2,), jnp.int32),
            pltpu.VMEM((total, width), BF16),
            pltpu.VMEM((total, width), BF16),
            pltpu.VMEM((width, total), BF16),
        )

    def join_halo(name, softmax, pieces, arrays):
        ins = tables + tuple(arrays) + (qk_weight, value_t, keyed) + tuple(softmax)
        first = len(ins) - 3
        return call(
            functools.partial(halo_kernel, size, pieces),
            name,
            ins,
            shapes,
            smem=3,
            scratch=flat(sum(a.shape[0] for a in arrays)),
            aliases={first + i: i for i in range(3)},
        )

    own = pltpu.with_memory_space_constraint(own, pltpu.HBM)
    (first_rows,) = call(
        cut_kernel,
        "cut",
        (own,),
        [((size, width), BF16)],
        scratch=(pltpu.SemaphoreType.DMA(()),),
        space=pltpu.HBM,
    )
    near_a0 = swap(first_rows, 1)
    steps = width // 256
    keyed, features, values_t, value_t, next_rows, last_rows, state = call(
        own_kernel,
        "own",
        (pltpu.with_memory_space_constraint(after(tokens[0], first_rows), pltpu.HBM),) + tuple(pltpu.with_memory_space_constraint(w, pltpu.HBM) for w in (qk_weight, value_weight)),
        [
            ((rows, width), BF16),
            ((rows, width), BF16),
            ((width, rows), BF16),
            ((width, width), BF16),
            (((half - 1) * size, width), BF16),
            (((blocks - half) * size, width), BF16),
            ((width, DL), BF16),
        ],
        scratch=(
            pltpu.VMEM((rows, width), BF16),
            pltpu.VMEM((width, width), BF16),
            pltpu.VMEM((width, width), BF16),
            pltpu.VMEM((rows, width), BF16),
            pltpu.VMEM((rows, width), BF16),
            pltpu.VMEM((width, rows), BF16),
            pltpu.VMEM((width, width), BF16),
            pltpu.SemaphoreType.DMA((1 + 2 * steps,)),
            pltpu.SemaphoreType.DMA((2 + 4 * steps,)),
        ),
        limit=56 * MIB,
        space=pltpu.HBM,
        out_space=[pltpu.HBM] * 6 + [pltpu.VMEM],
    )
    heard = [swap(after(state, near_a0), 1)]
    near_a1 = swap(next_rows, 1)
    far_a0 = onward(after(near_a0, state))
    far_b = across(last_rows)
    near_b = swap(last_rows, 1)
    total = state + heard[0]
    heard.append(swap(total, 2))
    shapes = [((blocks, H // 2, 2 * size), F32)] * 2 + [((blocks, width, size), F32)]
    in_hbm = [pltpu.with_memory_space_constraint(a, pltpu.HBM) for a in (keyed, values_t, features)]
    softmax = call(
        functools.partial(own_attention_kernel, size),
        "own_attention",
        tables + (after(in_hbm[0], total), in_hbm[1]),
        shapes,
        smem=3,
        scratch=(pltpu.SMEM((blocks + 1,), jnp.int32),),
    )
    far_a1 = onward(after(near_a1, softmax[0]))
    (within,) = call(
        within_kernel,
        "within",
        (after(in_hbm[2], softmax[0], near_a1), in_hbm[1]),
        [((width, rows), F32)],
    )
    stride = 4
    while stride < count:
        total = total + after(heard[-1], within)
        heard.append(swap(total, stride))
        stride *= 2
    softmax = join_halo(
        "halo_a", softmax, [(True, 0), (True, 1)], [after(near_a0, within, total), near_a1]
    )
    softmax = join_halo(
        "halo_b",
        softmax,
        [(False, 0), (False, 1), (False, half)],
        [after(far_a0, softmax[0]), far_a1, far_b],
    )
    (linear,) = call(
        functools.partial(linear_kernel, len(heard)),
        "linear",
        (position, after(features, softmax[0]), within) + tuple(heard),
        [((width, rows), F32)],
        smem=1,
    )
    pieces = [(True, half)]
    arrays = (after(near_b, linear),)
    ins = tables + arrays + (qk_weight, value_t, keyed, linear, out_weight) + tuple(softmax)
    first = len(ins) - 3
    update, *_ = call(
        functools.partial(final_kernel, size, pieces),
        "final",
        ins,
        [((rows, width), BF16)] + shapes,
        smem=3,
        scratch=(pltpu.VMEM((rows, width), BF16),) + flat(sum(a.shape[0] for a in arrays)),
        aliases={first + i: i + 1 for i in range(3)},
    )
    return update[None]


def solution(mesh):
    placed = (
        P(("groups", "dp"), "seq", None),
        P(),
        P(),
        P(),
        P(("groups", "dp"), "seq", None),
        P(("groups", "dp"), "seq"),
    )
    return jax.shard_map(
        on_device,
        mesh=mesh,
        in_specs=placed,
        out_specs=P(("groups", "dp"), "seq", None),
        check_vma=False,
    )
```

```python
import functools

import jax
import jax.numpy as jnp
from jax import lax
from jax.experimental import pallas as pl
from jax.experimental.pallas import tpu as pltpu
from jax.sharding import PartitionSpec as P

H = 16
DH = 64
HL = 8
DL = 128
F32 = jnp.float32
BF16 = jnp.bfloat16
NT = (((1,), (1,)), ((), ()))
SMEM = pl.BlockSpec(memory_space=pltpu.SMEM)
MIB = 1 << 20


def dot_nt(a, b):
    return lax.dot_general(a, b, NT, preferred_element_type=F32)


def dot_nn(a, b):
    return jnp.dot(a, b, preferred_element_type=F32)


def tile(i, size):
    return pl.ds(pl.multiple_of(i * size, size), size)


def silu(k):
    k = k.astype(F32)
    return (k / (1.0 + jnp.exp(-k))).astype(BF16)


def project(x, wk_ref, wv_ref, k_ref, vt_ref):
    k_ref[...] = dot_nn(x, wk_ref[...]).astype(BF16)
    step = 256
    for i in range(0, wv_ref.shape[1], step):
        part = slice(i, i + step)
        vt_ref[part, :] = dot_nn(x, wv_ref[:, part]).astype(BF16).T


def cut_kernel(x_hbm, a_ref, sem):
    copy = pltpu.make_async_copy(x_hbm.at[: a_ref.shape[0]], a_ref, sem)
    copy.start()
    copy.wait()


def own_kernel(
    x_hbm, wk_hbm, wv_hbm, k_hbm, vt_hbm, b_hbm, s_ref, x_ref, wk_ref, wv_ref, k_ref, vt_ref, in_sems, out_sems
):
    width = x_ref.shape[1]
    step = 256
    tiles = [slice(i, i + step) for i in range(0, width, step)]
    n = len(tiles)
    ins = [pltpu.make_async_copy(x_hbm, x_ref, in_sems.at[0])]
    for j, part in enumerate(tiles):
        for i, (src, dst) in enumerate(((wk_hbm, wk_ref), (wv_hbm, wv_ref))):
            ins.append(pltpu.make_async_copy(src.at[:, part], dst.at[:, part], in_sems.at[1 + 2 * j + i]))
    for copy in ins[:3]:
        copy.start()
    outs = []

    def put(src, dst):
        copy = pltpu.make_async_copy(src, dst, out_sems.at[len(outs)])
        copy.start()
        outs.append(copy)

    ins[0].wait()
    put(x_ref.at[x_ref.shape[0] - b_hbm.shape[0] :], b_hbm)
    for j, part in enumerate(tiles):
        for copy in ins[3 + 2 * j : 5 + 2 * j]:
            copy.start()
        ins[1 + 2 * j].wait()
        k = dot_nn(x_ref[...], wk_ref[:, part]).astype(BF16)
        k_ref[:, part] = k
        put(k_ref.at[:, part], k_hbm.at[:, part])
        f = silu(k)
        ins[2 + 2 * j].wait()
        vt_ref[part, :] = dot_nn(x_ref[...], wv_ref[:, part]).astype(BF16).T
        put(vt_ref.at[part], vt_hbm.at[part])
        for h in range(0, step, DL):
            head = slice(part.start + h, part.start + h + DL)
            s_ref[head, :] = dot_nn(vt_ref[head, :], f[:, h : h + DL]).astype(BF16)
    for copy in outs:
        copy.wait()


def within_kernel(k_ref, vt_ref, n_ref):
    rows = k_ref.shape[0]
    half = rows // 2
    upper = lax.broadcasted_iota(jnp.int32, (half, half), 0) <= lax.broadcasted_iota(
        jnp.int32, (half, half), 1
    )

    def head(h, carry):
        cols = tile(h, DL)
        f0 = silu(k_ref[:half, cols])
        f1 = silu(k_ref[half:, cols])
        v0 = vt_ref[cols, :half]
        v1 = vt_ref[cols, half:]
        a00 = jnp.where(upper, dot_nt(f0, f0), 0.0).astype(BF16)
        a01 = dot_nt(f0, f1).astype(BF16)
        a11 = jnp.where(upper, dot_nt(f1, f1), 0.0).astype(BF16)
        n_ref[cols, :half] = dot_nn(v0, a00)
        n_ref[cols, half:] = dot_nn(v0, a01) + dot_nn(v1, a11)
        return carry

    lax.fori_loop(0, HL, head, 0, unroll=2)


def set_bits(pos_ref, count):
    return [((pos_ref[0] >> (k + 1)) & 1).astype(F32) for k in range(count)]


def carry_kernel(stages, pos_ref, s_ref, *refs):
    bits = set_bits(pos_ref, stages)
    first = 1.0 - (pos_ref[0] & 1).astype(F32)
    total = s_ref[...].astype(F32) * first
    for ref, bit in zip(refs, bits):
        total = total + ref[...].astype(F32) * bit
    refs[stages][...] = total.astype(BF16)


def linear_kernel(stages, pos_ref, k_ref, n_ref, *refs):
    heard, message_ref, o_ref = refs[:stages], refs[stages], refs[stages + 1]
    bits = set_bits(pos_ref, stages)

    def head(h, carry):
        cols = tile(h, DL)
        before = message_ref[cols, :].astype(F32)
        for ref, bit in zip(heard, bits):
            before = before + ref[cols, :].astype(F32) * bit
        n = n_ref[cols, :] + dot_nt(before.astype(BF16), silu(k_ref[:, cols]))
        mean = jnp.sum(n * n, axis=0, keepdims=True) * (1.0 / DL)
        o_ref[cols, :] = n * lax.rsqrt(mean + 1e-06)
        return carry

    lax.fori_loop(0, HL, head, 0, unroll=2)


def listed(list_ref, count_ref, qb, block):
    found = False
    for j in range(list_ref.shape[1]):
        found = jnp.logical_or(
            found, jnp.logical_and(j < count_ref[qb], list_ref[qb, j] == block)
        )
    return found


def attend(first, size, qb, kbs, q_ref, k_ref, vt_ref, m_ref, l_ref, acc_ref):
    qrows = tile(qb, size)
    krows = [tile(kb, size) for kb in kbs]
    lane = lax.broadcasted_iota(jnp.int32, (size, 2 * DH), 1)
    pairs = H // 2
    cols = [slice(p * 2 * DH, (p + 1) * 2 * DH) for p in range(pairs)]
    if first:
        shape = (size * len(kbs), 2 * size)
        key = lax.broadcasted_iota(jnp.int32, shape, 0)
        query = lax.broadcasted_iota(jnp.int32, shape, 1) % size
        other = key != query
    else:
        tops = m_ref[qb]
        totals = l_ref[qb]
    scores = []
    for p in range(pairs):
        q = q_ref[qrows, cols[p]] * jnp.asarray(DH ** (-0.5), BF16)
        zero = jnp.zeros_like(q)
        pair = jnp.concatenate([jnp.where(lane < DH, q, zero), jnp.where(lane < DH, zero, q)], axis=0)
        k = jnp.concatenate([k_ref[r, cols[p]] for r in krows], axis=0)
        s = dot_nt(k, pair)
        scores.append(jnp.where(other, s, -1e30) if first else s)
    raised = []
    new_tops = []
    new_totals = []
    for p in range(pairs):
        top = jnp.max(scores[p], axis=0, keepdims=True)
        if not first:
            top = jnp.maximum(top, tops[p : p + 1])
        e = jnp.exp(scores[p] - top)
        new_tops.append(top)
        new_totals.append(jnp.sum(e, axis=0, keepdims=True))
        raised.append(e.astype(BF16))
    for p in range(pairs):
        v = jnp.concatenate([vt_ref[cols[p], r] for r in krows], axis=1)
        o = dot_nn(v, raised[p])
        o = jnp.concatenate([o[:DH, :size], o[DH:, size:]], axis=0)
        if not first:
            fade = jnp.exp(tops[p : p + 1] - new_tops[p])
            new_totals[p] = new_totals[p] + totals[p : p + 1] * fade
            o = o + acc_ref[qb, cols[p], :] * by_head(fade, size)
        acc_ref[qb, cols[p], :] = o
    m_ref[qb] = jnp.concatenate(new_tops, axis=0)
    l_ref[qb] = jnp.concatenate(new_totals, axis=0)


def by_head(row, size):
    return jnp.concatenate(
        [jnp.broadcast_to(row[:, :size], (DH, size)), jnp.broadcast_to(row[:, size:], (DH, size))], axis=0
    )


def attend_listed(own, size, blocks, list_ref, count_ref, found_ref, *rest):
    def query(qb, carry):
        found_ref[0] = qb
        n = jnp.int32(1 if own else 0)
        for kb, block in enumerate(blocks):
            wanted = listed(list_ref, count_ref, qb, block)
            if own:
                wanted = jnp.logical_and(wanted, qb != kb)

            @pl.when(wanted)
            def _(n=n, kb=kb):
                found_ref[n] = kb

            n = n + wanted.astype(jnp.int32)
        start = 0
        if own:

            @pl.when(n == 1)
            def _():
                attend(True, size, qb, [qb], *rest)

            @pl.when(n > 1)
            def _():
                attend(True, size, qb, [qb, found_ref[1]], *rest)

            start = 2
        if len(blocks) - start > 1:

            def two(i, carry):
                attend(False, size, qb, [found_ref[start + 2 * i], found_ref[start + 2 * i + 1]], *rest)
                return carry

            lax.fori_loop(0, jnp.maximum(n - start, 0) // 2, two, 0)

        @pl.when(jnp.logical_and(n > start, n % 2 == 1))
        def _():
            attend(False, size, qb, [found_ref[n - 1]], *rest)

        return carry

    lax.fori_loop(0, list_ref.shape[0], query, 0)


def own_attention_kernel(size, list_ref, count_ref, pos_ref, k_ref, vt_ref, m_ref, l_ref, acc_ref, found_ref):
    queries = list_ref.shape[0]
    blocks = [pos_ref[0] * queries + kb for kb in range(queries)]
    attend_listed(
        True, size, blocks, list_ref, count_ref, found_ref, k_ref, k_ref, vt_ref, m_ref, l_ref, acc_ref
    )


def attend_halo(size, pieces, list_ref, count_ref, pos_ref, piece_refs, wk_ref, wv_ref, q_ref, state, scratch):
    found_ref, x_ref, k_ref, vt_ref = scratch
    queries = list_ref.shape[0]
    pos = pos_ref[0]
    step = 1 - 2 * (pos % 2)
    row = 0
    blocks = []
    for (near, first), ref in zip(pieces, piece_refs):
        rows = ref.shape[0]
        x_ref[row : row + rows, :] = ref[...]
        row += rows
        run = pos + step if near else pos - step
        blocks += [run * queries + first + i for i in range(rows // size)]
    project(x_ref[...], wk_ref, wv_ref, k_ref, vt_ref)
    attend_listed(
        False, size, blocks, list_ref, count_ref, found_ref, q_ref, k_ref, vt_ref, *state
    )


def halo_kernel(size, pieces, list_ref, count_ref, pos_ref, *refs):
    n = len(pieces)
    wk_ref, wv_ref, q_ref = refs[n : n + 3]
    attend_halo(
        size, pieces, list_ref, count_ref, pos_ref, refs[:n], wk_ref, wv_ref, q_ref, refs[n + 6 : n + 9], refs[n + 9 :]
    )


def final_kernel(size, pieces, list_ref, count_ref, pos_ref, *refs):
    n = len(pieces)
    wk_ref, wv_ref, q_ref, lin_ref, wo_ref = refs[n : n + 5]
    out_ref, m_ref, l_ref, acc_ref, comb_ref = refs[n + 8 : n + 13]
    attend_halo(
        size,
        pieces,
        list_ref,
        count_ref,
        pos_ref,
        refs[:n],
        wk_ref,
        wv_ref,
        q_ref,
        (m_ref, l_ref, acc_ref),
        refs[n + 13 :],
    )

    def finish(qb, carry):
        rows = tile(qb, size)
        share = 1.0 / l_ref[qb]
        for p in range(H // 2):
            cols = slice(p * 2 * DH, (p + 1) * 2 * DH)
            both = acc_ref[qb, cols, :] * by_head(share[p : p + 1], size) + lin_ref[cols, rows]
            comb_ref[rows, cols] = both.T.astype(BF16)
        return carry

    lax.fori_loop(0, list_ref.shape[0], finish, 0)
    out_ref[...] = dot_nn(comb_ref[...], wo_ref[...]).astype(BF16)


COSTLY = ("within",)


def call(
    kernel,
    name,
    ins,
    outs,
    smem=0,
    scratch=(),
    aliases=None,
    limit=20 * MIB,
    space=pltpu.VMEM,
    out_space=pltpu.VMEM,
):
    return pl.pallas_call(
        kernel,
        name=name,
        in_specs=[SMEM] * smem + [pl.BlockSpec(memory_space=space)] * (len(ins) - smem),
        out_specs=[
            pl.BlockSpec(memory_space=m)
            for m in (out_space if isinstance(out_space, list) else [out_space] * len(outs))
        ],
        out_shape=[jax.ShapeDtypeStruct(s, d) for s, d in outs],
        scratch_shapes=list(scratch),
        input_output_aliases=aliases or {},
        cost_estimate=pl.CostEstimate(
            flops=10**11 if name in COSTLY else 1, bytes_accessed=1000, transcendentals=0
        ),
        compiler_params=pltpu.CompilerParams(vmem_limit_bytes=limit),
    )(*ins)


def after(value, *done):
    return lax.optimization_barrier((value,) + done)[0]


def on_device(tokens, qk_weight, value_weight, out_weight, neighbour_list, neighbour_count):
    rows = tokens.shape[1]
    width = tokens.shape[2]
    blocks = neighbour_list.shape[1]
    size = rows // blocks
    half = blocks // 2
    count = lax.axis_size("seq")
    position = lax.axis_index("seq").astype(jnp.int32).reshape(1)
    own = tokens[0]
    tables = (neighbour_list[0], neighbour_count[0], position)

    def swap(value, bit):
        return lax.ppermute(value, "seq", [(i, i ^ bit) for i in range(count)])

    def onward(value):
        pairs = [(i, i + 2) for i in range(0, count - 2, 2)] + [(i, i - 2) for i in range(3, count, 2)]
        return lax.ppermute(value, "seq", pairs)

    def across(value):
        odd = range(1, count - 1, 2)
        return lax.ppermute(value, "seq", [(i, i + 1) for i in odd] + [(i + 1, i) for i in odd])

    def flat(total):
        return (
            pltpu.SMEM((total // size + 2,), jnp.int32),
            pltpu.VMEM((total, width), BF16),
            pltpu.VMEM((total, width), BF16),
            pltpu.VMEM((width, total), BF16),
        )

    def join_halo(name, softmax, pieces, arrays):
        ins = tables + tuple(arrays) + (qk_weight, value_weight, keyed) + tuple(softmax)
        first = len(ins) - 3
        return call(
            functools.partial(halo_kernel, size, pieces),
            name,
            ins,
            shapes,
            smem=3,
            scratch=flat(sum(a.shape[0] for a in arrays)),
            aliases={first + i: i for i in range(3)},
        )

    cut = half * size
    in_hbm = functools.partial(pltpu.with_memory_space_constraint, memory_space=pltpu.HBM)
    (first_rows,) = call(
        cut_kernel,
        "cut",
        (in_hbm(own),),
        [((cut, width), BF16)],
        scratch=(pltpu.SemaphoreType.DMA(()),),
        space=pltpu.HBM,
    )
    near_a = swap(first_rows, 1)
    steps = width // 256
    keyed, values_t, last_rows, state = call(
        own_kernel,
        "own",
        (in_hbm(after(own, first_rows)), in_hbm(qk_weight), in_hbm(value_weight)),
        [
            ((rows, width), BF16),
            ((width, rows), BF16),
            ((rows - cut, width), BF16),
            ((width, DL), BF16),
        ],
        scratch=(
            pltpu.VMEM((rows, width), BF16),
            pltpu.VMEM((width, width), BF16),
            pltpu.VMEM((width, width), BF16),
            pltpu.VMEM((rows, width), BF16),
            pltpu.VMEM((width, rows), BF16),
            pltpu.SemaphoreType.DMA((1 + 2 * steps,)),
            pltpu.SemaphoreType.DMA((1 + 2 * steps,)),
        ),
        limit=56 * MIB,
        space=pltpu.HBM,
        out_space=[pltpu.HBM] * 3 + [pltpu.VMEM],
    )
    far_b = across(last_rows)
    heard = [swap(state, 2)]
    shapes = [((blocks, H // 2, 2 * size), F32)] * 2 + [((blocks, width, size), F32)]
    softmax = call(
        functools.partial(own_attention_kernel, size),
        "own_attention",
        tables + (in_hbm(keyed), in_hbm(values_t)),
        shapes,
        smem=3,
        scratch=(pltpu.SMEM((blocks + 1,), jnp.int32),),
    )
    total = state
    stride = 4
    while stride < count:
        total = total + after(heard[-1], softmax[0])
        heard.append(swap(total, stride))
        stride *= 2
    far_a = onward(after(near_a, total))
    near_b = swap(after(last_rows, near_a), 1)
    (within,) = call(
        within_kernel,
        "within",
        (after(in_hbm(keyed), softmax[0], near_a), in_hbm(values_t)),
        [((width, rows), F32)],
    )
    softmax = join_halo("halo_a", softmax, [(True, 0)], [after(near_a, within)])
    (message,) = call(
        functools.partial(carry_kernel, len(heard)),
        "carry",
        (position, after(state, softmax[0])) + tuple(heard),
        [((width, DL), BF16)],
        smem=1,
    )
    message = swap(message, 1)
    softmax = join_halo("halo_b", softmax, [(False, half)], [after(far_b, heard[-1], softmax[0])])
    softmax = join_halo("halo_c", softmax, [(False, 0)], [after(far_a, softmax[0])])
    (linear,) = call(
        functools.partial(linear_kernel, len(heard)),
        "linear",
        (position, after(keyed, softmax[0]), within) + tuple(heard) + (message,),
        [((width, rows), F32)],
        smem=1,
    )
    pieces = [(True, half)]
    arrays = (after(near_b, linear),)
    ins = tables + arrays + (qk_weight, value_weight, keyed, linear, out_weight) + tuple(softmax)
    first = len(ins) - 3
    update, *_ = call(
        functools.partial(final_kernel, size, pieces),
        "final",
        ins,
        [((rows, width), BF16)] + shapes,
        smem=3,
        scratch=(pltpu.VMEM((rows, width), BF16),) + flat(sum(a.shape[0] for a in arrays)),
        aliases={first + i: i + 1 for i in range(3)},
    )
    return update[None]


def solution(mesh):
    placed = (
        P(("groups", "dp"), "seq", None),
        P(),
        P(),
        P(),
        P(("groups", "dp"), "seq", None),
        P(("groups", "dp"), "seq"),
    )
    return jax.shard_map(
        on_device,
        mesh=mesh,
        in_specs=placed,
        out_specs=P(("groups", "dp"), "seq", None),
        check_vma=False,
    )
```

```python
import functools

import jax
import jax.numpy as jnp
from jax import lax
from jax.experimental import pallas as pl
from jax.experimental.pallas import tpu as pltpu
from jax.sharding import PartitionSpec as P

H = 16
DH = 64
HL = 8
DL = 128
F32 = jnp.float32
BF16 = jnp.bfloat16
NT = (((1,), (1,)), ((), ()))
SMEM = pl.BlockSpec(memory_space=pltpu.SMEM)
MIB = 1 << 20


def dot_nt(a, b):
    return lax.dot_general(a, b, NT, preferred_element_type=F32)


def dot_nn(a, b):
    return jnp.dot(a, b, preferred_element_type=F32)


def tile(i, size):
    return pl.ds(pl.multiple_of(i * size, size), size)


def silu(k):
    k = k.astype(F32)
    return (k / (1.0 + jnp.exp(-k))).astype(BF16)


def project(x, wk_ref, wv_ref, k_ref, vt_ref):
    k_ref[...] = dot_nn(x, wk_ref[...]).astype(BF16)
    step = 256
    for i in range(0, wv_ref.shape[1], step):
        part = slice(i, i + step)
        vt_ref[part, :] = dot_nn(x, wv_ref[:, part]).astype(BF16).T


def cut_kernel(x_hbm, a_ref, sem):
    copy = pltpu.make_async_copy(x_hbm.at[: a_ref.shape[0]], a_ref, sem)
    copy.start()
    copy.wait()


def own_kernel(
    x_hbm, wk_hbm, wv_hbm, k_hbm, vt_hbm, b_hbm, s_ref, x_ref, wk_ref, wv_ref, k_ref, vt_ref, in_sems, out_sems
):
    ins = [
        pltpu.make_async_copy(src, dst, in_sems.at[i])
        for i, (src, dst) in enumerate(((x_hbm, x_ref), (wk_hbm, wk_ref), (wv_hbm, wv_ref)))
    ]
    outs = [
        pltpu.make_async_copy(src, dst, out_sems.at[i])
        for i, (src, dst) in enumerate(
            ((x_ref.at[x_ref.shape[0] - b_hbm.shape[0] :], b_hbm), (k_ref, k_hbm), (vt_ref, vt_hbm))
        )
    ]
    for copy in ins:
        copy.start()
    ins[0].wait()
    outs[0].start()
    ins[1].wait()
    k_ref[...] = dot_nn(x_ref[...], wk_ref[...]).astype(BF16)
    outs[1].start()
    ins[2].wait()
    step = 256
    for i in range(0, wv_ref.shape[1], step):
        part = slice(i, i + step)
        vt_ref[part, :] = dot_nt(wv_ref[:, part].T, x_ref[...]).astype(BF16)
    for h in range(HL):
        part = slice(h * DL, (h + 1) * DL)
        s_ref[part, :] = dot_nn(vt_ref[part, :], silu(k_ref[:, part])).astype(BF16)
    outs[2].start()
    for copy in outs:
        copy.wait()


def within_kernel(k_ref, vt_ref, n_ref):
    rows = k_ref.shape[0]
    half = rows // 2
    upper = lax.broadcasted_iota(jnp.int32, (half, half), 0) <= lax.broadcasted_iota(
        jnp.int32, (half, half), 1
    )

    def head(h, carry):
        cols = tile(h, DL)
        f0 = silu(k_ref[:half, cols])
        f1 = silu(k_ref[half:, cols])
        v0 = vt_ref[cols, :half]
        v1 = vt_ref[cols, half:]
        a00 = jnp.where(upper, dot_nt(f0, f0), 0.0).astype(BF16)
        a01 = dot_nt(f0, f1).astype(BF16)
        a11 = jnp.where(upper, dot_nt(f1, f1), 0.0).astype(BF16)
        n_ref[cols, :half] = dot_nn(v0, a00)
        n_ref[cols, half:] = dot_nn(v0, a01) + dot_nn(v1, a11)
        return carry

    lax.fori_loop(0, HL, head, 0, unroll=2)


def set_bits(pos_ref, count):
    return [((pos_ref[0] >> (k + 1)) & 1).astype(F32) for k in range(count)]


def carry_kernel(stages, pos_ref, s_ref, *refs):
    bits = set_bits(pos_ref, stages)
    first = 1.0 - (pos_ref[0] & 1).astype(F32)
    total = s_ref[...].astype(F32) * first
    for ref, bit in zip(refs, bits):
        total = total + ref[...].astype(F32) * bit
    refs[stages][...] = total.astype(BF16)


def linear_kernel(stages, pos_ref, k_ref, n_ref, *refs):
    heard, message_ref, o_ref = refs[:stages], refs[stages], refs[stages + 1]
    bits = set_bits(pos_ref, stages)

    def head(h, carry):
        cols = tile(h, DL)
        before = message_ref[cols, :].astype(F32)
        for ref, bit in zip(heard, bits):
            before = before + ref[cols, :].astype(F32) * bit
        n = n_ref[cols, :] + dot_nt(before.astype(BF16), silu(k_ref[:, cols]))
        mean = jnp.sum(n * n, axis=0, keepdims=True) * (1.0 / DL)
        o_ref[cols, :] = n * lax.rsqrt(mean + 1e-06)
        return carry

    lax.fori_loop(0, HL, head, 0, unroll=2)


def listed(list_ref, count_ref, qb, block):
    found = False
    for j in range(list_ref.shape[1]):
        found = jnp.logical_or(
            found, jnp.logical_and(j < count_ref[qb], list_ref[qb, j] == block)
        )
    return found


def attend(first, size, qb, kbs, q_ref, k_ref, vt_ref, m_ref, l_ref, acc_ref):
    qrows = tile(qb, size)
    krows = [tile(kb, size) for kb in kbs]
    lane = lax.broadcasted_iota(jnp.int32, (size, 2 * DH), 1)
    pairs = H // 2
    cols = [slice(p * 2 * DH, (p + 1) * 2 * DH) for p in range(pairs)]
    if first:
        shape = (size * len(kbs), 2 * size)
        key = lax.broadcasted_iota(jnp.int32, shape, 0)
        query = lax.broadcasted_iota(jnp.int32, shape, 1) % size
        other = key != query
    else:
        tops = m_ref[qb]
        totals = l_ref[qb]
    scores = []
    for p in range(pairs):
        q = q_ref[qrows, cols[p]] * jnp.asarray(DH ** (-0.5), BF16)
        zero = jnp.zeros_like(q)
        pair = jnp.concatenate([jnp.where(lane < DH, q, zero), jnp.where(lane < DH, zero, q)], axis=0)
        k = jnp.concatenate([k_ref[r, cols[p]] for r in krows], axis=0)
        s = dot_nt(k, pair)
        scores.append(jnp.where(other, s, -1e30) if first else s)
    raised = []
    new_tops = []
    new_totals = []
    for p in range(pairs):
        top = jnp.max(scores[p], axis=0, keepdims=True)
        if not first:
            top = jnp.maximum(top, tops[p : p + 1])
        e = jnp.exp(scores[p] - top)
        new_tops.append(top)
        new_totals.append(jnp.sum(e, axis=0, keepdims=True))
        raised.append(e.astype(BF16))
    for p in range(pairs):
        v = jnp.concatenate([vt_ref[cols[p], r] for r in krows], axis=1)
        o = dot_nn(v, raised[p])
        o = jnp.concatenate([o[:DH, :size], o[DH:, size:]], axis=0)
        if not first:
            fade = jnp.exp(tops[p : p + 1] - new_tops[p])
            new_totals[p] = new_totals[p] + totals[p : p + 1] * fade
            o = o + acc_ref[qb, cols[p], :] * by_head(fade, size)
        acc_ref[qb, cols[p], :] = o
    m_ref[qb] = jnp.concatenate(new_tops, axis=0)
    l_ref[qb] = jnp.concatenate(new_totals, axis=0)


def by_head(row, size):
    return jnp.concatenate(
        [jnp.broadcast_to(row[:, :size], (DH, size)), jnp.broadcast_to(row[:, size:], (DH, size))], axis=0
    )


def attend_listed(own, size, blocks, list_ref, count_ref, found_ref, *rest):
    def query(qb, carry):
        found_ref[0] = qb
        n = jnp.int32(1 if own else 0)
        for kb, block in enumerate(blocks):
            wanted = listed(list_ref, count_ref, qb, block)
            if own:
                wanted = jnp.logical_and(wanted, qb != kb)

            @pl.when(wanted)
            def _(n=n, kb=kb):
                found_ref[n] = kb

            n = n + wanted.astype(jnp.int32)
        start = 0
        if own:

            @pl.when(n == 1)
            def _():
                attend(True, size, qb, [qb], *rest)

            @pl.when(n > 1)
            def _():
                attend(True, size, qb, [qb, found_ref[1]], *rest)

            start = 2
        if len(blocks) - start > 1:

            def two(i, carry):
                attend(False, size, qb, [found_ref[start + 2 * i], found_ref[start + 2 * i + 1]], *rest)
                return carry

            lax.fori_loop(0, jnp.maximum(n - start, 0) // 2, two, 0)

        @pl.when(jnp.logical_and(n > start, n % 2 == 1))
        def _():
            attend(False, size, qb, [found_ref[n - 1]], *rest)

        return carry

    lax.fori_loop(0, list_ref.shape[0], query, 0)


def own_attention_kernel(size, list_ref, count_ref, pos_ref, k_ref, vt_ref, m_ref, l_ref, acc_ref, found_ref):
    queries = list_ref.shape[0]
    blocks = [pos_ref[0] * queries + kb for kb in range(queries)]
    attend_listed(
        True, size, blocks, list_ref, count_ref, found_ref, k_ref, k_ref, vt_ref, m_ref, l_ref, acc_ref
    )


def attend_halo(size, pieces, list_ref, count_ref, pos_ref, piece_refs, wk_ref, wv_ref, q_ref, state, scratch):
    found_ref, x_ref, k_ref, vt_ref = scratch
    queries = list_ref.shape[0]
    pos = pos_ref[0]
    step = 1 - 2 * (pos % 2)
    row = 0
    blocks = []
    for (near, first), ref in zip(pieces, piece_refs):
        rows = ref.shape[0]
        x_ref[row : row + rows, :] = ref[...]
        row += rows
        run = pos + step if near else pos - step
        blocks += [run * queries + first + i for i in range(rows // size)]
    project(x_ref[...], wk_ref, wv_ref, k_ref, vt_ref)
    attend_listed(
        False, size, blocks, list_ref, count_ref, found_ref, q_ref, k_ref, vt_ref, *state
    )


def halo_kernel(size, pieces, list_ref, count_ref, pos_ref, *refs):
    n = len(pieces)
    wk_ref, wv_ref, q_ref = refs[n : n + 3]
    attend_halo(
        size, pieces, list_ref, count_ref, pos_ref, refs[:n], wk_ref, wv_ref, q_ref, refs[n + 6 : n + 9], refs[n + 9 :]
    )


def final_kernel(size, pieces, list_ref, count_ref, pos_ref, *refs):
    n = len(pieces)
    wk_ref, wv_ref, q_ref, lin_ref, wo_ref = refs[n : n + 5]
    out_ref, m_ref, l_ref, acc_ref, comb_ref = refs[n + 8 : n + 13]
    attend_halo(
        size,
        pieces,
        list_ref,
        count_ref,
        pos_ref,
        refs[:n],
        wk_ref,
        wv_ref,
        q_ref,
        (m_ref, l_ref, acc_ref),
        refs[n + 13 :],
    )

    def finish(qb, carry):
        rows = tile(qb, size)
        share = 1.0 / l_ref[qb]
        for p in range(H // 2):
            cols = slice(p * 2 * DH, (p + 1) * 2 * DH)
            both = acc_ref[qb, cols, :] * by_head(share[p : p + 1], size) + lin_ref[cols, rows]
            comb_ref[rows, cols] = both.T.astype(BF16)
        return carry

    lax.fori_loop(0, list_ref.shape[0], finish, 0)
    out_ref[...] = dot_nn(comb_ref[...], wo_ref[...]).astype(BF16)


COSTLY = ("within",)


def call(
    kernel,
    name,
    ins,
    outs,
    smem=0,
    scratch=(),
    aliases=None,
    limit=20 * MIB,
    space=pltpu.VMEM,
    out_space=pltpu.VMEM,
):
    return pl.pallas_call(
        kernel,
        name=name,
        in_specs=[SMEM] * smem + [pl.BlockSpec(memory_space=space)] * (len(ins) - smem),
        out_specs=[
            pl.BlockSpec(memory_space=m)
            for m in (out_space if isinstance(out_space, list) else [out_space] * len(outs))
        ],
        out_shape=[jax.ShapeDtypeStruct(s, d) for s, d in outs],
        scratch_shapes=list(scratch),
        input_output_aliases=aliases or {},
        cost_estimate=pl.CostEstimate(
            flops=10**11 if name in COSTLY else 1, bytes_accessed=1000, transcendentals=0
        ),
        compiler_params=pltpu.CompilerParams(vmem_limit_bytes=limit),
    )(*ins)


def after(value, *done):
    return lax.optimization_barrier((value,) + done)[0]


def on_device(tokens, qk_weight, value_weight, out_weight, neighbour_list, neighbour_count):
    rows = tokens.shape[1]
    width = tokens.shape[2]
    blocks = neighbour_list.shape[1]
    size = rows // blocks
    half = blocks // 2
    count = lax.axis_size("seq")
    position = lax.axis_index("seq").astype(jnp.int32).reshape(1)
    own = tokens[0]
    tables = (neighbour_list[0], neighbour_count[0], position)

    def swap(value, bit):
        return lax.ppermute(value, "seq", [(i, i ^ bit) for i in range(count)])

    def up(value, bit):
        return lax.ppermute(value, "seq", [(i, i | bit) for i in range(count) if not i & bit])

    def onward(value):
        pairs = [(i, i + 2) for i in range(0, count - 2, 2)] + [(i, i - 2) for i in range(3, count, 2)]
        return lax.ppermute(value, "seq", pairs)

    def across(value):
        odd = range(1, count - 1, 2)
        return lax.ppermute(value, "seq", [(i, i + 1) for i in odd] + [(i + 1, i) for i in odd])

    def flat(total):
        return (
            pltpu.SMEM((total // size + 2,), jnp.int32),
            pltpu.VMEM((total, width), BF16),
            pltpu.VMEM((total, width), BF16),
            pltpu.VMEM((width, total), BF16),
        )

    def join_halo(name, softmax, pieces, arrays):
        ins = tables + tuple(arrays) + (qk_weight, value_weight, keyed) + tuple(softmax)
        first = len(ins) - 3
        return call(
            functools.partial(halo_kernel, size, pieces),
            name,
            ins,
            shapes,
            smem=3,
            scratch=flat(sum(a.shape[0] for a in arrays)),
            aliases={first + i: i for i in range(3)},
        )

    cut = half * size
    in_hbm = functools.partial(pltpu.with_memory_space_constraint, memory_space=pltpu.HBM)
    (first_rows,) = call(
        cut_kernel,
        "cut",
        (in_hbm(own),),
        [((cut, width), BF16)],
        scratch=(pltpu.SemaphoreType.DMA(()),),
        space=pltpu.HBM,
    )
    near_a = swap(first_rows, 1)
    keyed, values_t, last_rows, state = call(
        own_kernel,
        "own",
        (in_hbm(after(own, first_rows)), in_hbm(qk_weight), in_hbm(value_weight)),
        [
            ((rows, width), BF16),
            ((width, rows), BF16),
            ((rows - cut, width), BF16),
            ((width, DL), BF16),
        ],
        scratch=(
            pltpu.VMEM((rows, width), BF16),
            pltpu.VMEM((width, width), BF16),
            pltpu.VMEM((width, width), BF16),
            pltpu.VMEM((rows, width), BF16),
            pltpu.VMEM((width, rows), BF16),
            pltpu.SemaphoreType.DMA((3,)),
            pltpu.SemaphoreType.DMA((3,)),
        ),
        limit=56 * MIB,
        space=pltpu.HBM,
        out_space=[pltpu.HBM] * 3 + [pltpu.VMEM],
    )
    far_b = across(last_rows)
    def halves(value, bit):
        return (swap if 2 * bit < count else up)(value, bit)

    heard = [halves(state, 2)]
    shapes = [((blocks, H // 2, 2 * size), F32)] * 2 + [((blocks, width, size), F32)]
    softmax = call(
        functools.partial(own_attention_kernel, size),
        "own_attention",
        tables + (in_hbm(keyed), in_hbm(values_t)),
        shapes,
        smem=3,
        scratch=(pltpu.SMEM((blocks + 1,), jnp.int32),),
    )
    total = state
    stride = 4
    while stride < count:
        total = total + after(heard[-1], softmax[0])
        heard.append(halves(total, stride))
        stride *= 2
    far_a = onward(after(near_a, total))
    near_b = swap(after(last_rows, near_a), 1)
    (within,) = call(
        within_kernel,
        "within",
        (after(keyed, softmax[0], near_a), values_t),
        [((width, rows), F32)],
    )
    softmax = join_halo("halo_a", softmax, [(True, 0)], [after(near_a, within)])
    (message,) = call(
        functools.partial(carry_kernel, len(heard)),
        "carry",
        (position, after(state, softmax[0])) + tuple(heard),
        [((width, DL), BF16)],
        smem=1,
    )
    message = swap(message, 1)
    softmax = join_halo("halo_b", softmax, [(False, half)], [after(far_b, heard[-1], softmax[0])])
    softmax = join_halo("halo_c", softmax, [(False, 0)], [after(far_a, softmax[0])])
    (linear,) = call(
        functools.partial(linear_kernel, len(heard)),
        "linear",
        (position, after(keyed, softmax[0]), within) + tuple(heard) + (message,),
        [((width, rows), F32)],
        smem=1,
    )
    pieces = [(True, half)]
    arrays = (after(near_b, linear),)
    ins = tables + arrays + (qk_weight, value_weight, keyed, linear, out_weight) + tuple(softmax)
    first = len(ins) - 3
    update, *_ = call(
        functools.partial(final_kernel, size, pieces),
        "final",
        ins,
        [((rows, width), BF16)] + shapes,
        smem=3,
        scratch=(pltpu.VMEM((rows, width), BF16),) + flat(sum(a.shape[0] for a in arrays)),
        aliases={first + i: i + 1 for i in range(3)},
    )
    return update[None]


def solution(mesh):
    placed = (
        P(("groups", "dp"), "seq", None),
        P(),
        P(),
        P(),
        P(("groups", "dp"), "seq", None),
        P(("groups", "dp"), "seq"),
    )
    return jax.shard_map(
        on_device,
        mesh=mesh,
        in_specs=placed,
        out_specs=P(("groups", "dp"), "seq", None),
        check_vma=False,
    )
```

```python
import functools

import jax
import jax.numpy as jnp
from jax import lax
from jax.experimental import pallas as pl
from jax.experimental.pallas import tpu as pltpu
from jax.sharding import PartitionSpec as P

H = 16
DH = 64
HL = 8
DL = 128
F32 = jnp.float32
BF16 = jnp.bfloat16
NT = (((1,), (1,)), ((), ()))
SMEM = pl.BlockSpec(memory_space=pltpu.SMEM)
MIB = 1 << 20


def dot_nt(a, b):
    return lax.dot_general(a, b, NT, preferred_element_type=F32)


def dot_nn(a, b):
    return jnp.dot(a, b, preferred_element_type=F32)


def tile(i, size):
    return pl.ds(pl.multiple_of(i * size, size), size)


def silu(k):
    k = k.astype(F32)
    return (k / (1.0 + jnp.exp(-k))).astype(BF16)


def project(x, wk_ref, wv_ref, k_ref, vt_ref):
    k_ref[...] = dot_nn(x, wk_ref[...]).astype(BF16)
    step = 256
    for i in range(0, wv_ref.shape[1], step):
        part = slice(i, i + step)
        vt_ref[part, :] = dot_nn(x, wv_ref[:, part]).astype(BF16).T


def cut_kernel(x_hbm, a_ref, sem):
    copy = pltpu.make_async_copy(x_hbm.at[: a_ref.shape[0]], a_ref, sem)
    copy.start()
    copy.wait()


def own_kernel(
    x_hbm, wk_hbm, wv_hbm, k_hbm, vt_hbm, b_hbm, s_ref, x_ref, wk_ref, wv_ref, k_ref, vt_ref, in_sems, out_sems
):
    ins = [
        pltpu.make_async_copy(src, dst, in_sems.at[i])
        for i, (src, dst) in enumerate(((x_hbm, x_ref), (wk_hbm, wk_ref), (wv_hbm, wv_ref)))
    ]
    outs = [
        pltpu.make_async_copy(src, dst, out_sems.at[i])
        for i, (src, dst) in enumerate(
            ((x_ref.at[x_ref.shape[0] - b_hbm.shape[0] :], b_hbm), (k_ref, k_hbm), (vt_ref, vt_hbm))
        )
    ]
    for copy in ins:
        copy.start()
    ins[0].wait()
    outs[0].start()
    ins[1].wait()
    k_ref[...] = dot_nn(x_ref[...], wk_ref[...]).astype(BF16)
    outs[1].start()
    ins[2].wait()
    step = 256
    for i in range(0, wv_ref.shape[1], step):
        part = slice(i, i + step)
        vt_ref[part, :] = dot_nt(wv_ref[:, part].T, x_ref[...]).astype(BF16)
    for h in range(HL):
        part = slice(h * DL, (h + 1) * DL)
        s_ref[part, :] = dot_nn(vt_ref[part, :], silu(k_ref[:, part])).astype(BF16)
    outs[2].start()
    for copy in outs:
        copy.wait()


def within_kernel(k_ref, vt_ref, n_ref):
    rows = k_ref.shape[0]
    half = rows // 2
    upper = lax.broadcasted_iota(jnp.int32, (half, half), 0) <= lax.broadcasted_iota(
        jnp.int32, (half, half), 1
    )

    def head(h, carry):
        cols = tile(h, DL)
        f0 = silu(k_ref[:half, cols])
        f1 = silu(k_ref[half:, cols])
        v0 = vt_ref[cols, :half]
        v1 = vt_ref[cols, half:]
        a00 = jnp.where(upper, dot_nt(f0, f0), 0.0).astype(BF16)
        a01 = dot_nt(f0, f1).astype(BF16)
        a11 = jnp.where(upper, dot_nt(f1, f1), 0.0).astype(BF16)
        n_ref[cols, :half] = dot_nn(v0, a00)
        n_ref[cols, half:] = dot_nn(v0, a01) + dot_nn(v1, a11)
        return carry

    lax.fori_loop(0, HL, head, 0, unroll=2)


def set_bits(pos_ref, count):
    return [((pos_ref[0] >> (k + 1)) & 1).astype(F32) for k in range(count)]


def carry_kernel(stages, pos_ref, s_ref, *refs):
    bits = set_bits(pos_ref, stages)
    first = 1.0 - (pos_ref[0] & 1).astype(F32)
    total = s_ref[...].astype(F32) * first
    for ref, bit in zip(refs, bits):
        total = total + ref[...].astype(F32) * bit
    refs[stages][...] = total.astype(BF16)


def linear_kernel(stages, pos_ref, k_ref, n_ref, *refs):
    heard, message_ref, o_ref = refs[:stages], refs[stages], refs[stages + 1]
    bits = set_bits(pos_ref, stages)

    def head(h, carry):
        cols = tile(h, DL)
        before = message_ref[cols, :].astype(F32)
        for ref, bit in zip(heard, bits):
            before = before + ref[cols, :].astype(F32) * bit
        n = n_ref[cols, :] + dot_nt(before.astype(BF16), silu(k_ref[:, cols]))
        mean = jnp.sum(n * n, axis=0, keepdims=True) * (1.0 / DL)
        o_ref[cols, :] = n * lax.rsqrt(mean + 1e-06)
        return carry

    lax.fori_loop(0, HL, head, 0, unroll=2)


def listed(list_ref, count_ref, qb, block):
    found = False
    for j in range(list_ref.shape[1]):
        found = jnp.logical_or(
            found, jnp.logical_and(j < count_ref[qb], list_ref[qb, j] == block)
        )
    return found


def attend(first, size, qb, kbs, q_ref, k_ref, vt_ref, m_ref, l_ref, acc_ref):
    qrows = tile(qb, size)
    krows = [tile(kb, size) for kb in kbs]
    lane = lax.broadcasted_iota(jnp.int32, (size, 2 * DH), 1)
    pairs = H // 2
    cols = [slice(p * 2 * DH, (p + 1) * 2 * DH) for p in range(pairs)]
    if first:
        shape = (size * len(kbs), 2 * size)
        key = lax.broadcasted_iota(jnp.int32, shape, 0)
        query = lax.broadcasted_iota(jnp.int32, shape, 1) % size
        other = key != query
    else:
        tops = m_ref[qb]
        totals = l_ref[qb]
    scores = []
    for p in range(pairs):
        q = q_ref[qrows, cols[p]] * jnp.asarray(DH ** (-0.5), BF16)
        zero = jnp.zeros_like(q)
        pair = jnp.concatenate([jnp.where(lane < DH, q, zero), jnp.where(lane < DH, zero, q)], axis=0)
        k = jnp.concatenate([k_ref[r, cols[p]] for r in krows], axis=0)
        s = dot_nt(k, pair)
        scores.append(jnp.where(other, s, -1e30) if first else s)
    raised = []
    new_tops = []
    new_totals = []
    for p in range(pairs):
        top = jnp.max(scores[p], axis=0, keepdims=True)
        if not first:
            top = jnp.maximum(top, tops[p : p + 1])
        e = jnp.exp(scores[p] - top)
        new_tops.append(top)
        new_totals.append(jnp.sum(e, axis=0, keepdims=True))
        raised.append(e.astype(BF16))
    for p in range(pairs):
        v = jnp.concatenate([vt_ref[cols[p], r] for r in krows], axis=1)
        o = dot_nn(v, raised[p])
        o = jnp.concatenate([o[:DH, :size], o[DH:, size:]], axis=0)
        if not first:
            fade = jnp.exp(tops[p : p + 1] - new_tops[p])
            new_totals[p] = new_totals[p] + totals[p : p + 1] * fade
            o = o + acc_ref[qb, cols[p], :] * by_head(fade, size)
        acc_ref[qb, cols[p], :] = o
    m_ref[qb] = jnp.concatenate(new_tops, axis=0)
    l_ref[qb] = jnp.concatenate(new_totals, axis=0)


def by_head(row, size):
    return jnp.concatenate(
        [jnp.broadcast_to(row[:, :size], (DH, size)), jnp.broadcast_to(row[:, size:], (DH, size))], axis=0
    )


def attend_listed(own, size, blocks, list_ref, count_ref, found_ref, *rest):
    def query(qb, carry):
        found_ref[0] = qb
        n = jnp.int32(1 if own else 0)
        for kb, block in enumerate(blocks):
            wanted = listed(list_ref, count_ref, qb, block)
            if own:
                wanted = jnp.logical_and(wanted, qb != kb)

            @pl.when(wanted)
            def _(n=n, kb=kb):
                found_ref[n] = kb

            n = n + wanted.astype(jnp.int32)
        start = 0
        if own:

            @pl.when(n == 1)
            def _():
                attend(True, size, qb, [qb], *rest)

            @pl.when(n > 1)
            def _():
                attend(True, size, qb, [qb, found_ref[1]], *rest)

            start = 2
        if len(blocks) - start > 1:

            def two(i, carry):
                attend(False, size, qb, [found_ref[start + 2 * i], found_ref[start + 2 * i + 1]], *rest)
                return carry

            lax.fori_loop(0, jnp.maximum(n - start, 0) // 2, two, 0)

        @pl.when(jnp.logical_and(n > start, n % 2 == 1))
        def _():
            attend(False, size, qb, [found_ref[n - 1]], *rest)

        return carry

    lax.fori_loop(0, list_ref.shape[0], query, 0)


def own_attention_kernel(size, list_ref, count_ref, pos_ref, k_ref, vt_ref, m_ref, l_ref, acc_ref, found_ref):
    queries = list_ref.shape[0]
    blocks = [pos_ref[0] * queries + kb for kb in range(queries)]
    attend_listed(
        True, size, blocks, list_ref, count_ref, found_ref, k_ref, k_ref, vt_ref, m_ref, l_ref, acc_ref
    )


def attend_halo(size, pieces, list_ref, count_ref, pos_ref, piece_refs, wk_ref, wv_ref, q_ref, state, scratch):
    found_ref, x_ref, k_ref, vt_ref = scratch
    queries = list_ref.shape[0]
    pos = pos_ref[0]
    step = 1 - 2 * (pos % 2)
    row = 0
    blocks = []
    for (near, first), ref in zip(pieces, piece_refs):
        rows = ref.shape[0]
        x_ref[row : row + rows, :] = ref[...]
        row += rows
        run = pos + step if near else pos - step
        blocks += [run * queries + first + i for i in range(rows // size)]
    project(x_ref[...], wk_ref, wv_ref, k_ref, vt_ref)
    attend_listed(
        False, size, blocks, list_ref, count_ref, found_ref, q_ref, k_ref, vt_ref, *state
    )


def halo_kernel(size, pieces, list_ref, count_ref, pos_ref, *refs):
    n = len(pieces)
    wk_ref, wv_ref, q_ref = refs[n : n + 3]
    attend_halo(
        size, pieces, list_ref, count_ref, pos_ref, refs[:n], wk_ref, wv_ref, q_ref, refs[n + 6 : n + 9], refs[n + 9 :]
    )


def final_kernel(size, pieces, list_ref, count_ref, pos_ref, *refs):
    n = len(pieces)
    wk_ref, wv_ref, q_ref, lin_ref, wo_ref = refs[n : n + 5]
    out_ref, m_ref, l_ref, acc_ref, comb_ref = refs[n + 8 : n + 13]
    attend_halo(
        size,
        pieces,
        list_ref,
        count_ref,
        pos_ref,
        refs[:n],
        wk_ref,
        wv_ref,
        q_ref,
        (m_ref, l_ref, acc_ref),
        refs[n + 13 :],
    )

    def finish(qb, carry):
        rows = tile(qb, size)
        share = 1.0 / l_ref[qb]
        for p in range(H // 2):
            cols = slice(p * 2 * DH, (p + 1) * 2 * DH)
            both = acc_ref[qb, cols, :] * by_head(share[p : p + 1], size) + lin_ref[cols, rows]
            comb_ref[rows, cols] = both.T.astype(BF16)
        return carry

    lax.fori_loop(0, list_ref.shape[0], finish, 0, unroll=True)
    out_ref[...] = dot_nn(comb_ref[...], wo_ref[...]).astype(BF16)


COSTLY = ("halo_a",)


def call(
    kernel,
    name,
    ins,
    outs,
    smem=0,
    scratch=(),
    aliases=None,
    limit=20 * MIB,
    space=pltpu.VMEM,
    out_space=pltpu.VMEM,
):
    return pl.pallas_call(
        kernel,
        name=name,
        in_specs=[SMEM] * smem + [pl.BlockSpec(memory_space=space)] * (len(ins) - smem),
        out_specs=[
            pl.BlockSpec(memory_space=m)
            for m in (out_space if isinstance(out_space, list) else [out_space] * len(outs))
        ],
        out_shape=[jax.ShapeDtypeStruct(s, d) for s, d in outs],
        scratch_shapes=list(scratch),
        input_output_aliases=aliases or {},
        cost_estimate=pl.CostEstimate(
            flops=10**11 if name in COSTLY else 1, bytes_accessed=1000, transcendentals=0
        ),
        compiler_params=pltpu.CompilerParams(vmem_limit_bytes=limit),
    )(*ins)


def after(value, *done):
    return lax.optimization_barrier((value,) + done)[0]


def on_device(tokens, qk_weight, value_weight, out_weight, neighbour_list, neighbour_count):
    rows = tokens.shape[1]
    width = tokens.shape[2]
    blocks = neighbour_list.shape[1]
    size = rows // blocks
    half = blocks // 2
    count = lax.axis_size("seq")
    position = lax.axis_index("seq").astype(jnp.int32).reshape(1)
    own = tokens[0]
    tables = (neighbour_list[0], neighbour_count[0], position)

    def swap(value, bit):
        return lax.ppermute(value, "seq", [(i, i ^ bit) for i in range(count)])

    def up(value, bit):
        return lax.ppermute(value, "seq", [(i, i | bit) for i in range(count) if not i & bit])

    def onward(value):
        pairs = [(i, i + 2) for i in range(0, count - 2, 2)] + [(i, i - 2) for i in range(3, count, 2)]
        return lax.ppermute(value, "seq", pairs)

    def across(value):
        odd = range(1, count - 1, 2)
        return lax.ppermute(value, "seq", [(i, i + 1) for i in odd] + [(i + 1, i) for i in odd])

    def flat(total):
        return (
            pltpu.SMEM((total // size + 2,), jnp.int32),
            pltpu.VMEM((total, width), BF16),
            pltpu.VMEM((total, width), BF16),
            pltpu.VMEM((width, total), BF16),
        )

    def join_halo(name, softmax, pieces, arrays):
        ins = tables + tuple(arrays) + (qk_weight, value_weight, keyed) + tuple(softmax)
        first = len(ins) - 3
        return call(
            functools.partial(halo_kernel, size, pieces),
            name,
            ins,
            shapes,
            smem=3,
            scratch=flat(sum(a.shape[0] for a in arrays)),
            aliases={first + i: i for i in range(3)},
        )

    cut = half * size
    in_hbm = functools.partial(pltpu.with_memory_space_constraint, memory_space=pltpu.HBM)
    (first_rows,) = call(
        cut_kernel,
        "cut",
        (in_hbm(own),),
        [((cut, width), BF16)],
        scratch=(pltpu.SemaphoreType.DMA(()),),
        space=pltpu.HBM,
    )
    near_a = swap(first_rows, 1)
    keyed, values_t, last_rows, state = call(
        own_kernel,
        "own",
        (in_hbm(after(own, first_rows)), in_hbm(qk_weight), in_hbm(value_weight)),
        [
            ((rows, width), BF16),
            ((width, rows), BF16),
            ((rows - cut, width), BF16),
            ((width, DL), BF16),
        ],
        scratch=(
            pltpu.VMEM((rows, width), BF16),
            pltpu.VMEM((width, width), BF16),
            pltpu.VMEM((width, width), BF16),
            pltpu.VMEM((rows, width), BF16),
            pltpu.VMEM((width, rows), BF16),
            pltpu.SemaphoreType.DMA((3,)),
            pltpu.SemaphoreType.DMA((3,)),
        ),
        limit=56 * MIB,
        space=pltpu.HBM,
        out_space=[pltpu.HBM] * 3 + [pltpu.VMEM],
    )
    far_b = across(last_rows)
    def halves(value, bit):
        return swap(value, bit)

    heard = [halves(state, 2)]
    shapes = [((blocks, H // 2, 2 * size), F32)] * 2 + [((blocks, width, size), F32)]
    softmax = call(
        functools.partial(own_attention_kernel, size),
        "own_attention",
        tables + (in_hbm(keyed), in_hbm(values_t)),
        shapes,
        smem=3,
        scratch=(pltpu.SMEM((blocks + 1,), jnp.int32),),
    )
    total = state
    stride = 4
    while stride < count:
        total = total + after(heard[-1], softmax[0])
        heard.append(halves(total, stride))
        stride *= 2
    far_a = onward(after(near_a, total))
    near_b = swap(after(last_rows, near_a), 1)
    (within,) = call(
        within_kernel,
        "within",
        (after(keyed, softmax[0], near_a), values_t),
        [((width, rows), F32)],
    )
    softmax = join_halo("halo_a", softmax, [(True, 0)], [after(near_a, within)])
    (message,) = call(
        functools.partial(carry_kernel, len(heard)),
        "carry",
        (position, after(state, softmax[0])) + tuple(heard),
        [((width, DL), BF16)],
        smem=1,
    )
    message = swap(message, 1)
    softmax = join_halo("halo_b", softmax, [(False, half)], [after(far_b, heard[-1], softmax[0])])
    softmax = join_halo("halo_c", softmax, [(False, 0)], [after(far_a, softmax[0])])
    (linear,) = call(
        functools.partial(linear_kernel, len(heard)),
        "linear",
        (position, after(keyed, softmax[0]), within) + tuple(heard) + (message,),
        [((width, rows), F32)],
        smem=1,
    )
    pieces = [(True, half)]
    arrays = (after(near_b, linear),)
    ins = tables + arrays + (qk_weight, value_weight, keyed, linear, out_weight) + tuple(softmax)
    first = len(ins) - 3
    update, *_ = call(
        functools.partial(final_kernel, size, pieces),
        "final",
        ins,
        [((rows, width), BF16)] + shapes,
        smem=3,
        scratch=(pltpu.VMEM((rows, width), BF16),) + flat(sum(a.shape[0] for a in arrays)),
        aliases={first + i: i + 1 for i in range(3)},
    )
    return update[None]


def solution(mesh):
    placed = (
        P(("groups", "dp"), "seq", None),
        P(),
        P(),
        P(),
        P(("groups", "dp"), "seq", None),
        P(("groups", "dp"), "seq"),
    )
    return jax.shard_map(
        on_device,
        mesh=mesh,
        in_specs=placed,
        out_specs=P(("groups", "dp"), "seq", None),
        check_vma=False,
    )
```

```python
import functools

import jax
import jax.numpy as jnp
from jax import lax
from jax.experimental import pallas as pl
from jax.experimental.pallas import tpu as pltpu
from jax.sharding import PartitionSpec as P

H = 16
DH = 64
HL = 8
DL = 128
F32 = jnp.float32
BF16 = jnp.bfloat16
NT = (((1,), (1,)), ((), ()))
SMEM = pl.BlockSpec(memory_space=pltpu.SMEM)
MIB = 1 << 20


def dot_nt(a, b):
    return lax.dot_general(a, b, NT, preferred_element_type=F32)


def dot_nn(a, b):
    return jnp.dot(a, b, preferred_element_type=F32)


def tile(i, size):
    return pl.ds(pl.multiple_of(i * size, size), size)


def silu(k):
    k = k.astype(F32)
    return (k / (1.0 + jnp.exp(-k))).astype(BF16)


def project(x, wk_ref, wv_ref, k_ref, vt_ref):
    k_ref[...] = dot_nn(x, wk_ref[...]).astype(BF16)
    step = 256
    for i in range(0, wv_ref.shape[1], step):
        part = slice(i, i + step)
        vt_ref[part, :] = dot_nn(x, wv_ref[:, part]).astype(BF16).T


def cut_kernel(x_hbm, a_ref, sem):
    copy = pltpu.make_async_copy(x_hbm.at[: a_ref.shape[0]], a_ref, sem)
    copy.start()
    copy.wait()


def own_kernel(
    x_hbm, wk_hbm, wv_hbm, k_hbm, vt_hbm, b_hbm, s_ref, x_ref, wk_ref, wv_ref, k_ref, vt_ref, in_sems, out_sems
):
    ins = [
        pltpu.make_async_copy(src, dst, in_sems.at[i])
        for i, (src, dst) in enumerate(((x_hbm, x_ref), (wk_hbm, wk_ref), (wv_hbm, wv_ref)))
    ]
    outs = [
        pltpu.make_async_copy(src, dst, out_sems.at[i])
        for i, (src, dst) in enumerate(
            ((x_ref.at[x_ref.shape[0] - b_hbm.shape[0] :], b_hbm), (k_ref, k_hbm), (vt_ref, vt_hbm))
        )
    ]
    for copy in ins:
        copy.start()
    ins[0].wait()
    outs[0].start()
    ins[1].wait()
    k_ref[...] = dot_nn(x_ref[...], wk_ref[...]).astype(BF16)
    outs[1].start()
    ins[2].wait()
    step = 256
    for i in range(0, wv_ref.shape[1], step):
        part = slice(i, i + step)
        vt_ref[part, :] = dot_nt(wv_ref[:, part].T, x_ref[...]).astype(BF16)
    for h in range(HL):
        part = slice(h * DL, (h + 1) * DL)
        s_ref[part, :] = dot_nn(vt_ref[part, :], silu(k_ref[:, part])).astype(BF16)
    outs[2].start()
    for copy in outs:
        copy.wait()


def within_kernel(k_ref, vt_ref, n_ref):
    rows = k_ref.shape[0]
    half = rows // 2
    upper = lax.broadcasted_iota(jnp.int32, (half, half), 0) <= lax.broadcasted_iota(
        jnp.int32, (half, half), 1
    )

    def head(h, carry):
        cols = tile(h, DL)
        f0 = silu(k_ref[:half, cols])
        f1 = silu(k_ref[half:, cols])
        v0 = vt_ref[cols, :half]
        v1 = vt_ref[cols, half:]
        a00 = jnp.where(upper, dot_nt(f0, f0), 0.0).astype(BF16)
        a01 = dot_nt(f0, f1).astype(BF16)
        a11 = jnp.where(upper, dot_nt(f1, f1), 0.0).astype(BF16)
        n_ref[cols, :half] = dot_nn(v0, a00)
        n_ref[cols, half:] = dot_nn(v0, a01) + dot_nn(v1, a11)
        return carry

    lax.fori_loop(0, HL, head, 0, unroll=2)


def set_bits(pos_ref, count):
    return [((pos_ref[0] >> (k + 1)) & 1).astype(F32) for k in range(count)]


def carry_kernel(stages, pos_ref, s_ref, *refs):
    bits = set_bits(pos_ref, stages)
    first = 1.0 - (pos_ref[0] & 1).astype(F32)
    total = s_ref[...].astype(F32) * first
    for ref, bit in zip(refs, bits):
        total = total + ref[...].astype(F32) * bit
    refs[stages][...] = total.astype(BF16)


def linear_kernel(stages, pos_ref, k_ref, n_ref, *refs):
    heard, message_ref, o_ref = refs[:stages], refs[stages], refs[stages + 1]
    bits = set_bits(pos_ref, stages)

    def head(h, carry):
        cols = tile(h, DL)
        before = message_ref[cols, :].astype(F32)
        for ref, bit in zip(heard, bits):
            before = before + ref[cols, :].astype(F32) * bit
        n = n_ref[cols, :] + dot_nt(before.astype(BF16), silu(k_ref[:, cols]))
        mean = jnp.sum(n * n, axis=0, keepdims=True) * (1.0 / DL)
        o_ref[cols, :] = n * lax.rsqrt(mean + 1e-06)
        return carry

    lax.fori_loop(0, HL, head, 0, unroll=2)


def listed(list_ref, count_ref, qb, block):
    found = False
    for j in range(list_ref.shape[1]):
        found = jnp.logical_or(
            found, jnp.logical_and(j < count_ref[qb], list_ref[qb, j] == block)
        )
    return found


def attend(first, size, qb, kbs, q_ref, k_ref, vt_ref, m_ref, l_ref, acc_ref):
    qrows = tile(qb, size)
    krows = [tile(kb, size) for kb in kbs]
    lane = lax.broadcasted_iota(jnp.int32, (size, 2 * DH), 1)
    pairs = H // 2
    cols = [slice(p * 2 * DH, (p + 1) * 2 * DH) for p in range(pairs)]
    if first:
        shape = (size * len(kbs), 2 * size)
        key = lax.broadcasted_iota(jnp.int32, shape, 0)
        query = lax.broadcasted_iota(jnp.int32, shape, 1) % size
        other = key != query
    else:
        tops = m_ref[qb]
        totals = l_ref[qb]
    scores = []
    for p in range(pairs):
        q = q_ref[qrows, cols[p]] * jnp.asarray(DH ** (-0.5), BF16)
        zero = jnp.zeros_like(q)
        pair = jnp.concatenate([jnp.where(lane < DH, q, zero), jnp.where(lane < DH, zero, q)], axis=0)
        k = jnp.concatenate([k_ref[r, cols[p]] for r in krows], axis=0)
        s = dot_nt(k, pair)
        scores.append(jnp.where(other, s, -1e30) if first else s)
    raised = []
    new_tops = []
    new_totals = []
    for p in range(pairs):
        top = jnp.max(scores[p], axis=0, keepdims=True)
        if not first:
            top = jnp.maximum(top, tops[p : p + 1])
        e = jnp.exp(scores[p] - top)
        new_tops.append(top)
        new_totals.append(jnp.sum(e, axis=0, keepdims=True))
        raised.append(e.astype(BF16))
    for p in range(pairs):
        v = jnp.concatenate([vt_ref[cols[p], r] for r in krows], axis=1)
        o = dot_nn(v, raised[p])
        o = jnp.concatenate([o[:DH, :size], o[DH:, size:]], axis=0)
        if not first:
            fade = jnp.exp(tops[p : p + 1] - new_tops[p])
            new_totals[p] = new_totals[p] + totals[p : p + 1] * fade
            o = o + acc_ref[qb, cols[p], :] * by_head(fade, size)
        acc_ref[qb, cols[p], :] = o
    m_ref[qb] = jnp.concatenate(new_tops, axis=0)
    l_ref[qb] = jnp.concatenate(new_totals, axis=0)


def by_head(row, size):
    return jnp.concatenate(
        [jnp.broadcast_to(row[:, :size], (DH, size)), jnp.broadcast_to(row[:, size:], (DH, size))], axis=0
    )


def attend_listed(own, size, blocks, list_ref, count_ref, found_ref, *rest):
    def query(qb, carry):
        found_ref[0] = qb
        n = jnp.int32(1 if own else 0)
        for kb, block in enumerate(blocks):
            wanted = listed(list_ref, count_ref, qb, block)
            if own:
                wanted = jnp.logical_and(wanted, qb != kb)

            @pl.when(wanted)
            def _(n=n, kb=kb):
                found_ref[n] = kb

            n = n + wanted.astype(jnp.int32)
        start = 0
        if own:

            @pl.when(n == 1)
            def _():
                attend(True, size, qb, [qb], *rest)

            @pl.when(n > 1)
            def _():
                attend(True, size, qb, [qb, found_ref[1]], *rest)

            start = 2
        if len(blocks) - start > 1:

            def two(i, carry):
                attend(False, size, qb, [found_ref[start + 2 * i], found_ref[start + 2 * i + 1]], *rest)
                return carry

            lax.fori_loop(0, jnp.maximum(n - start, 0) // 2, two, 0)

        @pl.when(jnp.logical_and(n > start, n % 2 == 1))
        def _():
            attend(False, size, qb, [found_ref[n - 1]], *rest)

        return carry

    lax.fori_loop(0, list_ref.shape[0], query, 0)


def own_attention_kernel(size, list_ref, count_ref, pos_ref, k_ref, vt_ref, m_ref, l_ref, acc_ref, found_ref):
    queries = list_ref.shape[0]
    blocks = [pos_ref[0] * queries + kb for kb in range(queries)]
    attend_listed(
        True, size, blocks, list_ref, count_ref, found_ref, k_ref, k_ref, vt_ref, m_ref, l_ref, acc_ref
    )


def attend_halo(size, pieces, list_ref, count_ref, pos_ref, piece_refs, wk_ref, wv_ref, q_ref, state, scratch):
    found_ref, x_ref, k_ref, vt_ref = scratch
    queries = list_ref.shape[0]
    pos = pos_ref[0]
    step = 1 - 2 * (pos % 2)
    row = 0
    blocks = []
    for (near, first), ref in zip(pieces, piece_refs):
        rows = ref.shape[0]
        x_ref[row : row + rows, :] = ref[...]
        row += rows
        run = pos + step if near else pos - step
        blocks += [run * queries + first + i for i in range(rows // size)]
    project(x_ref[...], wk_ref, wv_ref, k_ref, vt_ref)
    attend_listed(
        False, size, blocks, list_ref, count_ref, found_ref, q_ref, k_ref, vt_ref, *state
    )


def halo_kernel(size, pieces, list_ref, count_ref, pos_ref, *refs):
    n = len(pieces)
    wk_ref, wv_ref, q_ref = refs[n : n + 3]
    attend_halo(
        size, pieces, list_ref, count_ref, pos_ref, refs[:n], wk_ref, wv_ref, q_ref, refs[n + 6 : n + 9], refs[n + 9 :]
    )


def final_kernel(size, pieces, list_ref, count_ref, pos_ref, *refs):
    n = len(pieces)
    wk_ref, wv_ref, q_ref, lin_ref, wo_ref = refs[n : n + 5]
    out_ref, m_ref, l_ref, acc_ref, comb_ref = refs[n + 8 : n + 13]
    attend_halo(
        size,
        pieces,
        list_ref,
        count_ref,
        pos_ref,
        refs[:n],
        wk_ref,
        wv_ref,
        q_ref,
        (m_ref, l_ref, acc_ref),
        refs[n + 13 :],
    )

    def finish(qb, carry):
        rows = tile(qb, size)
        share = 1.0 / l_ref[qb]
        for p in range(H // 2):
            cols = slice(p * 2 * DH, (p + 1) * 2 * DH)
            both = acc_ref[qb, cols, :] * by_head(share[p : p + 1], size) + lin_ref[cols, rows]
            comb_ref[rows, cols] = both.T.astype(BF16)
        return carry

    lax.fori_loop(0, list_ref.shape[0], finish, 0, unroll=True)
    out_ref[...] = dot_nn(comb_ref[...], wo_ref[...]).astype(BF16)


COSTLY = ("halo_a",)


def call(
    kernel,
    name,
    ins,
    outs,
    smem=0,
    scratch=(),
    aliases=None,
    limit=20 * MIB,
    space=pltpu.VMEM,
    out_space=pltpu.VMEM,
):
    return pl.pallas_call(
        kernel,
        name=name,
        in_specs=[SMEM] * smem + [pl.BlockSpec(memory_space=space)] * (len(ins) - smem),
        out_specs=[
            pl.BlockSpec(memory_space=m)
            for m in (out_space if isinstance(out_space, list) else [out_space] * len(outs))
        ],
        out_shape=[jax.ShapeDtypeStruct(s, d) for s, d in outs],
        scratch_shapes=list(scratch),
        input_output_aliases=aliases or {},
        cost_estimate=pl.CostEstimate(
            flops=10**11 if name in COSTLY else 1, bytes_accessed=1000, transcendentals=0
        ),
        compiler_params=pltpu.CompilerParams(vmem_limit_bytes=limit),
    )(*ins)


def after(value, *done):
    return lax.optimization_barrier((value,) + done)[0]


def on_device(tokens, qk_weight, value_weight, out_weight, neighbour_list, neighbour_count):
    rows = tokens.shape[1]
    width = tokens.shape[2]
    blocks = neighbour_list.shape[1]
    size = rows // blocks
    half = blocks // 2
    count = lax.axis_size("seq")
    position = lax.axis_index("seq").astype(jnp.int32).reshape(1)
    own = tokens[0]
    tables = (neighbour_list[0], neighbour_count[0], position)

    def swap(value, bit):
        return lax.ppermute(value, "seq", [(i, i ^ bit) for i in range(count)])

    def up(value, bit):
        return lax.ppermute(value, "seq", [(i, i | bit) for i in range(count) if not i & bit])

    def onward(value):
        pairs = [(i, i + 2) for i in range(0, count - 2, 2)] + [(i, i - 2) for i in range(3, count, 2)]
        return lax.ppermute(value, "seq", pairs)

    def across(value):
        odd = range(1, count - 1, 2)
        return lax.ppermute(value, "seq", [(i, i + 1) for i in odd] + [(i + 1, i) for i in odd])

    def flat(total):
        return (
            pltpu.SMEM((total // size + 2,), jnp.int32),
            pltpu.VMEM((total, width), BF16),
            pltpu.VMEM((total, width), BF16),
            pltpu.VMEM((width, total), BF16),
        )

    def join_halo(name, softmax, pieces, arrays):
        ins = tables + tuple(arrays) + (qk_weight, value_weight, keyed) + tuple(softmax)
        first = len(ins) - 3
        return call(
            functools.partial(halo_kernel, size, pieces),
            name,
            ins,
            shapes,
            smem=3,
            scratch=flat(sum(a.shape[0] for a in arrays)),
            aliases={first + i: i for i in range(3)},
        )

    cut = half * size
    in_hbm = functools.partial(pltpu.with_memory_space_constraint, memory_space=pltpu.HBM)
    (first_rows,) = call(
        cut_kernel,
        "cut",
        (in_hbm(own),),
        [((cut, width), BF16)],
        scratch=(pltpu.SemaphoreType.DMA(()),),
        space=pltpu.HBM,
    )
    near_a = swap(first_rows, 1)
    keyed, values_t, last_rows, state = call(
        own_kernel,
        "own",
        (in_hbm(after(own, first_rows)), in_hbm(qk_weight), in_hbm(value_weight)),
        [
            ((rows, width), BF16),
            ((width, rows), BF16),
            ((rows - cut, width), BF16),
            ((width, DL), BF16),
        ],
        scratch=(
            pltpu.VMEM((rows, width), BF16),
            pltpu.VMEM((width, width), BF16),
            pltpu.VMEM((width, width), BF16),
            pltpu.VMEM((rows, width), BF16),
            pltpu.VMEM((width, rows), BF16),
            pltpu.SemaphoreType.DMA((3,)),
            pltpu.SemaphoreType.DMA((3,)),
        ),
        limit=56 * MIB,
        space=pltpu.HBM,
        out_space=[pltpu.HBM] * 3 + [pltpu.VMEM],
    )
    far_b = across(last_rows)
    def halves(value, bit):
        return swap(value, bit)

    heard = [halves(state, 2)]
    shapes = [((blocks, H // 2, 2 * size), F32)] * 2 + [((blocks, width, size), F32)]
    softmax = call(
        functools.partial(own_attention_kernel, size),
        "own_attention",
        tables + (in_hbm(keyed), in_hbm(values_t)),
        shapes,
        smem=3,
        scratch=(pltpu.SMEM((blocks + 1,), jnp.int32),),
    )
    total = state
    stride = 4
    while stride < count:
        total = total + after(heard[-1], softmax[0])
        heard.append(halves(total, stride))
        stride *= 2
    far_a = onward(after(near_a, total))
    near_b = swap(after(last_rows, near_a), 1)
    (within,) = call(
        within_kernel,
        "within",
        (after(keyed, softmax[0], near_a), values_t),
        [((width, rows), F32)],
    )
    softmax = join_halo("halo_a", softmax, [(True, 0)], [after(near_a, within)])
    (message,) = call(
        functools.partial(carry_kernel, len(heard)),
        "carry",
        (position, after(state, softmax[0])) + tuple(heard),
        [((width, DL), BF16)],
        smem=1,
    )
    message = swap(message, 1)
    softmax = join_halo("halo_b", softmax, [(False, half)], [after(far_b, heard[-1], softmax[0])])
    softmax = join_halo("halo_c", softmax, [(True, half)], [after(near_b, softmax[0])])
    (linear,) = call(
        functools.partial(linear_kernel, len(heard)),
        "linear",
        (position, after(keyed, softmax[0]), within) + tuple(heard) + (message,),
        [((width, rows), F32)],
        smem=1,
    )
    pieces = [(False, 0)]
    arrays = (after(far_a, linear),)
    ins = tables + arrays + (qk_weight, value_weight, keyed, linear, out_weight) + tuple(softmax)
    first = len(ins) - 3
    update, *_ = call(
        functools.partial(final_kernel, size, pieces),
        "final",
        ins,
        [((rows, width), BF16)] + shapes,
        smem=3,
        scratch=(pltpu.VMEM((rows, width), BF16),) + flat(sum(a.shape[0] for a in arrays)),
        aliases={first + i: i + 1 for i in range(3)},
    )
    return update[None]


def solution(mesh):
    placed = (
        P(("groups", "dp"), "seq", None),
        P(),
        P(),
        P(),
        P(("groups", "dp"), "seq", None),
        P(("groups", "dp"), "seq"),
    )
    return jax.shard_map(
        on_device,
        mesh=mesh,
        in_specs=placed,
        out_specs=P(("groups", "dp"), "seq", None),
        check_vma=False,
    )
```

```python
import functools

import jax
import jax.numpy as jnp
from jax import lax
from jax.experimental import pallas as pl
from jax.experimental.pallas import tpu as pltpu
from jax.sharding import PartitionSpec as P

H = 16
DH = 64
HL = 8
DL = 128
F32 = jnp.float32
BF16 = jnp.bfloat16
NT = (((1,), (1,)), ((), ()))
SMEM = pl.BlockSpec(memory_space=pltpu.SMEM)
MIB = 1 << 20


def dot_nt(a, b):
    return lax.dot_general(a, b, NT, preferred_element_type=F32)


def dot_nn(a, b):
    return jnp.dot(a, b, preferred_element_type=F32)


def tile(i, size):
    return pl.ds(pl.multiple_of(i * size, size), size)


def silu(k):
    k = k.astype(F32)
    return (k / (1.0 + jnp.exp(-k))).astype(BF16)


def project(x, wk_ref, wv_ref, k_ref, vt_ref):
    k_ref[...] = dot_nn(x, wk_ref[...]).astype(BF16)
    step = 256
    for i in range(0, wv_ref.shape[1], step):
        part = slice(i, i + step)
        vt_ref[part, :] = dot_nn(x, wv_ref[:, part]).astype(BF16).T


def cut_kernel(x_hbm, a_ref, sem):
    copy = pltpu.make_async_copy(x_hbm.at[: a_ref.shape[0]], a_ref, sem)
    copy.start()
    copy.wait()


def own_kernel(
    x_hbm, wk_hbm, wv_hbm, k_hbm, vt_hbm, b_hbm, s_ref, x_ref, wk_ref, wv_ref, k_ref, vt_ref, in_sems, out_sems
):
    ins = [
        pltpu.make_async_copy(src, dst, in_sems.at[i])
        for i, (src, dst) in enumerate(((x_hbm, x_ref), (wk_hbm, wk_ref), (wv_hbm, wv_ref)))
    ]
    outs = [
        pltpu.make_async_copy(src, dst, out_sems.at[i])
        for i, (src, dst) in enumerate(
            ((x_ref.at[x_ref.shape[0] - b_hbm.shape[0] :], b_hbm), (k_ref, k_hbm), (vt_ref, vt_hbm))
        )
    ]
    for copy in ins:
        copy.start()
    ins[0].wait()
    outs[0].start()
    ins[1].wait()
    k_ref[...] = dot_nn(x_ref[...], wk_ref[...]).astype(BF16)
    outs[1].start()
    ins[2].wait()
    step = 256
    for i in range(0, wv_ref.shape[1], step):
        part = slice(i, i + step)
        vt_ref[part, :] = dot_nt(wv_ref[:, part].T, x_ref[...]).astype(BF16)
    for h in range(HL):
        part = slice(h * DL, (h + 1) * DL)
        s_ref[part, :] = dot_nn(vt_ref[part, :], silu(k_ref[:, part])).astype(BF16)
    outs[2].start()
    for copy in outs:
        copy.wait()


def within_kernel(k_ref, vt_ref, n_ref):
    rows = k_ref.shape[0]
    half = rows // 2
    upper = lax.broadcasted_iota(jnp.int32, (half, half), 0) <= lax.broadcasted_iota(
        jnp.int32, (half, half), 1
    )

    def head(h, carry):
        cols = tile(h, DL)
        f0 = silu(k_ref[:half, cols])
        f1 = silu(k_ref[half:, cols])
        v0 = vt_ref[cols, :half]
        v1 = vt_ref[cols, half:]
        a00 = jnp.where(upper, dot_nt(f0, f0), 0.0).astype(BF16)
        a01 = dot_nt(f0, f1).astype(BF16)
        a11 = jnp.where(upper, dot_nt(f1, f1), 0.0).astype(BF16)
        n_ref[cols, :half] = dot_nn(v0, a00)
        n_ref[cols, half:] = dot_nn(v0, a01) + dot_nn(v1, a11)
        return carry

    lax.fori_loop(0, HL, head, 0, unroll=8)


def set_bits(pos_ref, count):
    return [((pos_ref[0] >> (k + 1)) & 1).astype(F32) for k in range(count)]


def carry_kernel(stages, pos_ref, s_ref, *refs):
    bits = set_bits(pos_ref, stages)
    first = 1.0 - (pos_ref[0] & 1).astype(F32)
    total = s_ref[...].astype(F32) * first
    for ref, bit in zip(refs, bits):
        total = total + ref[...].astype(F32) * bit
    refs[stages][...] = total.astype(BF16)


def linear_kernel(stages, pos_ref, k_ref, n_ref, *refs):
    heard, message_ref, o_ref = refs[:stages], refs[stages], refs[stages + 1]
    bits = set_bits(pos_ref, stages)

    def head(h, carry):
        cols = tile(h, DL)
        before = message_ref[cols, :].astype(F32)
        for ref, bit in zip(heard, bits):
            before = before + ref[cols, :].astype(F32) * bit
        n = n_ref[cols, :] + dot_nt(before.astype(BF16), silu(k_ref[:, cols]))
        mean = jnp.sum(n * n, axis=0, keepdims=True) * (1.0 / DL)
        o_ref[cols, :] = n * lax.rsqrt(mean + 1e-06)
        return carry

    lax.fori_loop(0, HL, head, 0, unroll=8)


def listed(list_ref, count_ref, qb, block):
    found = False
    for j in range(list_ref.shape[1]):
        found = jnp.logical_or(
            found, jnp.logical_and(j < count_ref[qb], list_ref[qb, j] == block)
        )
    return found


def attend(first, size, qb, kbs, q_ref, k_ref, vt_ref, m_ref, l_ref, acc_ref):
    qrows = tile(qb, size)
    krows = [tile(kb, size) for kb in kbs]
    lane = lax.broadcasted_iota(jnp.int32, (size, 2 * DH), 1)
    pairs = H // 2
    cols = [slice(p * 2 * DH, (p + 1) * 2 * DH) for p in range(pairs)]
    if first:
        shape = (size * len(kbs), 2 * size)
        key = lax.broadcasted_iota(jnp.int32, shape, 0)
        query = lax.broadcasted_iota(jnp.int32, shape, 1) % size
        other = key != query
    else:
        tops = m_ref[qb]
        totals = l_ref[qb]
    scores = []
    for p in range(pairs):
        q = q_ref[qrows, cols[p]] * jnp.asarray(DH ** (-0.5), BF16)
        zero = jnp.zeros_like(q)
        pair = jnp.concatenate([jnp.where(lane < DH, q, zero), jnp.where(lane < DH, zero, q)], axis=0)
        k = jnp.concatenate([k_ref[r, cols[p]] for r in krows], axis=0)
        s = dot_nt(k, pair)
        scores.append(jnp.where(other, s, -1e30) if first else s)
    raised = []
    new_tops = []
    new_totals = []
    for p in range(pairs):
        top = jnp.max(scores[p], axis=0, keepdims=True)
        if not first:
            top = jnp.maximum(top, tops[p : p + 1])
        e = jnp.exp(scores[p] - top)
        new_tops.append(top)
        new_totals.append(jnp.sum(e, axis=0, keepdims=True))
        raised.append(e.astype(BF16))
    for p in range(pairs):
        v = jnp.concatenate([vt_ref[cols[p], r] for r in krows], axis=1)
        o = dot_nn(v, raised[p])
        o = jnp.concatenate([o[:DH, :size], o[DH:, size:]], axis=0)
        if not first:
            fade = jnp.exp(tops[p : p + 1] - new_tops[p])
            new_totals[p] = new_totals[p] + totals[p : p + 1] * fade
            o = o + acc_ref[qb, cols[p], :] * by_head(fade, size)
        acc_ref[qb, cols[p], :] = o
    m_ref[qb] = jnp.concatenate(new_tops, axis=0)
    l_ref[qb] = jnp.concatenate(new_totals, axis=0)


def by_head(row, size):
    return jnp.concatenate(
        [jnp.broadcast_to(row[:, :size], (DH, size)), jnp.broadcast_to(row[:, size:], (DH, size))], axis=0
    )


def attend_listed(own, size, blocks, list_ref, count_ref, found_ref, *rest):
    def query(qb, carry):
        found_ref[0] = qb
        n = jnp.int32(1 if own else 0)
        for kb, block in enumerate(blocks):
            wanted = listed(list_ref, count_ref, qb, block)
            if own:
                wanted = jnp.logical_and(wanted, qb != kb)

            @pl.when(wanted)
            def _(n=n, kb=kb):
                found_ref[n] = kb

            n = n + wanted.astype(jnp.int32)
        start = 0
        if own:

            @pl.when(n == 1)
            def _():
                attend(True, size, qb, [qb], *rest)

            @pl.when(n > 1)
            def _():
                attend(True, size, qb, [qb, found_ref[1]], *rest)

            start = 2
        if len(blocks) - start > 1:

            def two(i, carry):
                attend(False, size, qb, [found_ref[start + 2 * i], found_ref[start + 2 * i + 1]], *rest)
                return carry

            lax.fori_loop(0, jnp.maximum(n - start, 0) // 2, two, 0)

        @pl.when(jnp.logical_and(n > start, n % 2 == 1))
        def _():
            attend(False, size, qb, [found_ref[n - 1]], *rest)

        return carry

    lax.fori_loop(0, list_ref.shape[0], query, 0)


def own_attention_kernel(
    size, list_ref, count_ref, pos_ref, k_ref, vt_ref, s_ref, m_ref, l_ref, acc_ref, kept_ref, found_ref
):
    kept_ref[...] = s_ref[...]
    queries = list_ref.shape[0]
    blocks = [pos_ref[0] * queries + kb for kb in range(queries)]
    attend_listed(
        True, size, blocks, list_ref, count_ref, found_ref, k_ref, k_ref, vt_ref, m_ref, l_ref, acc_ref
    )


def attend_halo(size, pieces, list_ref, count_ref, pos_ref, piece_refs, wk_ref, wv_ref, q_ref, state, scratch):
    found_ref, x_ref, k_ref, vt_ref = scratch
    queries = list_ref.shape[0]
    pos = pos_ref[0]
    step = 1 - 2 * (pos % 2)
    row = 0
    blocks = []
    for (near, first), ref in zip(pieces, piece_refs):
        rows = ref.shape[0]
        x_ref[row : row + rows, :] = ref[...]
        row += rows
        run = pos + step if near else pos - step
        blocks += [run * queries + first + i for i in range(rows // size)]
    project(x_ref[...], wk_ref, wv_ref, k_ref, vt_ref)
    attend_listed(
        False, size, blocks, list_ref, count_ref, found_ref, q_ref, k_ref, vt_ref, *state
    )


def halo_kernel(size, pieces, list_ref, count_ref, pos_ref, *refs):
    n = len(pieces)
    wk_ref, wv_ref, q_ref = refs[n : n + 3]
    attend_halo(
        size, pieces, list_ref, count_ref, pos_ref, refs[:n], wk_ref, wv_ref, q_ref, refs[n + 6 : n + 9], refs[n + 9 :]
    )


def final_kernel(size, pieces, list_ref, count_ref, pos_ref, *refs):
    n = len(pieces)
    wk_ref, wv_ref, q_ref, lin_ref, wo_ref = refs[n : n + 5]
    out_ref, m_ref, l_ref, acc_ref, comb_ref = refs[n + 8 : n + 13]
    attend_halo(
        size,
        pieces,
        list_ref,
        count_ref,
        pos_ref,
        refs[:n],
        wk_ref,
        wv_ref,
        q_ref,
        (m_ref, l_ref, acc_ref),
        refs[n + 13 :],
    )

    def finish(qb, carry):
        rows = tile(qb, size)
        share = 1.0 / l_ref[qb]
        for p in range(H // 2):
            cols = slice(p * 2 * DH, (p + 1) * 2 * DH)
            both = acc_ref[qb, cols, :] * by_head(share[p : p + 1], size) + lin_ref[cols, rows]
            comb_ref[rows, cols] = both.T.astype(BF16)
        return carry

    lax.fori_loop(0, list_ref.shape[0], finish, 0, unroll=True)
    out_ref[...] = dot_nn(comb_ref[...], wo_ref[...]).astype(BF16)


COSTLY = ("halo_a",)


def call(
    kernel,
    name,
    ins,
    outs,
    smem=0,
    scratch=(),
    aliases=None,
    limit=20 * MIB,
    space=pltpu.VMEM,
    out_space=pltpu.VMEM,
):
    return pl.pallas_call(
        kernel,
        name=name,
        in_specs=[SMEM] * smem + [pl.BlockSpec(memory_space=space)] * (len(ins) - smem),
        out_specs=[
            pl.BlockSpec(memory_space=m)
            for m in (out_space if isinstance(out_space, list) else [out_space] * len(outs))
        ],
        out_shape=[jax.ShapeDtypeStruct(s, d) for s, d in outs],
        scratch_shapes=list(scratch),
        input_output_aliases=aliases or {},
        cost_estimate=pl.CostEstimate(
            flops=10**11 if name in COSTLY else 1, bytes_accessed=1000, transcendentals=0
        ),
        compiler_params=pltpu.CompilerParams(vmem_limit_bytes=limit),
    )(*ins)


def after(value, *done):
    return lax.optimization_barrier((value,) + done)[0]


def on_device(tokens, qk_weight, value_weight, out_weight, neighbour_list, neighbour_count):
    rows = tokens.shape[1]
    width = tokens.shape[2]
    blocks = neighbour_list.shape[1]
    size = rows // blocks
    half = blocks // 2
    count = lax.axis_size("seq")
    position = lax.axis_index("seq").astype(jnp.int32).reshape(1)
    own = tokens[0]
    tables = (neighbour_list[0], neighbour_count[0], position)

    def swap(value, bit):
        return lax.ppermute(value, "seq", [(i, i ^ bit) for i in range(count)])

    def up(value, bit):
        return lax.ppermute(value, "seq", [(i, i | bit) for i in range(count) if not i & bit])

    def onward(value):
        pairs = [(i, i + 2) for i in range(0, count - 2, 2)] + [(i, i - 2) for i in range(3, count, 2)]
        return lax.ppermute(value, "seq", pairs)

    def across(value):
        odd = range(1, count - 1, 2)
        return lax.ppermute(value, "seq", [(i, i + 1) for i in odd] + [(i + 1, i) for i in odd])

    def flat(total):
        return (
            pltpu.SMEM((total // size + 2,), jnp.int32),
            pltpu.VMEM((total, width), BF16),
            pltpu.VMEM((total, width), BF16),
            pltpu.VMEM((width, total), BF16),
        )

    def join_halo(name, softmax, pieces, arrays):
        ins = tables + tuple(arrays) + (qk_weight, value_weight, keyed) + tuple(softmax)
        first = len(ins) - 3
        return call(
            functools.partial(halo_kernel, size, pieces),
            name,
            ins,
            shapes,
            smem=3,
            scratch=flat(sum(a.shape[0] for a in arrays)),
            aliases={first + i: i for i in range(3)},
        )

    cut = half * size
    in_hbm = functools.partial(pltpu.with_memory_space_constraint, memory_space=pltpu.HBM)
    (first_rows,) = call(
        cut_kernel,
        "cut",
        (in_hbm(own),),
        [((cut, width), BF16)],
        scratch=(pltpu.SemaphoreType.DMA(()),),
        space=pltpu.HBM,
    )
    near_a = swap(first_rows, 1)
    keyed, values_t, last_rows, state = call(
        own_kernel,
        "own",
        (in_hbm(after(own, first_rows)), in_hbm(qk_weight), in_hbm(value_weight)),
        [
            ((rows, width), BF16),
            ((width, rows), BF16),
            ((rows - cut, width), BF16),
            ((width, DL), BF16),
        ],
        scratch=(
            pltpu.VMEM((rows, width), BF16),
            pltpu.VMEM((width, width), BF16),
            pltpu.VMEM((width, width), BF16),
            pltpu.VMEM((rows, width), BF16),
            pltpu.VMEM((width, rows), BF16),
            pltpu.SemaphoreType.DMA((3,)),
            pltpu.SemaphoreType.DMA((3,)),
        ),
        limit=56 * MIB,
        space=pltpu.HBM,
        out_space=[pltpu.HBM] * 3 + [pltpu.VMEM],
    )
    far_b = across(last_rows)
    def halves(value, bit):
        return swap(value, bit)

    heard = [halves(state, 2)]
    shapes = [((blocks, H // 2, 2 * size), F32)] * 2 + [((blocks, width, size), F32)]
    *softmax, kept = call(
        functools.partial(own_attention_kernel, size),
        "own_attention",
        tables + (in_hbm(keyed), in_hbm(values_t), in_hbm(state)),
        shapes + [((width, DL), BF16)],
        smem=3,
        scratch=(pltpu.SMEM((blocks + 1,), jnp.int32),),
    )
    total = kept
    stride = 4
    while stride < count:
        total = total + after(heard[-1], softmax[0])
        heard.append(halves(total, stride))
        stride *= 2
    far_a = onward(after(near_a, total))
    near_b = swap(after(last_rows, near_a), 1)
    (within,) = call(
        within_kernel,
        "within",
        (after(keyed, softmax[0], near_a), values_t),
        [((width, rows), F32)],
    )
    softmax = join_halo("halo_a", softmax, [(True, 0)], [after(near_a, within)])
    (message,) = call(
        functools.partial(carry_kernel, len(heard)),
        "carry",
        (position, after(state, softmax[0])) + tuple(heard),
        [((width, DL), BF16)],
        smem=1,
    )
    message = swap(message, 1)
    softmax = join_halo("halo_b", softmax, [(False, half)], [after(far_b, heard[-1], softmax[0])])
    softmax = join_halo("halo_c", softmax, [(True, half)], [after(near_b, softmax[0])])
    (linear,) = call(
        functools.partial(linear_kernel, len(heard)),
        "linear",
        (position, after(keyed, softmax[0]), within) + tuple(heard) + (message,),
        [((width, rows), F32)],
        smem=1,
    )
    pieces = [(False, 0)]
    arrays = (after(far_a, linear),)
    ins = tables + arrays + (qk_weight, value_weight, keyed, linear, out_weight) + tuple(softmax)
    first = len(ins) - 3
    update, *_ = call(
        functools.partial(final_kernel, size, pieces),
        "final",
        ins,
        [((rows, width), BF16)] + shapes,
        smem=3,
        scratch=(pltpu.VMEM((rows, width), BF16),) + flat(sum(a.shape[0] for a in arrays)),
        aliases={first + i: i + 1 for i in range(3)},
    )
    return update[None]


def solution(mesh):
    placed = (
        P(("groups", "dp"), "seq", None),
        P(),
        P(),
        P(),
        P(("groups", "dp"), "seq", None),
        P(("groups", "dp"), "seq"),
    )
    return jax.shard_map(
        on_device,
        mesh=mesh,
        in_specs=placed,
        out_specs=P(("groups", "dp"), "seq", None),
        check_vma=False,
    )
```

```python
import functools

import jax
import jax.numpy as jnp
from jax import lax
from jax.experimental import pallas as pl
from jax.experimental.pallas import tpu as pltpu
from jax.sharding import PartitionSpec as P

H = 16
DH = 64
HL = 8
DL = 128
F32 = jnp.float32
BF16 = jnp.bfloat16
NT = (((1,), (1,)), ((), ()))
SMEM = pl.BlockSpec(memory_space=pltpu.SMEM)
MIB = 1 << 20


def dot_nt(a, b):
    return lax.dot_general(a, b, NT, preferred_element_type=F32)


def dot_nn(a, b):
    return jnp.dot(a, b, preferred_element_type=F32)


def tile(i, size):
    return pl.ds(pl.multiple_of(i * size, size), size)


def silu(k):
    k = k.astype(F32)
    return (k / (1.0 + jnp.exp(-k))).astype(BF16)


def project(x, wk_ref, wv_ref, k_ref, vt_ref):
    k_ref[...] = dot_nn(x, wk_ref[...]).astype(BF16)
    step = 256
    for i in range(0, wv_ref.shape[1], step):
        part = slice(i, i + step)
        vt_ref[part, :] = dot_nn(x, wv_ref[:, part]).astype(BF16).T


def cut_kernel(x_hbm, a_ref, sem):
    copy = pltpu.make_async_copy(x_hbm.at[: a_ref.shape[0]], a_ref, sem)
    copy.start()
    copy.wait()


def own_kernel(
    x_hbm, wk_hbm, wv_hbm, k_hbm, vt_hbm, b_hbm, s_ref, x_ref, wk_ref, wv_ref, k_ref, vt_ref, in_sems, out_sems
):
    ins = [
        pltpu.make_async_copy(src, dst, in_sems.at[i])
        for i, (src, dst) in enumerate(((x_hbm, x_ref), (wk_hbm, wk_ref), (wv_hbm, wv_ref)))
    ]
    outs = [
        pltpu.make_async_copy(src, dst, out_sems.at[i])
        for i, (src, dst) in enumerate(
            ((x_ref.at[x_ref.shape[0] - b_hbm.shape[0] :], b_hbm), (k_ref, k_hbm), (vt_ref, vt_hbm))
        )
    ]
    for copy in ins:
        copy.start()
    ins[0].wait()
    outs[0].start()
    ins[1].wait()
    k_ref[...] = dot_nn(x_ref[...], wk_ref[...]).astype(BF16)
    outs[1].start()
    ins[2].wait()
    step = 256
    for i in range(0, wv_ref.shape[1], step):
        part = slice(i, i + step)
        vt_ref[part, :] = dot_nt(wv_ref[:, part].T, x_ref[...]).astype(BF16)
    for h in range(HL):
        part = slice(h * DL, (h + 1) * DL)
        s_ref[part, :] = dot_nn(vt_ref[part, :], silu(k_ref[:, part])).astype(BF16)
    outs[2].start()
    for copy in outs:
        copy.wait()


def within_kernel(k_ref, vt_ref, n_ref):
    rows = k_ref.shape[0]
    half = rows // 2
    upper = lax.broadcasted_iota(jnp.int32, (half, half), 0) <= lax.broadcasted_iota(
        jnp.int32, (half, half), 1
    )

    def head(h, carry):
        cols = tile(h, DL)
        f0 = silu(k_ref[:half, cols])
        f1 = silu(k_ref[half:, cols])
        v0 = vt_ref[cols, :half]
        v1 = vt_ref[cols, half:]
        a00 = jnp.where(upper, dot_nt(f0, f0), 0.0).astype(BF16)
        a01 = dot_nt(f0, f1).astype(BF16)
        a11 = jnp.where(upper, dot_nt(f1, f1), 0.0).astype(BF16)
        n_ref[cols, :half] = dot_nn(v0, a00)
        n_ref[cols, half:] = dot_nn(v0, a01) + dot_nn(v1, a11)
        return carry

    lax.fori_loop(0, HL, head, 0, unroll=8)


def set_bits(pos_ref, count):
    return [((pos_ref[0] >> (k + 1)) & 1).astype(F32) for k in range(count)]


def carry_kernel(stages, pos_ref, s_ref, *refs):
    bits = set_bits(pos_ref, stages)
    first = 1.0 - (pos_ref[0] & 1).astype(F32)
    total = s_ref[...].astype(F32) * first
    for ref, bit in zip(refs, bits):
        total = total + ref[...].astype(F32) * bit
    refs[stages][...] = total.astype(BF16)


def linear_kernel(stages, pos_ref, k_ref, n_ref, *refs):
    heard, message_ref, o_ref = refs[:stages], refs[stages], refs[stages + 1]
    bits = set_bits(pos_ref, stages)

    def head(h, carry):
        cols = tile(h, DL)
        before = message_ref[cols, :].astype(F32)
        for ref, bit in zip(heard, bits):
            before = before + ref[cols, :].astype(F32) * bit
        n = n_ref[cols, :] + dot_nt(before.astype(BF16), silu(k_ref[:, cols]))
        mean = jnp.sum(n * n, axis=0, keepdims=True) * (1.0 / DL)
        o_ref[cols, :] = n * lax.rsqrt(mean + 1e-06)
        return carry

    lax.fori_loop(0, HL, head, 0, unroll=8)


def listed(list_ref, count_ref, qb, block):
    found = False
    for j in range(list_ref.shape[1]):
        found = jnp.logical_or(
            found, jnp.logical_and(j < count_ref[qb], list_ref[qb, j] == block)
        )
    return found


def attend(first, size, qb, kbs, q_ref, k_ref, vt_ref, m_ref, l_ref, acc_ref):
    qrows = tile(qb, size)
    krows = [tile(kb, size) for kb in kbs]
    lane = lax.broadcasted_iota(jnp.int32, (size, 2 * DH), 1)
    pairs = H // 2
    cols = [slice(p * 2 * DH, (p + 1) * 2 * DH) for p in range(pairs)]
    if first:
        shape = (size * len(kbs), 2 * size)
        key = lax.broadcasted_iota(jnp.int32, shape, 0)
        query = lax.broadcasted_iota(jnp.int32, shape, 1) % size
        other = key != query
    else:
        tops = m_ref[qb]
        totals = l_ref[qb]
    scores = []
    for p in range(pairs):
        q = q_ref[qrows, cols[p]] * jnp.asarray(DH ** (-0.5), BF16)
        zero = jnp.zeros_like(q)
        pair = jnp.concatenate([jnp.where(lane < DH, q, zero), jnp.where(lane < DH, zero, q)], axis=0)
        k = jnp.concatenate([k_ref[r, cols[p]] for r in krows], axis=0)
        s = dot_nt(k, pair)
        scores.append(jnp.where(other, s, -1e30) if first else s)
    raised = []
    new_tops = []
    new_totals = []
    for p in range(pairs):
        top = jnp.max(scores[p], axis=0, keepdims=True)
        if not first:
            top = jnp.maximum(top, tops[p : p + 1])
        e = jnp.exp(scores[p] - top)
        new_tops.append(top)
        new_totals.append(jnp.sum(e, axis=0, keepdims=True))
        raised.append(e.astype(BF16))
    for p in range(pairs):
        v = jnp.concatenate([vt_ref[cols[p], r] for r in krows], axis=1)
        o = dot_nn(v, raised[p])
        o = jnp.concatenate([o[:DH, :size], o[DH:, size:]], axis=0)
        if not first:
            fade = jnp.exp(tops[p : p + 1] - new_tops[p])
            new_totals[p] = new_totals[p] + totals[p : p + 1] * fade
            o = o + acc_ref[qb, cols[p], :] * by_head(fade, size)
        acc_ref[qb, cols[p], :] = o
    m_ref[qb] = jnp.concatenate(new_tops, axis=0)
    l_ref[qb] = jnp.concatenate(new_totals, axis=0)


def by_head(row, size):
    return jnp.concatenate(
        [jnp.broadcast_to(row[:, :size], (DH, size)), jnp.broadcast_to(row[:, size:], (DH, size))], axis=0
    )


def attend_listed(own, size, blocks, list_ref, count_ref, found_ref, *rest):
    def query(qb, carry):
        found_ref[0] = qb
        n = jnp.int32(1 if own else 0)
        for kb, block in enumerate(blocks):
            wanted = listed(list_ref, count_ref, qb, block)
            if own:
                wanted = jnp.logical_and(wanted, qb != kb)

            @pl.when(wanted)
            def _(n=n, kb=kb):
                found_ref[n] = kb

            n = n + wanted.astype(jnp.int32)
        start = 0
        if own:

            @pl.when(n == 1)
            def _():
                attend(True, size, qb, [qb], *rest)

            @pl.when(n > 1)
            def _():
                attend(True, size, qb, [qb, found_ref[1]], *rest)

            start = 2
        if len(blocks) - start > 1:

            def two(i, carry):
                attend(False, size, qb, [found_ref[start + 2 * i], found_ref[start + 2 * i + 1]], *rest)
                return carry

            lax.fori_loop(0, jnp.maximum(n - start, 0) // 2, two, 0)

        @pl.when(jnp.logical_and(n > start, n % 2 == 1))
        def _():
            attend(False, size, qb, [found_ref[n - 1]], *rest)

        return carry

    lax.fori_loop(0, list_ref.shape[0], query, 0)


def own_attention_kernel(
    size, list_ref, count_ref, pos_ref, k_ref, vt_ref, s_ref, m_ref, l_ref, acc_ref, kept_ref, found_ref
):
    kept_ref[...] = s_ref[...]
    queries = list_ref.shape[0]
    blocks = [pos_ref[0] * queries + kb for kb in range(queries)]
    attend_listed(
        True, size, blocks, list_ref, count_ref, found_ref, k_ref, k_ref, vt_ref, m_ref, l_ref, acc_ref
    )


def attend_halo(size, pieces, list_ref, count_ref, pos_ref, piece_refs, wk_ref, wv_ref, q_ref, state, scratch):
    found_ref, x_ref, k_ref, vt_ref = scratch
    queries = list_ref.shape[0]
    pos = pos_ref[0]
    step = 1 - 2 * (pos % 2)
    row = 0
    blocks = []
    for (near, first), ref in zip(pieces, piece_refs):
        rows = ref.shape[0]
        if len(pieces) > 1:
            x_ref[row : row + rows, :] = ref[...]
        row += rows
        run = pos + step if near else pos - step
        blocks += [run * queries + first + i for i in range(rows // size)]
    x = piece_refs[0][...] if len(pieces) == 1 else x_ref[...]
    project(x, wk_ref, wv_ref, k_ref, vt_ref)
    attend_listed(
        False, size, blocks, list_ref, count_ref, found_ref, q_ref, k_ref, vt_ref, *state
    )


def halo_kernel(size, pieces, list_ref, count_ref, pos_ref, *refs):
    n = len(pieces)
    wk_ref, wv_ref, q_ref = refs[n : n + 3]
    attend_halo(
        size, pieces, list_ref, count_ref, pos_ref, refs[:n], wk_ref, wv_ref, q_ref, refs[n + 6 : n + 9], refs[n + 9 :]
    )


def final_kernel(size, pieces, list_ref, count_ref, pos_ref, *refs):
    n = len(pieces)
    wk_ref, wv_ref, q_ref, lin_ref, wo_ref = refs[n : n + 5]
    out_ref, m_ref, l_ref, acc_ref, comb_ref = refs[n + 8 : n + 13]
    attend_halo(
        size,
        pieces,
        list_ref,
        count_ref,
        pos_ref,
        refs[:n],
        wk_ref,
        wv_ref,
        q_ref,
        (m_ref, l_ref, acc_ref),
        refs[n + 13 :],
    )

    def finish(qb, carry):
        rows = tile(qb, size)
        share = 1.0 / l_ref[qb]
        for p in range(H // 2):
            cols = slice(p * 2 * DH, (p + 1) * 2 * DH)
            both = acc_ref[qb, cols, :] * by_head(share[p : p + 1], size) + lin_ref[cols, rows]
            comb_ref[rows, cols] = both.T.astype(BF16)
        return carry

    lax.fori_loop(0, list_ref.shape[0], finish, 0, unroll=True)
    out_ref[...] = dot_nn(comb_ref[...], wo_ref[...]).astype(BF16)


COSTLY = ("halo_a",)


def call(
    kernel,
    name,
    ins,
    outs,
    smem=0,
    scratch=(),
    aliases=None,
    limit=20 * MIB,
    space=pltpu.VMEM,
    out_space=pltpu.VMEM,
):
    return pl.pallas_call(
        kernel,
        name=name,
        in_specs=[SMEM] * smem + [pl.BlockSpec(memory_space=space)] * (len(ins) - smem),
        out_specs=[
            pl.BlockSpec(memory_space=m)
            for m in (out_space if isinstance(out_space, list) else [out_space] * len(outs))
        ],
        out_shape=[jax.ShapeDtypeStruct(s, d) for s, d in outs],
        scratch_shapes=list(scratch),
        input_output_aliases=aliases or {},
        cost_estimate=pl.CostEstimate(
            flops=10**11 if name in COSTLY else 1, bytes_accessed=1000, transcendentals=0
        ),
        compiler_params=pltpu.CompilerParams(vmem_limit_bytes=limit),
    )(*ins)


def after(value, *done):
    return lax.optimization_barrier((value,) + done)[0]


def on_device(tokens, qk_weight, value_weight, out_weight, neighbour_list, neighbour_count):
    rows = tokens.shape[1]
    width = tokens.shape[2]
    blocks = neighbour_list.shape[1]
    size = rows // blocks
    half = blocks // 2
    count = lax.axis_size("seq")
    position = lax.axis_index("seq").astype(jnp.int32).reshape(1)
    own = tokens[0]
    tables = (neighbour_list[0], neighbour_count[0], position)

    def swap(value, bit):
        return lax.ppermute(value, "seq", [(i, i ^ bit) for i in range(count)])

    def up(value, bit):
        return lax.ppermute(value, "seq", [(i, i | bit) for i in range(count) if not i & bit])

    def onward(value):
        pairs = [(i, i + 2) for i in range(0, count - 2, 2)] + [(i, i - 2) for i in range(3, count, 2)]
        return lax.ppermute(value, "seq", pairs)

    def across(value):
        odd = range(1, count - 1, 2)
        return lax.ppermute(value, "seq", [(i, i + 1) for i in odd] + [(i + 1, i) for i in odd])

    def flat(total):
        return (
            pltpu.SMEM((total // size + 2,), jnp.int32),
            pltpu.VMEM((total, width), BF16),
            pltpu.VMEM((total, width), BF16),
            pltpu.VMEM((width, total), BF16),
        )

    def join_halo(name, softmax, pieces, arrays):
        ins = tables + tuple(arrays) + (qk_weight, value_weight, keyed) + tuple(softmax)
        first = len(ins) - 3
        return call(
            functools.partial(halo_kernel, size, pieces),
            name,
            ins,
            shapes,
            smem=3,
            scratch=flat(sum(a.shape[0] for a in arrays)),
            aliases={first + i: i for i in range(3)},
        )

    cut = half * size
    in_hbm = functools.partial(pltpu.with_memory_space_constraint, memory_space=pltpu.HBM)
    (first_rows,) = call(
        cut_kernel,
        "cut",
        (in_hbm(own),),
        [((cut, width), BF16)],
        scratch=(pltpu.SemaphoreType.DMA(()),),
        space=pltpu.HBM,
    )
    near_a = swap(first_rows, 1)
    keyed, values_t, last_rows, state = call(
        own_kernel,
        "own",
        (in_hbm(after(own, first_rows)), in_hbm(qk_weight), in_hbm(value_weight)),
        [
            ((rows, width), BF16),
            ((width, rows), BF16),
            ((rows - cut, width), BF16),
            ((width, DL), BF16),
        ],
        scratch=(
            pltpu.VMEM((rows, width), BF16),
            pltpu.VMEM((width, width), BF16),
            pltpu.VMEM((width, width), BF16),
            pltpu.VMEM((rows, width), BF16),
            pltpu.VMEM((width, rows), BF16),
            pltpu.SemaphoreType.DMA((3,)),
            pltpu.SemaphoreType.DMA((3,)),
        ),
        limit=56 * MIB,
        space=pltpu.HBM,
        out_space=[pltpu.HBM] * 3 + [pltpu.VMEM],
    )
    far_b = across(last_rows)
    def halves(value, bit):
        return swap(value, bit)

    heard = [halves(state, 2)]
    shapes = [((blocks, H // 2, 2 * size), F32)] * 2 + [((blocks, width, size), F32)]
    *softmax, kept = call(
        functools.partial(own_attention_kernel, size),
        "own_attention",
        tables + (in_hbm(keyed), in_hbm(values_t), in_hbm(state)),
        shapes + [((width, DL), BF16)],
        smem=3,
        scratch=(pltpu.SMEM((blocks + 1,), jnp.int32),),
    )
    total = kept
    stride = 4
    while stride < count:
        total = total + after(heard[-1], softmax[0])
        heard.append(halves(total, stride))
        stride *= 2
    far_a = onward(after(near_a, total))
    near_b = swap(after(last_rows, near_a), 1)
    (within,) = call(
        within_kernel,
        "within",
        (after(keyed, softmax[0], near_a), values_t),
        [((width, rows), F32)],
    )
    softmax = join_halo("halo_a", softmax, [(True, 0)], [after(near_a, within)])
    (message,) = call(
        functools.partial(carry_kernel, len(heard)),
        "carry",
        (position, after(state, softmax[0])) + tuple(heard),
        [((width, DL), BF16)],
        smem=1,
    )
    message = swap(message, 1)
    softmax = join_halo("halo_b", softmax, [(False, half)], [after(far_b, heard[-1], softmax[0])])
    softmax = join_halo("halo_c", softmax, [(True, half)], [after(near_b, softmax[0])])
    (linear,) = call(
        functools.partial(linear_kernel, len(heard)),
        "linear",
        (position, after(keyed, softmax[0]), within) + tuple(heard) + (message,),
        [((width, rows), F32)],
        smem=1,
    )
    pieces = [(False, 0)]
    arrays = (after(far_a, linear),)
    ins = tables + arrays + (qk_weight, value_weight, keyed, linear, out_weight) + tuple(softmax)
    first = len(ins) - 3
    update, *_ = call(
        functools.partial(final_kernel, size, pieces),
        "final",
        ins,
        [((rows, width), BF16)] + shapes,
        smem=3,
        scratch=(pltpu.VMEM((rows, width), BF16),) + flat(sum(a.shape[0] for a in arrays)),
        aliases={first + i: i + 1 for i in range(3)},
    )
    return update[None]


def solution(mesh):
    placed = (
        P(("groups", "dp"), "seq", None),
        P(),
        P(),
        P(),
        P(("groups", "dp"), "seq", None),
        P(("groups", "dp"), "seq"),
    )
    return jax.shard_map(
        on_device,
        mesh=mesh,
        in_specs=placed,
        out_specs=P(("groups", "dp"), "seq", None),
        check_vma=False,
    )
```

```python
import functools

import jax
import jax.numpy as jnp
from jax import lax
from jax.experimental import pallas as pl
from jax.experimental.pallas import tpu as pltpu
from jax.sharding import PartitionSpec as P

H = 16
DH = 64
HL = 8
DL = 128
F32 = jnp.float32
BF16 = jnp.bfloat16
NT = (((1,), (1,)), ((), ()))
SMEM = pl.BlockSpec(memory_space=pltpu.SMEM)
MIB = 1 << 20


def dot_nt(a, b):
    return lax.dot_general(a, b, NT, preferred_element_type=F32)


def dot_nn(a, b):
    return jnp.dot(a, b, preferred_element_type=F32)


def tile(i, size):
    return pl.ds(pl.multiple_of(i * size, size), size)


def silu(k):
    k = k.astype(F32)
    return (k / (1.0 + jnp.exp(-k))).astype(BF16)


def project(x, wk_ref, wv_ref, k_ref, vt_ref):
    k_ref[...] = dot_nn(x, wk_ref[...]).astype(BF16)
    vt_ref[...] = dot_nn(x, wv_ref[...]).astype(BF16).T


def cut_kernel(x_hbm, a_ref, sem):
    copy = pltpu.make_async_copy(x_hbm.at[: a_ref.shape[0]], a_ref, sem)
    copy.start()
    copy.wait()


def own_kernel(
    x_hbm, wk_hbm, wv_hbm, k_hbm, vt_hbm, b_hbm, s_ref, x_ref, wk_ref, wv_ref, k_ref, vt_ref, in_sems, out_sems
):
    ins = [
        pltpu.make_async_copy(src, dst, in_sems.at[i])
        for i, (src, dst) in enumerate(((x_hbm, x_ref), (wk_hbm, wk_ref), (wv_hbm, wv_ref)))
    ]
    outs = [
        pltpu.make_async_copy(src, dst, out_sems.at[i])
        for i, (src, dst) in enumerate(
            ((x_ref.at[x_ref.shape[0] - b_hbm.shape[0] :], b_hbm), (k_ref, k_hbm), (vt_ref, vt_hbm))
        )
    ]
    for copy in ins:
        copy.start()
    ins[0].wait()
    outs[0].start()
    ins[1].wait()
    k_ref[...] = dot_nn(x_ref[...], wk_ref[...]).astype(BF16)
    outs[1].start()
    ins[2].wait()
    step = 256
    for i in range(0, wv_ref.shape[1], step):
        part = slice(i, i + step)
        vt_ref[part, :] = dot_nt(wv_ref[:, part].T, x_ref[...]).astype(BF16)
    for h in range(HL):
        part = slice(h * DL, (h + 1) * DL)
        s_ref[part, :] = dot_nn(vt_ref[part, :], silu(k_ref[:, part])).astype(BF16)
    outs[2].start()
    for copy in outs:
        copy.wait()


def within_kernel(k_ref, vt_ref, n_ref):
    rows = k_ref.shape[0]
    half = rows // 2
    upper = lax.broadcasted_iota(jnp.int32, (half, half), 0) <= lax.broadcasted_iota(
        jnp.int32, (half, half), 1
    )

    def head(h, carry):
        cols = tile(h, DL)
        f0 = silu(k_ref[:half, cols])
        f1 = silu(k_ref[half:, cols])
        v0 = vt_ref[cols, :half]
        v1 = vt_ref[cols, half:]
        a00 = jnp.where(upper, dot_nt(f0, f0), 0.0).astype(BF16)
        a01 = dot_nt(f0, f1).astype(BF16)
        a11 = jnp.where(upper, dot_nt(f1, f1), 0.0).astype(BF16)
        n_ref[cols, :half] = dot_nn(v0, a00)
        n_ref[cols, half:] = dot_nn(v0, a01) + dot_nn(v1, a11)
        return carry

    lax.fori_loop(0, HL, head, 0, unroll=8)


def set_bits(pos_ref, count):
    return [((pos_ref[0] >> (k + 1)) & 1).astype(F32) for k in range(count)]


def carry_kernel(stages, pos_ref, s_ref, *refs):
    bits = set_bits(pos_ref, stages)
    first = 1.0 - (pos_ref[0] & 1).astype(F32)
    total = s_ref[...].astype(F32) * first
    for ref, bit in zip(refs, bits):
        total = total + ref[...].astype(F32) * bit
    refs[stages][...] = total.astype(BF16)


def linear_kernel(stages, pos_ref, k_ref, n_ref, *refs):
    heard, message_ref, o_ref = refs[:stages], refs[stages], refs[stages + 1]
    bits = set_bits(pos_ref, stages)

    def head(h, carry):
        cols = tile(h, DL)
        before = message_ref[cols, :].astype(F32)
        for ref, bit in zip(heard, bits):
            before = before + ref[cols, :].astype(F32) * bit
        n = n_ref[cols, :] + dot_nt(before.astype(BF16), silu(k_ref[:, cols]))
        mean = jnp.sum(n * n, axis=0, keepdims=True) * (1.0 / DL)
        o_ref[cols, :] = n * lax.rsqrt(mean + 1e-06)
        return carry

    lax.fori_loop(0, HL, head, 0, unroll=8)


def listed(list_ref, count_ref, qb, block):
    found = False
    for j in range(list_ref.shape[1]):
        found = jnp.logical_or(
            found, jnp.logical_and(j < count_ref[qb], list_ref[qb, j] == block)
        )
    return found


def attend(first, size, qb, kbs, q_ref, k_ref, vt_ref, m_ref, l_ref, acc_ref):
    qrows = tile(qb, size)
    krows = [tile(kb, size) for kb in kbs]
    lane = lax.broadcasted_iota(jnp.int32, (size, 2 * DH), 1)
    pairs = H // 2
    cols = [slice(p * 2 * DH, (p + 1) * 2 * DH) for p in range(pairs)]
    if first:
        shape = (size * len(kbs), 2 * size)
        key = lax.broadcasted_iota(jnp.int32, shape, 0)
        query = lax.broadcasted_iota(jnp.int32, shape, 1) % size
        other = key != query
    else:
        tops = m_ref[qb]
        totals = l_ref[qb]
    scores = []
    for p in range(pairs):
        q = q_ref[qrows, cols[p]] * jnp.asarray(DH ** (-0.5), BF16)
        zero = jnp.zeros_like(q)
        pair = jnp.concatenate([jnp.where(lane < DH, q, zero), jnp.where(lane < DH, zero, q)], axis=0)
        k = jnp.concatenate([k_ref[r, cols[p]] for r in krows], axis=0)
        s = dot_nt(k, pair)
        scores.append(jnp.where(other, s, -1e30) if first else s)
    raised = []
    new_tops = []
    new_totals = []
    for p in range(pairs):
        top = jnp.max(scores[p], axis=0, keepdims=True)
        if not first:
            top = jnp.maximum(top, tops[p : p + 1])
        e = jnp.exp(scores[p] - top)
        new_tops.append(top)
        new_totals.append(jnp.sum(e, axis=0, keepdims=True))
        raised.append(e.astype(BF16))
    for p in range(pairs):
        v = jnp.concatenate([vt_ref[cols[p], r] for r in krows], axis=1)
        o = dot_nn(v, raised[p])
        o = jnp.concatenate([o[:DH, :size], o[DH:, size:]], axis=0)
        if not first:
            fade = jnp.exp(tops[p : p + 1] - new_tops[p])
            new_totals[p] = new_totals[p] + totals[p : p + 1] * fade
            o = o + acc_ref[qb, cols[p], :] * by_head(fade, size)
        acc_ref[qb, cols[p], :] = o
    m_ref[qb] = jnp.concatenate(new_tops, axis=0)
    l_ref[qb] = jnp.concatenate(new_totals, axis=0)


def by_head(row, size):
    return jnp.concatenate(
        [jnp.broadcast_to(row[:, :size], (DH, size)), jnp.broadcast_to(row[:, size:], (DH, size))], axis=0
    )


def attend_listed(own, size, blocks, list_ref, count_ref, found_ref, *rest):
    def query(qb, carry):
        found_ref[0] = qb
        n = jnp.int32(1 if own else 0)
        for kb, block in enumerate(blocks):
            wanted = listed(list_ref, count_ref, qb, block)
            if own:
                wanted = jnp.logical_and(wanted, qb != kb)

            @pl.when(wanted)
            def _(n=n, kb=kb):
                found_ref[n] = kb

            n = n + wanted.astype(jnp.int32)
        start = 0
        if own:

            @pl.when(n == 1)
            def _():
                attend(True, size, qb, [qb], *rest)

            @pl.when(n > 1)
            def _():
                attend(True, size, qb, [qb, found_ref[1]], *rest)

            start = 2
        if len(blocks) - start > 1:

            def two(i, carry):
                attend(False, size, qb, [found_ref[start + 2 * i], found_ref[start + 2 * i + 1]], *rest)
                return carry

            lax.fori_loop(0, jnp.maximum(n - start, 0) // 2, two, 0)

        @pl.when(jnp.logical_and(n > start, n % 2 == 1))
        def _():
            attend(False, size, qb, [found_ref[n - 1]], *rest)

        return carry

    lax.fori_loop(0, list_ref.shape[0], query, 0)


def own_attention_kernel(
    size, list_ref, count_ref, pos_ref, k_ref, vt_ref, s_ref, m_ref, l_ref, acc_ref, kept_ref, found_ref
):
    kept_ref[...] = s_ref[...]
    queries = list_ref.shape[0]
    blocks = [pos_ref[0] * queries + kb for kb in range(queries)]
    attend_listed(
        True, size, blocks, list_ref, count_ref, found_ref, k_ref, k_ref, vt_ref, m_ref, l_ref, acc_ref
    )


def attend_halo(size, pieces, list_ref, count_ref, pos_ref, piece_refs, wk_ref, wv_ref, q_ref, state, scratch):
    found_ref, x_ref, k_ref, vt_ref = scratch
    queries = list_ref.shape[0]
    pos = pos_ref[0]
    step = 1 - 2 * (pos % 2)
    row = 0
    blocks = []
    for (near, first), ref in zip(pieces, piece_refs):
        rows = ref.shape[0]
        if len(pieces) > 1:
            x_ref[row : row + rows, :] = ref[...]
        row += rows
        run = pos + step if near else pos - step
        blocks += [run * queries + first + i for i in range(rows // size)]
    x = piece_refs[0][...] if len(pieces) == 1 else x_ref[...]
    project(x, wk_ref, wv_ref, k_ref, vt_ref)
    attend_listed(
        False, size, blocks, list_ref, count_ref, found_ref, q_ref, k_ref, vt_ref, *state
    )


def halo_kernel(size, pieces, list_ref, count_ref, pos_ref, *refs):
    n = len(pieces)
    wk_ref, wv_ref, q_ref = refs[n : n + 3]
    attend_halo(
        size, pieces, list_ref, count_ref, pos_ref, refs[:n], wk_ref, wv_ref, q_ref, refs[n + 6 : n + 9], refs[n + 9 :]
    )


def final_kernel(size, pieces, list_ref, count_ref, pos_ref, *refs):
    n = len(pieces)
    wk_ref, wv_ref, q_ref, lin_ref, wo_ref = refs[n : n + 5]
    out_ref, m_ref, l_ref, acc_ref, comb_ref = refs[n + 8 : n + 13]
    attend_halo(
        size,
        pieces,
        list_ref,
        count_ref,
        pos_ref,
        refs[:n],
        wk_ref,
        wv_ref,
        q_ref,
        (m_ref, l_ref, acc_ref),
        refs[n + 13 :],
    )

    def finish(qb, carry):
        rows = tile(qb, size)
        share = 1.0 / l_ref[qb]
        for p in range(H // 2):
            cols = slice(p * 2 * DH, (p + 1) * 2 * DH)
            both = acc_ref[qb, cols, :] * by_head(share[p : p + 1], size) + lin_ref[cols, rows]
            comb_ref[rows, cols] = both.T.astype(BF16)
        return carry

    lax.fori_loop(0, list_ref.shape[0], finish, 0, unroll=True)
    out_ref[...] = dot_nn(comb_ref[...], wo_ref[...]).astype(BF16)


COSTLY = ("halo_a",)


def call(
    kernel,
    name,
    ins,
    outs,
    smem=0,
    scratch=(),
    aliases=None,
    limit=20 * MIB,
    space=pltpu.VMEM,
    out_space=pltpu.VMEM,
):
    return pl.pallas_call(
        kernel,
        name=name,
        in_specs=[SMEM] * smem + [pl.BlockSpec(memory_space=space)] * (len(ins) - smem),
        out_specs=[
            pl.BlockSpec(memory_space=m)
            for m in (out_space if isinstance(out_space, list) else [out_space] * len(outs))
        ],
        out_shape=[jax.ShapeDtypeStruct(s, d) for s, d in outs],
        scratch_shapes=list(scratch),
        input_output_aliases=aliases or {},
        cost_estimate=pl.CostEstimate(
            flops=10**11 if name in COSTLY else 1, bytes_accessed=1000, transcendentals=0
        ),
        compiler_params=pltpu.CompilerParams(vmem_limit_bytes=limit),
    )(*ins)


def after(value, *done):
    return lax.optimization_barrier((value,) + done)[0]


def on_device(tokens, qk_weight, value_weight, out_weight, neighbour_list, neighbour_count):
    rows = tokens.shape[1]
    width = tokens.shape[2]
    blocks = neighbour_list.shape[1]
    size = rows // blocks
    half = blocks // 2
    count = lax.axis_size("seq")
    position = lax.axis_index("seq").astype(jnp.int32).reshape(1)
    own = tokens[0]
    tables = (neighbour_list[0], neighbour_count[0], position)

    def swap(value, bit):
        return lax.ppermute(value, "seq", [(i, i ^ bit) for i in range(count)])

    def up(value, bit):
        return lax.ppermute(value, "seq", [(i, i | bit) for i in range(count) if not i & bit])

    def onward(value):
        pairs = [(i, i + 2) for i in range(0, count - 2, 2)] + [(i, i - 2) for i in range(3, count, 2)]
        return lax.ppermute(value, "seq", pairs)

    def across(value):
        odd = range(1, count - 1, 2)
        return lax.ppermute(value, "seq", [(i, i + 1) for i in odd] + [(i + 1, i) for i in odd])

    def flat(total):
        return (
            pltpu.SMEM((total // size + 2,), jnp.int32),
            pltpu.VMEM((total, width), BF16),
            pltpu.VMEM((total, width), BF16),
            pltpu.VMEM((width, total), BF16),
        )

    def join_halo(name, softmax, pieces, arrays):
        ins = tables + tuple(arrays) + (qk_weight, value_weight, keyed) + tuple(softmax)
        first = len(ins) - 3
        return call(
            functools.partial(halo_kernel, size, pieces),
            name,
            ins,
            shapes,
            smem=3,
            scratch=flat(sum(a.shape[0] for a in arrays)),
            aliases={first + i: i for i in range(3)},
        )

    cut = half * size
    in_hbm = functools.partial(pltpu.with_memory_space_constraint, memory_space=pltpu.HBM)
    (first_rows,) = call(
        cut_kernel,
        "cut",
        (in_hbm(own),),
        [((cut, width), BF16)],
        scratch=(pltpu.SemaphoreType.DMA(()),),
        space=pltpu.HBM,
    )
    near_a = swap(first_rows, 1)
    keyed, values_t, last_rows, state = call(
        own_kernel,
        "own",
        (in_hbm(after(own, first_rows)), in_hbm(qk_weight), in_hbm(value_weight)),
        [
            ((rows, width), BF16),
            ((width, rows), BF16),
            ((rows - cut, width), BF16),
            ((width, DL), BF16),
        ],
        scratch=(
            pltpu.VMEM((rows, width), BF16),
            pltpu.VMEM((width, width), BF16),
            pltpu.VMEM((width, width), BF16),
            pltpu.VMEM((rows, width), BF16),
            pltpu.VMEM((width, rows), BF16),
            pltpu.SemaphoreType.DMA((3,)),
            pltpu.SemaphoreType.DMA((3,)),
        ),
        limit=56 * MIB,
        space=pltpu.HBM,
        out_space=[pltpu.HBM] * 3 + [pltpu.VMEM],
    )
    far_b = across(last_rows)
    def halves(value, bit):
        return swap(value, bit)

    heard = [halves(state, 2)]
    shapes = [((blocks, H // 2, 2 * size), F32)] * 2 + [((blocks, width, size), F32)]
    *softmax, kept = call(
        functools.partial(own_attention_kernel, size),
        "own_attention",
        tables + (in_hbm(keyed), in_hbm(values_t), in_hbm(state)),
        shapes + [((width, DL), BF16)],
        smem=3,
        scratch=(pltpu.SMEM((blocks + 1,), jnp.int32),),
    )
    total = kept
    stride = 4
    while stride < count:
        total = total + after(heard[-1], softmax[0])
        heard.append(halves(total, stride))
        stride *= 2
    far_a = onward(after(near_a, total))
    near_b = swap(after(last_rows, near_a), 1)
    (within,) = call(
        within_kernel,
        "within",
        (after(keyed, softmax[0], near_a), values_t),
        [((width, rows), F32)],
    )
    softmax = join_halo("halo_a", softmax, [(True, 0)], [after(near_a, within)])
    (message,) = call(
        functools.partial(carry_kernel, len(heard)),
        "carry",
        (position, after(state, softmax[0])) + tuple(heard),
        [((width, DL), BF16)],
        smem=1,
    )
    message = swap(message, 1)
    softmax = join_halo("halo_b", softmax, [(False, half)], [after(far_b, heard[-1], softmax[0])])
    softmax = join_halo("halo_c", softmax, [(True, half)], [after(near_b, softmax[0])])
    (linear,) = call(
        functools.partial(linear_kernel, len(heard)),
        "linear",
        (position, after(keyed, softmax[0]), within) + tuple(heard) + (message,),
        [((width, rows), F32)],
        smem=1,
    )
    pieces = [(False, 0)]
    arrays = (after(far_a, linear),)
    ins = tables + arrays + (qk_weight, value_weight, keyed, linear, out_weight) + tuple(softmax)
    first = len(ins) - 3
    update, *_ = call(
        functools.partial(final_kernel, size, pieces),
        "final",
        ins,
        [((rows, width), BF16)] + shapes,
        smem=3,
        scratch=(pltpu.VMEM((rows, width), BF16),) + flat(sum(a.shape[0] for a in arrays)),
        aliases={first + i: i + 1 for i in range(3)},
    )
    return update[None]


def solution(mesh):
    placed = (
        P(("groups", "dp"), "seq", None),
        P(),
        P(),
        P(),
        P(("groups", "dp"), "seq", None),
        P(("groups", "dp"), "seq"),
    )
    return jax.shard_map(
        on_device,
        mesh=mesh,
        in_specs=placed,
        out_specs=P(("groups", "dp"), "seq", None),
        check_vma=False,
    )
```
